32 devices in a mesh: groups: 2 (over y), inst: 4 (over z), space: 4 (over x, core).
Axes of the slice: x: 2, y: 2, z: 4, core: 2. Of those that a mesh axis runs over, the one named last changes fastest.
Arguments:
- flow_state: float32 [8, 5, 16, 16, 128], P(('groups', 'inst'), None, 'space'), parts along dimension 0, may hold values from -1 to 1
- period_match: int32 [16], replicated, may hold values from 0 to 15, each once
Outputs:
- residual: float32 [8, 5, 16, 16, 128], P(('groups', 'inst'), None, 'space'), parts along dimension 0
The draws below stay inside these ranges and needn't reach their ends.
There are 2 independent parts, one for each index of `groups`. The reference program is written for one: setup_inputs(seed, part) draws one part's arguments, and reference() takes and returns one part's arrays. A program takes and returns all parts, laid end to end along the dimension named above; an argument that names none is the same for every part. Nothing has to cross between parts.
Inputs may be any that keep to these rules, and one draw needn't show every extreme that they name: period_match is a permutation of the 16 spanwise layers.
All inputs are finite; a program needn't handle non-finite values.
Results may differ from the reference program's by a relative error of at most 0.0003.
Values sent between devices are 32-bit elements; how exact they have to be, the bound alone decides.
No kernel may reach another device: no remote copies, remote signals or barrier semaphores. Data moves between devices by JAX's collectives and lax.ppermute only.
A program may use at most 64 MiB of HBM per device.

```python
import math
import jax
import jax.numpy as jnp
from jax import lax

NK = 16
NJ = 128
N_TIME = 4
LAG = 1
NI = 16


def block_levels(own_key, shape, shards, smallest, high):
    def one(dim, blocks):
        heights = jax.random.uniform(jax.random.fold_in(jax.random.fold_in(own_key, 6), dim), (blocks,), jnp.float32, smallest / len(shards), high / len(shards))
        return jnp.repeat(jnp.exp(heights), shape[dim] // blocks).reshape((-1,) + (1,) * (len(shape) - dim - 1))

    gain = one(*shards[0])
    for cut in shards[1:]:
        gain = gain * one(*cut)
    return gain


def setup_inputs(seed: int = 0, part: int = 0) -> dict:
    key_list = jax.random.split(jax.random.key(seed), 3)
    part_splits = jax.random.split(jax.random.fold_in(key_list[2], part), 3)
    return {
        "flow_state": jnp.clip(jax.random.uniform(part_splits[0], (N_TIME, 5, NI, NK, NJ), jnp.float32, -1.0, 1.0) * block_levels(part_splits[0], (N_TIME, 5, NI, NK, NJ), ((0, 4), (2, 4)), -0.4, 0.0), -1.0, 1.0),
        "period_match": jax.random.permutation(key_list[1], NK).astype(jnp.int32),
    }


gamma_gas = 1.4
prandtl = 0.72
viscosity = 0.1
pseudo_step = 0.03
entropy_share = 0.1

def from_draw(draws):
    shape = (5,) + (1,) * (draws.ndim - 1)
    offsets = jnp.array([1.0, 0.8, 0.0, 0.0, 0.8], jnp.float32).reshape(shape)
    spreads = jnp.array([0.3, 0.3, 0.3, 0.3, 0.2], jnp.float32).reshape(shape)
    return offsets + spreads * draws

def conserved(primitives):
    dens = primitives[0]
    velocity = primitives[1:4]
    kinetic = 0.5 * dens * lax.optimization_barrier(jnp.sum(velocity * velocity, axis=0))
    energy = primitives[4] / (gamma_gas - 1.0) + kinetic
    return jnp.concatenate([dens[None], dens[None] * velocity, energy[None]], axis=0)

def primitive(conserved_vars):
    dens = conserved_vars[0]
    velocity = conserved_vars[1:4] / dens
    pressure = (gamma_gas - 1.0) * (conserved_vars[4] - 0.5 * dens * lax.optimization_barrier(jnp.sum(velocity * velocity, axis=0)))
    return jnp.concatenate([dens[None], velocity, pressure[None]], axis=0)

def entropy_fix(eigen_val, sound_speed):
    spread = entropy_share * sound_speed
    magnitude = jnp.abs(eigen_val)
    return jnp.where(magnitude >= spread, magnitude, (eigen_val * eigen_val + spread * spread) / (2.0 * spread))

def euler_flux(dens, velocity, pressure, enthalpy, normal):
    normal_vel = velocity[normal]
    values = [dens * normal_vel]
    for component in range(3):
        moment = dens * velocity[component] * normal_vel
        if component == normal:
            moment = moment + pressure
        values.append(moment)
    values.append(dens * enthalpy * normal_vel)
    return values

def face_flux(left_cells, right_cells, normal):
    dens_left, vel_left, pres_left = (left_cells[0], left_cells[1:4], left_cells[4])
    dens_right, vel_right, pres_right = (right_cells[0], right_cells[1:4], right_cells[4])
    ratio = gamma_gas / (gamma_gas - 1.0)
    sq_left = lax.optimization_barrier(jnp.sum(vel_left * vel_left, axis=0))
    sq_right = lax.optimization_barrier(jnp.sum(vel_right * vel_right, axis=0))
    enth_left = ratio * pres_left / dens_left + 0.5 * sq_left
    enth_right = ratio * pres_right / dens_right + 0.5 * sq_right
    flux_left = euler_flux(dens_left, vel_left, pres_left, enth_left, normal)
    flux_right = euler_flux(dens_right, vel_right, pres_right, enth_right, normal)
    root_left = jnp.sqrt(dens_left)
    root_right = jnp.sqrt(dens_right)
    root_sum = root_left + root_right
    vel_roe = (root_left * vel_left + root_right * vel_right) / root_sum
    enth_roe = (root_left * enth_left + root_right * enth_right) / root_sum
    speed_sq = lax.optimization_barrier(jnp.sum(vel_roe * vel_roe, axis=0))
    sound_sq = (gamma_gas - 1.0) * (enth_roe - 0.5 * speed_sq)
    sound_speed = jnp.sqrt(sound_sq)
    normal_vel = vel_roe[normal]
    dens_roe = root_left * root_right
    jump_dens = dens_right - dens_left
    jump_pres = pres_right - pres_left
    jump_vel = vel_right - vel_left
    jump_normal = jump_vel[normal]
    wave_slow = (jump_pres - dens_roe * sound_speed * jump_normal) / (2.0 * sound_sq)
    wave_fast = (jump_pres + dens_roe * sound_speed * jump_normal) / (2.0 * sound_sq)
    wave_mid = jump_dens - jump_pres / sound_sq
    eigen_mid = entropy_fix(normal_vel, sound_speed)
    flux_slow = entropy_fix(normal_vel - sound_speed, sound_speed) * wave_slow
    flux_fast = entropy_fix(normal_vel + sound_speed, sound_speed) * wave_fast
    dissipation = [flux_slow + eigen_mid * wave_mid + flux_fast]
    for component in range(3):
        unit_dir = 1.0 if component == normal else 0.0
        term = flux_slow * (vel_roe[component] - unit_dir * sound_speed)
        term = term + eigen_mid * (wave_mid * vel_roe[component] + dens_roe * (jump_vel[component] - unit_dir * jump_normal))
        term = term + flux_fast * (vel_roe[component] + unit_dir * sound_speed)
        dissipation.append(term)
    shear_work = lax.optimization_barrier(jnp.sum(vel_roe * jump_vel, axis=0)) - normal_vel * jump_normal
    energy_term = flux_slow * (enth_roe - normal_vel * sound_speed)
    energy_term = energy_term + eigen_mid * (wave_mid * 0.5 * speed_sq + dens_roe * shear_work)
    energy_term = energy_term + flux_fast * (enth_roe + normal_vel * sound_speed)
    dissipation.append(energy_term)
    jump_temp = pres_right / dens_right - pres_left / dens_left
    jump_kin = 0.5 * (sq_right - sq_left)
    viscous_terms = [jnp.zeros_like(jump_dens), jump_vel[0], jump_vel[1], jump_vel[2], jump_kin + gamma_gas / ((gamma_gas - 1.0) * prandtl) * jump_temp]
    values = []
    for component in range(5):
        values.append(0.5 * (flux_left[component] + flux_right[component]) - 0.5 * dissipation[component] - viscosity * viscous_terms[component])
    return jnp.stack(values, axis=0)

def flux_change(padded, along, normal):
    length = padded.shape[along]
    face_values = face_flux(lax.slice_in_dim(padded, 0, length - 1, axis=along), lax.slice_in_dim(padded, 1, length, axis=along), normal)
    return lax.slice_in_dim(face_values, 1, length - 1, axis=along) - lax.slice_in_dim(face_values, 0, length - 2, axis=along)

def spectral_entry(offset, number):
    wrapped = jnp.mod(offset, number)
    parity = 1.0 - 2.0 * jnp.mod(wrapped, 2).astype(jnp.float32)
    angles = math.pi * wrapped.astype(jnp.float32) / number
    sine_val = jnp.where(wrapped == 0, 1.0, jnp.sin(angles))
    derivative = jnp.where(wrapped == 0, 0.0, math.pi / number * parity * jnp.cos(angles) / sine_val)
    return derivative + 0.5 * parity

def reference(flow_state, period_match):
    start = from_draw(jnp.moveaxis(flow_state, 1, 0))
    inverse = jnp.argsort(period_match).astype(jnp.int32)
    labels = jnp.arange(N_TIME, dtype=jnp.int32)
    matrix = spectral_entry(labels[:, None] - labels[None, :], N_TIME)
    mirror = jnp.array([1.0, 1.0, 1.0, -1.0, 1.0], jnp.float32).reshape(5, 1, 1, 1, 1)

    def evaluate(conserved_vars):
        prims = primitive(conserved_vars)
        along_axial = jnp.concatenate([prims[:, :, :1], prims, prims[:, :, -1:]], axis=2)
        along_span = jnp.concatenate([prims[:, :, :, :1] * mirror, prims, prims[:, :, :, -1:] * mirror], axis=3)
        ghost_below = jnp.take(jnp.roll(prims[..., -1], LAG, axis=1), period_match, axis=3)
        ghost_above = jnp.take(jnp.roll(prims[..., 0], -LAG, axis=1), inverse, axis=3)
        along_pitch = jnp.concatenate([ghost_below[..., None], prims, ghost_above[..., None]], axis=4)
        spatial = flux_change(along_axial, 2, 0) + flux_change(along_span, 3, 2) + flux_change(along_pitch, 4, 1)
        timewise = jnp.einsum('nm,cmikj->cnikj', matrix, conserved_vars, precision=lax.Precision.HIGHEST)
        return timewise + spatial
    initial = conserved(start)
    section_state = initial - pseudo_step * evaluate(initial)
    return jnp.moveaxis(evaluate(section_state), 0, 1)
```

```python
import math

import jax
import jax.numpy as jnp
from jax import lax
from jax.experimental import pallas as pl
from jax.experimental.pallas import tpu as pltpu
from jax.sharding import PartitionSpec as P

gamma_gas = 1.4
prandtl = 0.72
viscosity = 0.1
pseudo_step = 0.03
entropy_share = 0.1


def from_behind(block, axis, distance):
    devices = range(lax.axis_size(axis))
    route = [((i - distance) % len(devices), i) for i in devices]
    return lax.ppermute(block, axis, route)


def extended(cells, sides, width):
    for axis, dim in sides:
        count = lax.axis_size(axis)
        ends = count - 1
        head = lax.slice_in_dim(cells, 0, width, axis=dim)
        tail = lax.slice_in_dim(cells, cells.shape[dim] - width, cells.shape[dim], axis=dim)
        cells = jnp.concatenate(
            [
                lax.ppermute(tail, axis, [(i, (i + 1) % count) for i in range(ends)]),
                cells,
                lax.ppermute(head, axis, [((i + 1) % count, i) for i in range(ends)]),
            ],
            axis=dim,
        )
    return cells


def from_draw(draws):
    shape = (5,) + (1,) * (draws.ndim - 1)
    offsets = jnp.array([1.0, 0.8, 0.0, 0.0, 0.8], jnp.float32).reshape(shape)
    spreads = jnp.array([0.3, 0.3, 0.3, 0.3, 0.2], jnp.float32).reshape(shape)
    return offsets + spreads * draws


def conserved(primitives):
    dens = primitives[0]
    velocity = primitives[1:4]
    kinetic = 0.5 * dens * jnp.sum(velocity * velocity, axis=0)
    energy = primitives[4] / (gamma_gas - 1.0) + kinetic
    return jnp.concatenate([dens[None], dens[None] * velocity, energy[None]], axis=0)


def primitive(conserved_vars):
    dens = conserved_vars[0]
    velocity = conserved_vars[1:4] / dens
    pressure = (gamma_gas - 1.0) * (
        conserved_vars[4] - 0.5 * dens * jnp.sum(velocity * velocity, axis=0)
    )
    return jnp.concatenate([dens[None], velocity, pressure[None]], axis=0)


def entropy_fix(eigen_val, sound_speed):
    spread = entropy_share * sound_speed
    magnitude = jnp.abs(eigen_val)
    return jnp.where(
        magnitude >= spread, magnitude, (eigen_val * eigen_val + spread * spread) / (2.0 * spread)
    )


def euler_flux(dens, velocity, pressure, enthalpy, normal):
    normal_vel = velocity[normal]
    values = [dens * normal_vel]
    for component in range(3):
        moment = dens * velocity[component] * normal_vel
        if component == normal:
            moment = moment + pressure
        values.append(moment)
    values.append(dens * enthalpy * normal_vel)
    return values


def face_flux(left_cells, right_cells, normal):
    dens_left, vel_left, pres_left = (left_cells[0], left_cells[1:4], left_cells[4])
    dens_right, vel_right, pres_right = (right_cells[0], right_cells[1:4], right_cells[4])
    ratio = gamma_gas / (gamma_gas - 1.0)
    sq_left = jnp.sum(vel_left * vel_left, axis=0)
    sq_right = jnp.sum(vel_right * vel_right, axis=0)
    enth_left = ratio * pres_left / dens_left + 0.5 * sq_left
    enth_right = ratio * pres_right / dens_right + 0.5 * sq_right
    flux_left = euler_flux(dens_left, vel_left, pres_left, enth_left, normal)
    flux_right = euler_flux(dens_right, vel_right, pres_right, enth_right, normal)
    root_left = jnp.sqrt(dens_left)
    root_right = jnp.sqrt(dens_right)
    root_sum = root_left + root_right
    vel_roe = (root_left * vel_left + root_right * vel_right) / root_sum
    enth_roe = (root_left * enth_left + root_right * enth_right) / root_sum
    speed_sq = jnp.sum(vel_roe * vel_roe, axis=0)
    sound_sq = (gamma_gas - 1.0) * (enth_roe - 0.5 * speed_sq)
    sound_speed = jnp.sqrt(sound_sq)
    normal_vel = vel_roe[normal]
    dens_roe = root_left * root_right
    jump_dens = dens_right - dens_left
    jump_pres = pres_right - pres_left
    jump_vel = vel_right - vel_left
    jump_normal = jump_vel[normal]
    wave_slow = (jump_pres - dens_roe * sound_speed * jump_normal) / (2.0 * sound_sq)
    wave_fast = (jump_pres + dens_roe * sound_speed * jump_normal) / (2.0 * sound_sq)
    wave_mid = jump_dens - jump_pres / sound_sq
    eigen_mid = entropy_fix(normal_vel, sound_speed)
    flux_slow = entropy_fix(normal_vel - sound_speed, sound_speed) * wave_slow
    flux_fast = entropy_fix(normal_vel + sound_speed, sound_speed) * wave_fast
    dissipation = [flux_slow + eigen_mid * wave_mid + flux_fast]
    for component in range(3):
        unit_dir = 1.0 if component == normal else 0.0
        term = flux_slow * (vel_roe[component] - unit_dir * sound_speed)
        term = term + eigen_mid * (
            wave_mid * vel_roe[component]
            + dens_roe * (jump_vel[component] - unit_dir * jump_normal)
        )
        term = term + flux_fast * (vel_roe[component] + unit_dir * sound_speed)
        dissipation.append(term)
    shear_work = jnp.sum(vel_roe * jump_vel, axis=0) - normal_vel * jump_normal
    energy_term = flux_slow * (enth_roe - normal_vel * sound_speed)
    energy_term = energy_term + eigen_mid * (wave_mid * 0.5 * speed_sq + dens_roe * shear_work)
    energy_term = energy_term + flux_fast * (enth_roe + normal_vel * sound_speed)
    dissipation.append(energy_term)
    jump_temp = pres_right / dens_right - pres_left / dens_left
    jump_kin = 0.5 * (sq_right - sq_left)
    viscous_terms = [
        jnp.zeros_like(jump_dens),
        jump_vel[0],
        jump_vel[1],
        jump_vel[2],
        jump_kin + gamma_gas / ((gamma_gas - 1.0) * prandtl) * jump_temp,
    ]
    values = []
    for component in range(5):
        values.append(
            0.5 * (flux_left[component] + flux_right[component])
            - 0.5 * dissipation[component]
            - viscosity * viscous_terms[component]
        )
    return jnp.stack(values, axis=0)


def flux_change(padded, along, normal):
    length = padded.shape[along]
    face_values = face_flux(
        lax.slice_in_dim(padded, 0, length - 1, axis=along),
        lax.slice_in_dim(padded, 1, length, axis=along),
        normal,
    )
    return lax.slice_in_dim(face_values, 1, length - 1, axis=along) - lax.slice_in_dim(
        face_values, 0, length - 2, axis=along
    )


def spectral_entry(offset, number):
    wrapped = jnp.mod(offset, number)
    parity = 1.0 - 2.0 * jnp.mod(wrapped, 2).astype(jnp.float32)
    angles = math.pi * wrapped.astype(jnp.float32) / number
    sine_val = jnp.where(wrapped == 0, 1.0, jnp.sin(angles))
    derivative = jnp.where(
        wrapped == 0, 0.0, math.pi / number * parity * jnp.cos(angles) / sine_val
    )
    return derivative + 0.5 * parity


def on_device(flow_state, period_match):
    instances = lax.axis_size("inst")
    phase_lag = instances // 4
    instance = lax.axis_index("inst")
    space_parts = lax.axis_size("space")
    position = lax.axis_index("space")
    labels = jnp.arange(period_match.shape[0], dtype=jnp.int32)
    matches = (period_match[:, None] == labels[None, :]).astype(jnp.int32)
    inverse = jnp.sum(labels[:, None] * matches, axis=0)
    mirror = jnp.array([1.0, 1.0, 1.0, -1.0, 1.0], jnp.float32).reshape(5, 1, 1, 1)

    def lagged(plane, steps):
        return from_behind(plane, "inst", steps)

    def timewise(conserved_vars):
        pieces = lax.all_gather(conserved_vars[None], "inst", axis=0, tiled=True)
        number = pieces.shape[0]
        others = jnp.arange(number, dtype=jnp.int32)
        weights = spectral_entry(instance - others, instances)
        return jnp.tensordot(weights, pieces, axes=1, precision=lax.Precision.HIGHEST)

    def evaluate(conserved_vars):
        prims = primitive(conserved_vars)
        padded = extended(prims, (("space", 1),), 1)
        lower_edge = jnp.where(position == 0, prims[:, :1], padded[:, :1])
        upper_edge = jnp.where(position == space_parts - 1, prims[:, -1:], padded[:, -1:])
        along_axial = jnp.concatenate([lower_edge, prims, upper_edge], axis=1)
        along_span = jnp.concatenate(
            [prims[:, :, :1] * mirror, prims, prims[:, :, -1:] * mirror], axis=2
        )
        ghost_below = jnp.take(lagged(prims[..., -1], phase_lag), period_match, axis=2)
        ghost_above = jnp.take(lagged(prims[..., 0], -phase_lag), inverse, axis=2)
        along_pitch = jnp.concatenate(
            [ghost_below[..., None], prims, ghost_above[..., None]], axis=3
        )
        spatial = (
            flux_change(along_axial, 1, 0)
            + flux_change(along_span, 2, 2)
            + flux_change(along_pitch, 3, 1)
        )
        return timewise(conserved_vars) + spatial

    initial = conserved(from_draw(flow_state[0]))
    section_state = initial - pseudo_step * evaluate(initial)
    return evaluate(section_state)[None]


inst_count = 4
layers = 4
chunk = 32
rows = 16
lanes = 128
tile = (rows, lanes)
vmem = pl.BlockSpec(memory_space=pltpu.VMEM)
smem = pl.BlockSpec(memory_space=pltpu.SMEM)
starts = (1.0, 0.8, 0.0, 0.0, 0.8)
spreads_of = (0.3, 0.3, 0.3, 0.3, 0.2)
ratio = gamma_gas / (gamma_gas - 1.0)


def weight_of(distance):
    parity = 1.0 - 2.0 * (distance % 2)
    if distance == 0:
        return 0.5
    if 2 * distance == inst_count:
        return 0.5 * parity
    angle = math.pi * distance / inst_count
    return math.pi / inst_count * parity * math.cos(angle) / math.sin(angle) + 0.5 * parity


def lane_ids():
    return lax.broadcasted_iota(jnp.int32, tile, 1)


def row_ids():
    return lax.broadcasted_iota(jnp.int32, tile, 0)


def pick_lanes(values, index):
    return jnp.take_along_axis(values, index, axis=1, mode="promise_in_bounds")


def pick_rows(values, index):
    half = rows // 2
    low, high = values[:half], values[half:]
    parts = []
    for part in (index[:half], index[half:]):
        inner = jnp.bitwise_and(part, half - 1)
        from_low = jnp.take_along_axis(low, inner, axis=0, mode="promise_in_bounds")
        from_high = jnp.take_along_axis(high, inner, axis=0, mode="promise_in_bounds")
        parts.append(jnp.where(part < half, from_low, from_high))
    return jnp.concatenate(parts, axis=0)


def turn(values, amount):
    return pltpu.roll(values, amount % lanes if isinstance(amount, int) else amount, 1)


def mod_lanes(amount):
    return jnp.bitwise_and(amount, lanes - 1)


def pack_tile(layer_tiles, part):
    group = lane_ids() // chunk
    out = None
    for layer in range(layers):
        moved = turn(layer_tiles[layer], mod_lanes(chunk * (layer - part) + lanes))
        out = moved if out is None else jnp.where(group == layer, moved, out)
    return out


def pack_kernel(flow, *messages):
    me = lax.axis_index("inst")
    lane = lane_ids()
    slot = jnp.bitwise_and(lane, 3)
    step = jnp.where(slot < 2, slot - 2, slot + chunk - 2)
    for distance in range(inst_count):
        part = jnp.bitwise_xor(me, distance)
        index = mod_lanes(step + (chunk * part + lanes))
        edge = None
        for field in range(5):
            tiles = [flow[0, field, layer] for layer in range(layers)]
            messages[distance][field] = pack_tile(tiles, part)
            for layer in range(layers):
                got = pick_lanes(tiles[layer], index)
                here = lane // 4 == field * 4 + layer
                edge = got if edge is None else jnp.where(here, got, edge)
        messages[distance][5] = edge


def spread_tiles(received, field, me):
    group = lane_ids() // chunk
    outs = [None] * layers
    for distance in range(inst_count):
        part = jnp.bitwise_xor(me, distance)
        values = received[distance][field]
        for layer in range(layers):
            moved = turn(values, mod_lanes(chunk * (part - layer) + lanes))
            outs[layer] = moved if outs[layer] is None else jnp.where(group == part, moved, outs[layer])
    return outs


def unpack_kernel(*refs):
    received, (main, halo, near_a, near_b) = refs[:4], refs[4:]
    me = lax.axis_index("inst")
    even = jnp.bitwise_and(lax.axis_index("space"), 1) == 0
    lane = lane_ids()
    owner = jnp.bitwise_and(lane // 4, 3)
    level = lane // 16 - 1
    inner = jnp.clip(level, 0, layers - 1) * 4 + jnp.bitwise_and(lane, 3)
    up_edge = down_edge = None
    for field in range(5):
        tiles = spread_tiles(received, field, me)
        for layer in range(layers):
            main[field, layer] = tiles[layer]
        for place in range(2):
            near_a[2 * field + place] = jnp.where(even, tiles[2 + place], tiles[place])
            near_b[2 * field + place] = jnp.where(even, tiles[place], tiles[2 + place])
        edges = None
        for distance in range(inst_count):
            part = jnp.bitwise_xor(me, distance)
            got = pick_lanes(received[distance][5], inner + 16 * field)
            edges = got if edges is None else jnp.where(owner == part, got, edges)
        halo[field] = edges
        up = turn(edges, 16 * field - 16 * layers)
        down = turn(edges, 16 * field - 16)
        here = lane // 16 == field
        up_edge = up if up_edge is None else jnp.where(here, up, up_edge)
        down_edge = down if down_edge is None else jnp.where(here, down, down_edge)
    near_a[10] = jnp.where(even, up_edge, down_edge)
    near_b[10] = jnp.where(even, down_edge, up_edge)


class Cells:
    def __init__(self, parts):
        self.parts = list(parts)
        self.dens, self.vel, self.pres = parts[0], list(parts[1:4]), parts[4]
        self.root, self.enth, self.heat = parts[5], parts[6], parts[7]

    def map(self, change):
        return Cells([change(part) for part in self.parts])

    def conserved(self):
        dens, enth = self.dens, self.enth
        return [dens] + [dens * part for part in self.vel] + [dens * enth - self.pres]


def cells_of(dens, vel, pres):
    inverse_root = lax.rsqrt(dens)
    root = dens * inverse_root
    temp = pres * (inverse_root * inverse_root)
    kinetic = 0.5 * (vel[0] * vel[0] + vel[1] * vel[1] + vel[2] * vel[2])
    enth = ratio * temp + kinetic
    heat = 2.0 * viscosity * (kinetic + ratio / prandtl * temp)
    return Cells([dens] + list(vel) + [pres, root, enth, heat])


def cells_of_draws(draws):
    start = [base + spread * draw if base else spread * draw for base, spread, draw in zip(starts, spreads_of, draws)]
    return cells_of(start[0], start[1:4], start[4])


def cells_of_conserved(state):
    dens = state[0]
    inverse = 1.0 / dens
    vel = [part * inverse for part in state[1:4]]
    kinetic = vel[0] * vel[0] + vel[1] * vel[1] + vel[2] * vel[2]
    pres = (gamma_gas - 1.0) * (state[4] - 0.5 * dens * kinetic)
    return cells_of(dens, vel, pres)


def roe_flux(low, high, normal):
    jump_dens = high.dens - low.dens
    jump_pres = high.pres - low.pres
    jump = [b - a for a, b in zip(low.vel, high.vel)]
    share = high.root / (low.root + high.root)
    vel = [a + share * d for a, d in zip(low.vel, jump)]
    enth = low.enth + share * (high.enth - low.enth)
    half_sq = 0.5 * (vel[0] * vel[0] + vel[1] * vel[1] + vel[2] * vel[2])
    sound_sq = (gamma_gas - 1.0) * (enth - half_sq)
    inverse = lax.rsqrt(sound_sq)
    sound = sound_sq * inverse
    dens_roe = low.root * high.root
    along = vel[normal]
    jump_along = jump[normal]
    press_part = jump_pres * (inverse * inverse)
    speed_part = dens_roe * inverse * jump_along
    bound = entropy_share * sound
    curve = (0.5 / entropy_share) * inverse
    floor = 0.5 * bound

    def fixed(speed):
        size = jnp.abs(speed)
        return jnp.where(size >= bound, size, speed * speed * curve + floor)

    slow = 0.5 * fixed(along - sound) * (press_part - speed_part)
    fast = 0.5 * fixed(along + sound) * (press_part + speed_part)
    middle = fixed(along)
    entropy = middle * (jump_dens - press_part)
    both = slow + fast
    total = both + entropy
    push = sound * (fast - slow)
    shear = middle * dens_roe
    mass_low = low.dens * low.vel[normal]
    mass_high = high.dens * high.vel[normal]
    out = [mass_low + mass_high - total]
    work = None
    for part in range(3):
        value = mass_low * low.vel[part] + mass_high * high.vel[part] - vel[part] * total
        if part == normal:
            value = value + (low.pres + high.pres) - push - (2.0 * viscosity) * jump_along
        else:
            value = value - (shear + 2.0 * viscosity) * jump[part]
            term = vel[part] * jump[part]
            work = term if work is None else work + term
        out.append(value)
    lost = enth * both + along * push + entropy * half_sq + shear * work
    out.append(mass_low * low.enth + mass_high * high.enth - lost - (high.heat - low.heat))
    return out


def span_change(cells):
    row = row_ids()
    faces = roe_flux(cells, cells.map(lambda part: pltpu.roll(part, rows - 1, 0)), 2)
    w = cells.vel[2]
    sound_sq = (gamma_gas - 1.0) * (cells.enth - 0.5 * (cells.vel[0] * cells.vel[0] + cells.vel[1] * cells.vel[1]))
    sound = sound_sq * lax.rsqrt(sound_sq)
    still = 2.0 * (cells.dens * w * w + cells.pres)
    moving = 2.0 * w * (sound * cells.dens + 2.0 * viscosity)
    changes = []
    for part in range(5):
        top = still + moving if part == 3 else 0.0
        bottom = still - moving if part == 3 else 0.0
        upper = jnp.where(row == rows - 1, top, faces[part])
        lower = jnp.where(row == 0, bottom, pltpu.roll(faces[part], 1, 0))
        changes.append(upper - lower)
    return changes


def over_instances(values):
    out = weight_of(0) * values
    for distance in range(1, inst_count):
        out = out + weight_of(distance) * turn(values, chunk * distance)
    return out


def shift_slots(values, distance):
    owner = jnp.bitwise_and(lane_ids() // 4, 3)
    distance = distance % inst_count
    return jnp.where(owner >= distance, turn(values, 4 * distance), turn(values, 4 * distance - 16))


def over_slots(values):
    out = weight_of(0) * values
    for distance in range(1, inst_count):
        out = out + weight_of(distance) * shift_slots(values, distance)
    return out


def put(ref, place, cells):
    for number, part in enumerate(cells.parts):
        ref[place, number] = part


def get(ref, place):
    return Cells([ref[place, number] for number in range(8)])


def main_kernel(match, main, halo, near_a, near_b, *refs):
    messages, (first, second, edge_faces) = refs[:4], refs[4:]
    me = lax.axis_index("inst")
    where_on = lax.axis_index("space")
    parts_on = lax.axis_size("space")
    even = jnp.bitwise_and(where_on, 1) == 0
    at_low = where_on == 0
    at_high = where_on == parts_on - 1
    lag = inst_count // 4
    lane = lane_ids()
    row = row_ids()
    slot = jnp.bitwise_and(lane, 3)
    owner_main = lane // chunk
    column = jnp.bitwise_and(lane, chunk - 1)
    is_first, is_last = column == 0, column == chunk - 1
    seam_slot = jnp.where(me == 0, 1, jnp.where(me == inst_count - 1, 3, -1))
    seam = slot == seam_slot
    below_of = jnp.zeros(tile, jnp.int32)
    above_of = jnp.zeros(tile, jnp.int32)
    for k in range(rows):
        value = match[k]
        below_of = jnp.where(row == k, value, below_of)
        above_of = jnp.where(row == value, k, above_of)

    def edge_lane(layer):
        return (layer + 1) * 16 + owner_main * 4 + jnp.where(is_first, 1, 3)

    near = [[jnp.where(even, b[...], a[...]) for a, b in ((near_a.at[j], near_b.at[j]),)][0] for j in range(11)]
    far = [[jnp.where(even, a[...], b[...]) for a, b in ((near_a.at[j], near_b.at[j]),)][0] for j in range(11)]
    for layer in range(layers):
        put(first, layer + 2, cells_of_draws([main[field, layer] for field in range(5)]))
    for place in range(2):
        draws = [jnp.where(at_low, main[field, 0], near[2 * field + place]) for field in range(5)]
        put(first, place, cells_of_draws(draws))
        draws = [jnp.where(at_high, main[field, layers - 1], far[2 * field + place]) for field in range(5)]
        put(first, layers + 2 + place, cells_of_draws(draws))
    band = lane // 16
    edges = []
    for field in range(5):
        inside = halo[field]
        low = jnp.where(at_low, turn(inside, -16), turn(near[10], -16 * field))
        high = jnp.where(at_high, turn(inside, 16), turn(far[10], 16 * (layers + 1 - field)))
        edges.append(jnp.where(band == 0, low, jnp.where(band == layers + 1, high, inside)))
    edge_cells = cells_of_draws(edges)

    def mains_at_slots(ref, start, low, high):
        group = jnp.bitwise_and(lane // 4, 3) * chunk
        index = group + jnp.where(slot == 1, 0, chunk - 1)
        out = [None] * 8
        for layer in range(low, high):
            for number in range(8):
                got = pick_lanes(ref[layer + start, number], index)
                out[number] = got if out[number] is None else jnp.where(band == layer + 1, got, out[number])
        return Cells(out)

    def pitch_edges(cells, mains):
        lower = Cells([jnp.where(slot == 3, b, a) for a, b in zip(cells.parts, mains.parts)])
        upper = []
        for a, b in zip(cells.parts, mains.parts):
            value = jnp.where(slot == 3, turn(a, 1), turn(a, -1))
            value = jnp.where(slot == 1, b, value)
            other = pick_rows(shift_slots(value, -lag), above_of)
            upper.append(jnp.where(seam, other, value))
        faces = roe_flux(lower, Cells(upper), 1)
        lower_use = [jnp.where(seam, pick_rows(shift_slots(face, lag), below_of), face) for face in faces]
        return faces, lower_use

    def pitch_change(cells, layer):
        faces = roe_flux(cells, cells.map(lambda part: turn(part, -1)), 1)
        index = edge_lane(layer)
        changes = []
        for part in range(5):
            edge = pick_lanes(edge_faces[part], index)
            upper = jnp.where(is_last, edge, faces[part])
            lower = jnp.where(is_first, edge, turn(faces[part], 1))
            changes.append(upper - lower)
        return changes

    def set_edges(faces, lower_use):
        for part in range(5):
            edge_faces[part] = jnp.where(slot == 1, lower_use[part], faces[part])

    faces, lower_use = pitch_edges(edge_cells, mains_at_slots(first, 2, -1, layers + 1))
    set_edges(faces, lower_use)
    span = span_change(edge_cells)
    axial = roe_flux(edge_cells, edge_cells.map(lambda part: turn(part, -16)), 0)
    state = edge_cells.conserved()
    for part in range(5):
        pitch = jnp.where(slot == 1, faces[part] - turn(faces[part], 1), faces[part] - turn(lower_use[part], -1))
        change = pitch + span[part] + (axial[part] - turn(axial[part], 16))
        state[part] = state[part] - pseudo_step * over_slots(state[part]) - (0.5 * pseudo_step) * change
    edge_second = cells_of_conserved(state)

    def first_step(count, below):
        cells = get(first, count + 1)
        above = roe_flux(cells, get(first, count + 2), 0)
        span = span_change(cells)
        pitch = pitch_change(cells, count - 1)
        state = cells.conserved()
        for part in range(5):
            change = (above[part] - below[part]) + span[part] + pitch[part]
            state[part] = state[part] - pseudo_step * over_instances(state[part]) - (0.5 * pseudo_step) * change
        put(second, count, cells_of_conserved(state))
        return above

    lax.fori_loop(0, layers + 2, first_step, roe_flux(get(first, 0), get(first, 1), 0))

    for number in range(8):
        second[0, number] = jnp.where(at_low, second[1, number], second[0, number])
        second[layers + 1, number] = jnp.where(at_high, second[layers, number], second[layers + 1, number])

    set_edges(*pitch_edges(edge_second, mains_at_slots(second, 1, 0, layers)))

    def second_step(layer, below):
        cells = get(second, layer + 1)
        above = roe_flux(cells, get(second, layer + 2), 0)
        span = span_change(cells)
        pitch = pitch_change(cells, layer)
        state = cells.conserved()
        for part in range(5):
            change = (above[part] - below[part]) + span[part] + pitch[part]
            first[layer, part] = over_instances(state[part]) + 0.5 * change
        return above

    lax.fori_loop(0, layers, second_step, roe_flux(get(second, 0), get(second, 1), 0))
    for distance in range(inst_count):
        part = jnp.bitwise_xor(me, distance)
        for field in range(5):
            messages[distance][field] = pack_tile([first[layer, field] for layer in range(layers)], part)


def return_kernel(*refs):
    received, out = refs[:4], refs[4]
    me = lax.axis_index("inst")
    for field in range(5):
        for layer, values in enumerate(spread_tiles(received, field, me)):
            out[0, field, layer] = values


def call(kernel, outs, operands, scratch=(), scalars=0):
    shapes = [jax.ShapeDtypeStruct(shape, jnp.float32) for shape in outs]
    return pl.pallas_call(
        kernel,
        out_shape=shapes,
        in_specs=[smem] * scalars + [vmem] * (len(operands) - scalars),
        out_specs=[vmem] * len(shapes),
        scratch_shapes=scratch,
        compiler_params=pltpu.CompilerParams(vmem_limit_bytes=16 * 2**20),
    )(*operands)


def swap_instances(messages):
    got = [messages[0]] + [None] * (inst_count - 1)
    for distance in (2, 3, 1):
        route = [(i, i ^ distance) for i in range(inst_count)]
        got[distance] = lax.ppermute(messages[distance], "inst", route)
    return got


def on_device_fast(flow_state, period_match):
    count = lax.axis_size("space")
    messages = call(pack_kernel, [(6, rows, lanes)] * inst_count, [flow_state])
    main, halo, near_a, near_b = call(
        unpack_kernel,
        [(5, layers, rows, lanes), (5, rows, lanes), (11, rows, lanes), (11, rows, lanes)],
        swap_instances(messages),
    )
    route_a = [(i, i ^ 1) for i in range(count)]
    route_b = [(i, ((i - 1) ^ 1) + 1) if 0 < i < count - 1 else (i, count - 1 - i) for i in range(count)]
    near_b = lax.ppermute(near_b, "space", route_b)
    near_a = lax.ppermute(near_a, "space", route_a)
    results = call(
        main_kernel,
        [(5, rows, lanes)] * inst_count,
        [period_match, main, halo, near_a, near_b],
        [
            pltpu.VMEM((layers + 4, 8, rows, lanes), jnp.float32),
            pltpu.VMEM((layers + 2, 8, rows, lanes), jnp.float32),
            pltpu.VMEM((5, rows, lanes), jnp.float32),
        ],
        scalars=1,
    )
    return call(return_kernel, [flow_state.shape], swap_instances(results))[0]


def solution(mesh):
    in_specs = (P(("groups", "inst"), None, "space", None, None), P())
    out_specs = P(("groups", "inst"), None, "space", None, None)

    def whole(flow_state, period_match):
        block = (flow_state.shape[2] // mesh.shape["space"],) + flow_state.shape[3:]
        fits = mesh.shape["inst"] == inst_count and mesh.shape["space"] % 2 == 0
        body = on_device_fast if fits and block == (layers, rows, lanes) else on_device
        return jax.shard_map(body, mesh=mesh, in_specs=in_specs, out_specs=out_specs, check_vma=False)(
            flow_state, period_match
        )

    return whole
```

```python
import math

import jax
import jax.numpy as jnp
from jax import lax
from jax.experimental import pallas as pl
from jax.experimental.pallas import tpu as pltpu
from jax.sharding import PartitionSpec as P

gamma_gas = 1.4
prandtl = 0.72
viscosity = 0.1
pseudo_step = 0.03
entropy_share = 0.1


def from_behind(block, axis, distance):
    devices = range(lax.axis_size(axis))
    route = [((i - distance) % len(devices), i) for i in devices]
    return lax.ppermute(block, axis, route)


def extended(cells, sides, width):
    for axis, dim in sides:
        count = lax.axis_size(axis)
        ends = count - 1
        head = lax.slice_in_dim(cells, 0, width, axis=dim)
        tail = lax.slice_in_dim(cells, cells.shape[dim] - width, cells.shape[dim], axis=dim)
        cells = jnp.concatenate(
            [
                lax.ppermute(tail, axis, [(i, (i + 1) % count) for i in range(ends)]),
                cells,
                lax.ppermute(head, axis, [((i + 1) % count, i) for i in range(ends)]),
            ],
            axis=dim,
        )
    return cells


def from_draw(draws):
    shape = (5,) + (1,) * (draws.ndim - 1)
    offsets = jnp.array([1.0, 0.8, 0.0, 0.0, 0.8], jnp.float32).reshape(shape)
    spreads = jnp.array([0.3, 0.3, 0.3, 0.3, 0.2], jnp.float32).reshape(shape)
    return offsets + spreads * draws


def conserved(primitives):
    dens = primitives[0]
    velocity = primitives[1:4]
    kinetic = 0.5 * dens * jnp.sum(velocity * velocity, axis=0)
    energy = primitives[4] / (gamma_gas - 1.0) + kinetic
    return jnp.concatenate([dens[None], dens[None] * velocity, energy[None]], axis=0)


def primitive(conserved_vars):
    dens = conserved_vars[0]
    velocity = conserved_vars[1:4] / dens
    pressure = (gamma_gas - 1.0) * (
        conserved_vars[4] - 0.5 * dens * jnp.sum(velocity * velocity, axis=0)
    )
    return jnp.concatenate([dens[None], velocity, pressure[None]], axis=0)


def entropy_fix(eigen_val, sound_speed):
    spread = entropy_share * sound_speed
    magnitude = jnp.abs(eigen_val)
    return jnp.where(
        magnitude >= spread, magnitude, (eigen_val * eigen_val + spread * spread) / (2.0 * spread)
    )


def euler_flux(dens, velocity, pressure, enthalpy, normal):
    normal_vel = velocity[normal]
    values = [dens * normal_vel]
    for component in range(3):
        moment = dens * velocity[component] * normal_vel
        if component == normal:
            moment = moment + pressure
        values.append(moment)
    values.append(dens * enthalpy * normal_vel)
    return values


def face_flux(left_cells, right_cells, normal):
    dens_left, vel_left, pres_left = (left_cells[0], left_cells[1:4], left_cells[4])
    dens_right, vel_right, pres_right = (right_cells[0], right_cells[1:4], right_cells[4])
    ratio = gamma_gas / (gamma_gas - 1.0)
    sq_left = jnp.sum(vel_left * vel_left, axis=0)
    sq_right = jnp.sum(vel_right * vel_right, axis=0)
    enth_left = ratio * pres_left / dens_left + 0.5 * sq_left
    enth_right = ratio * pres_right / dens_right + 0.5 * sq_right
    flux_left = euler_flux(dens_left, vel_left, pres_left, enth_left, normal)
    flux_right = euler_flux(dens_right, vel_right, pres_right, enth_right, normal)
    root_left = jnp.sqrt(dens_left)
    root_right = jnp.sqrt(dens_right)
    root_sum = root_left + root_right
    vel_roe = (root_left * vel_left + root_right * vel_right) / root_sum
    enth_roe = (root_left * enth_left + root_right * enth_right) / root_sum
    speed_sq = jnp.sum(vel_roe * vel_roe, axis=0)
    sound_sq = (gamma_gas - 1.0) * (enth_roe - 0.5 * speed_sq)
    sound_speed = jnp.sqrt(sound_sq)
    normal_vel = vel_roe[normal]
    dens_roe = root_left * root_right
    jump_dens = dens_right - dens_left
    jump_pres = pres_right - pres_left
    jump_vel = vel_right - vel_left
    jump_normal = jump_vel[normal]
    wave_slow = (jump_pres - dens_roe * sound_speed * jump_normal) / (2.0 * sound_sq)
    wave_fast = (jump_pres + dens_roe * sound_speed * jump_normal) / (2.0 * sound_sq)
    wave_mid = jump_dens - jump_pres / sound_sq
    eigen_mid = entropy_fix(normal_vel, sound_speed)
    flux_slow = entropy_fix(normal_vel - sound_speed, sound_speed) * wave_slow
    flux_fast = entropy_fix(normal_vel + sound_speed, sound_speed) * wave_fast
    dissipation = [flux_slow + eigen_mid * wave_mid + flux_fast]
    for component in range(3):
        unit_dir = 1.0 if component == normal else 0.0
        term = flux_slow * (vel_roe[component] - unit_dir * sound_speed)
        term = term + eigen_mid * (
            wave_mid * vel_roe[component]
            + dens_roe * (jump_vel[component] - unit_dir * jump_normal)
        )
        term = term + flux_fast * (vel_roe[component] + unit_dir * sound_speed)
        dissipation.append(term)
    shear_work = jnp.sum(vel_roe * jump_vel, axis=0) - normal_vel * jump_normal
    energy_term = flux_slow * (enth_roe - normal_vel * sound_speed)
    energy_term = energy_term + eigen_mid * (wave_mid * 0.5 * speed_sq + dens_roe * shear_work)
    energy_term = energy_term + flux_fast * (enth_roe + normal_vel * sound_speed)
    dissipation.append(energy_term)
    jump_temp = pres_right / dens_right - pres_left / dens_left
    jump_kin = 0.5 * (sq_right - sq_left)
    viscous_terms = [
        jnp.zeros_like(jump_dens),
        jump_vel[0],
        jump_vel[1],
        jump_vel[2],
        jump_kin + gamma_gas / ((gamma_gas - 1.0) * prandtl) * jump_temp,
    ]
    values = []
    for component in range(5):
        values.append(
            0.5 * (flux_left[component] + flux_right[component])
            - 0.5 * dissipation[component]
            - viscosity * viscous_terms[component]
        )
    return jnp.stack(values, axis=0)


def flux_change(padded, along, normal):
    length = padded.shape[along]
    face_values = face_flux(
        lax.slice_in_dim(padded, 0, length - 1, axis=along),
        lax.slice_in_dim(padded, 1, length, axis=along),
        normal,
    )
    return lax.slice_in_dim(face_values, 1, length - 1, axis=along) - lax.slice_in_dim(
        face_values, 0, length - 2, axis=along
    )


def spectral_entry(offset, number):
    wrapped = jnp.mod(offset, number)
    parity = 1.0 - 2.0 * jnp.mod(wrapped, 2).astype(jnp.float32)
    angles = math.pi * wrapped.astype(jnp.float32) / number
    sine_val = jnp.where(wrapped == 0, 1.0, jnp.sin(angles))
    derivative = jnp.where(
        wrapped == 0, 0.0, math.pi / number * parity * jnp.cos(angles) / sine_val
    )
    return derivative + 0.5 * parity


def on_device(flow_state, period_match):
    instances = lax.axis_size("inst")
    phase_lag = instances // 4
    instance = lax.axis_index("inst")
    space_parts = lax.axis_size("space")
    position = lax.axis_index("space")
    labels = jnp.arange(period_match.shape[0], dtype=jnp.int32)
    matches = (period_match[:, None] == labels[None, :]).astype(jnp.int32)
    inverse = jnp.sum(labels[:, None] * matches, axis=0)
    mirror = jnp.array([1.0, 1.0, 1.0, -1.0, 1.0], jnp.float32).reshape(5, 1, 1, 1)

    def lagged(plane, steps):
        return from_behind(plane, "inst", steps)

    def timewise(conserved_vars):
        pieces = lax.all_gather(conserved_vars[None], "inst", axis=0, tiled=True)
        number = pieces.shape[0]
        others = jnp.arange(number, dtype=jnp.int32)
        weights = spectral_entry(instance - others, instances)
        return jnp.tensordot(weights, pieces, axes=1, precision=lax.Precision.HIGHEST)

    def evaluate(conserved_vars):
        prims = primitive(conserved_vars)
        padded = extended(prims, (("space", 1),), 1)
        lower_edge = jnp.where(position == 0, prims[:, :1], padded[:, :1])
        upper_edge = jnp.where(position == space_parts - 1, prims[:, -1:], padded[:, -1:])
        along_axial = jnp.concatenate([lower_edge, prims, upper_edge], axis=1)
        along_span = jnp.concatenate(
            [prims[:, :, :1] * mirror, prims, prims[:, :, -1:] * mirror], axis=2
        )
        ghost_below = jnp.take(lagged(prims[..., -1], phase_lag), period_match, axis=2)
        ghost_above = jnp.take(lagged(prims[..., 0], -phase_lag), inverse, axis=2)
        along_pitch = jnp.concatenate(
            [ghost_below[..., None], prims, ghost_above[..., None]], axis=3
        )
        spatial = (
            flux_change(along_axial, 1, 0)
            + flux_change(along_span, 2, 2)
            + flux_change(along_pitch, 3, 1)
        )
        return timewise(conserved_vars) + spatial

    initial = conserved(from_draw(flow_state[0]))
    section_state = initial - pseudo_step * evaluate(initial)
    return evaluate(section_state)[None]


inst_count = 4
layers = 4
chunk = 32
rows = 16
lanes = 128
tile = (rows, lanes)
vmem = pl.BlockSpec(memory_space=pltpu.VMEM)
smem = pl.BlockSpec(memory_space=pltpu.SMEM)
starts = (1.0, 0.8, 0.0, 0.0, 0.8)
spreads_of = (0.3, 0.3, 0.3, 0.3, 0.2)
ratio = gamma_gas / (gamma_gas - 1.0)


def weight_of(distance):
    parity = 1.0 - 2.0 * (distance % 2)
    if distance == 0:
        return 0.5
    if 2 * distance == inst_count:
        return 0.5 * parity
    angle = math.pi * distance / inst_count
    return math.pi / inst_count * parity * math.cos(angle) / math.sin(angle) + 0.5 * parity


order = (2, 3, 1, 0)


def in_order(items):
    return [items[order.index(distance)] for distance in range(inst_count)]


def unrolled(count, body, carry=None):
    for number in range(count):
        carry = body(number, carry)
    return carry


def lane_ids():
    return lax.broadcasted_iota(jnp.int32, tile, 1)


def row_ids():
    return lax.broadcasted_iota(jnp.int32, tile, 0)


def pick_lanes(values, index):
    return jnp.take_along_axis(values, index, axis=1, mode="promise_in_bounds")


def pick_rows(values, index):
    half = rows // 2
    low, high = values[:half], values[half:]
    parts = []
    for part in (index[:half], index[half:]):
        inner = jnp.bitwise_and(part, half - 1)
        from_low = jnp.take_along_axis(low, inner, axis=0, mode="promise_in_bounds")
        from_high = jnp.take_along_axis(high, inner, axis=0, mode="promise_in_bounds")
        parts.append(jnp.where(part < half, from_low, from_high))
    return jnp.concatenate(parts, axis=0)


def turn(values, amount):
    return pltpu.roll(values, amount % lanes if isinstance(amount, int) else amount, 1)


def mod_lanes(amount):
    return jnp.bitwise_and(amount, lanes - 1)


def pack_tile(layer_tiles, part):
    group = lane_ids() // chunk
    out = None
    for layer in range(layers):
        moved = turn(layer_tiles[layer], mod_lanes(chunk * (layer - part) + lanes))
        out = moved if out is None else jnp.where(group == layer, moved, out)
    return out


def pack_kernel(flow, *refs):
    messages = in_order(refs)
    me = lax.axis_index("inst")
    lane = lane_ids()
    slot = jnp.bitwise_and(lane, 3)
    step = jnp.where(slot < 2, slot - 2, slot + chunk - 2)
    parts = [jnp.bitwise_xor(me, distance) for distance in range(inst_count)]
    index = [mod_lanes(step + (chunk * part + lanes)) for part in parts]

    def one_field(field, edges):
        tiles = [flow[0, field, layer] for layer in range(layers)]
        edges = list(edges)
        for distance, part in enumerate(parts):
            messages[distance][field] = pack_tile(tiles, part)
            for layer in range(layers):
                here = lane // 4 == field * 4 + layer
                edges[distance] = jnp.where(here, pick_lanes(tiles[layer], index[distance]), edges[distance])
        return tuple(edges)

    edges = unrolled(5, one_field, (jnp.zeros(tile, jnp.float32),) * inst_count)
    for distance in range(inst_count):
        messages[distance][5] = edges[distance]


def spread_tiles(received, field, me):
    group = lane_ids() // chunk
    outs = [None] * layers
    for distance in range(inst_count):
        part = jnp.bitwise_xor(me, distance)
        values = received[distance][field]
        for layer in range(layers):
            moved = turn(values, mod_lanes(chunk * (part - layer) + lanes))
            outs[layer] = moved if outs[layer] is None else jnp.where(group == part, moved, outs[layer])
    return outs


def unpack_kernel(*refs):
    received, (near_b, near_a, main, halo) = in_order(refs[:4]), refs[4:]
    me = lax.axis_index("inst")
    even = jnp.bitwise_and(lax.axis_index("space"), 1) == 0
    lane = lane_ids()
    owner = jnp.bitwise_and(lane // 4, 3)
    level = lane // 16 - 1
    inner = jnp.clip(level, 0, layers - 1) * 4 + jnp.bitwise_and(lane, 3)

    def one_field(field, ends):
        tiles = spread_tiles(received, field, me)
        for layer in range(layers):
            main[field, layer] = tiles[layer]
        for place in range(2):
            near_a[2 * field + place] = jnp.where(even, tiles[2 + place], tiles[place])
            near_b[2 * field + place] = jnp.where(even, tiles[place], tiles[2 + place])
        edges = None
        for distance in range(inst_count):
            part = jnp.bitwise_xor(me, distance)
            got = pick_lanes(received[distance][5], inner + 16 * field)
            edges = got if edges is None else jnp.where(owner == part, got, edges)
        halo[field] = edges
        here = lane // 16 == field
        up = turn(edges, mod_lanes(16 * field - 16 * layers + lanes))
        down = turn(edges, mod_lanes(16 * field - 16 + lanes))
        return jnp.where(here, up, ends[0]), jnp.where(here, down, ends[1])

    up_edge, down_edge = unrolled(5, one_field, (jnp.zeros(tile, jnp.float32),) * 2)
    near_a[10] = jnp.where(even, up_edge, down_edge)
    near_b[10] = jnp.where(even, down_edge, up_edge)


class Cells:
    def __init__(self, parts):
        self.parts = list(parts)
        self.dens, self.vel, self.pres = parts[0], list(parts[1:4]), parts[4]
        self.root, self.enth, self.heat = parts[5], parts[6], parts[7]

    def map(self, change):
        return Cells([change(part) for part in self.parts])

    def conserved(self):
        dens, enth = self.dens, self.enth
        return [dens] + [dens * part for part in self.vel] + [dens * enth - self.pres]


def cells_of(dens, vel, pres):
    inverse_root = lax.rsqrt(dens)
    root = dens * inverse_root
    temp = pres * (inverse_root * inverse_root)
    kinetic = 0.5 * (vel[0] * vel[0] + vel[1] * vel[1] + vel[2] * vel[2])
    enth = ratio * temp + kinetic
    heat = 2.0 * viscosity * (kinetic + ratio / prandtl * temp)
    return Cells([dens] + list(vel) + [pres, root, enth, heat])


def cells_of_draws(draws):
    start = [base + spread * draw if base else spread * draw for base, spread, draw in zip(starts, spreads_of, draws)]
    return cells_of(start[0], start[1:4], start[4])


def cells_of_conserved(state):
    dens = state[0]
    inverse = 1.0 / dens
    vel = [part * inverse for part in state[1:4]]
    kinetic = vel[0] * vel[0] + vel[1] * vel[1] + vel[2] * vel[2]
    pres = (gamma_gas - 1.0) * (state[4] - 0.5 * dens * kinetic)
    return cells_of(dens, vel, pres)


def roe_flux(low, high, normal):
    jump_dens = high.dens - low.dens
    jump_pres = high.pres - low.pres
    jump = [b - a for a, b in zip(low.vel, high.vel)]
    share = high.root / (low.root + high.root)
    vel = [a + share * d for a, d in zip(low.vel, jump)]
    enth = low.enth + share * (high.enth - low.enth)
    half_sq = 0.5 * (vel[0] * vel[0] + vel[1] * vel[1] + vel[2] * vel[2])
    sound_sq = (gamma_gas - 1.0) * (enth - half_sq)
    inverse = lax.rsqrt(sound_sq)
    sound = sound_sq * inverse
    dens_roe = low.root * high.root
    along = vel[normal]
    jump_along = jump[normal]
    press_part = jump_pres * (inverse * inverse)
    speed_part = dens_roe * inverse * jump_along
    bound = entropy_share * sound
    curve = (0.5 / entropy_share) * inverse
    floor = 0.5 * bound

    def fixed(speed):
        size = jnp.abs(speed)
        return jnp.where(size >= bound, size, speed * speed * curve + floor)

    slow = 0.5 * fixed(along - sound) * (press_part - speed_part)
    fast = 0.5 * fixed(along + sound) * (press_part + speed_part)
    middle = fixed(along)
    entropy = middle * (jump_dens - press_part)
    both = slow + fast
    total = both + entropy
    push = sound * (fast - slow)
    shear = middle * dens_roe
    mass_low = low.dens * low.vel[normal]
    mass_high = high.dens * high.vel[normal]
    out = [mass_low + mass_high - total]
    work = None
    for part in range(3):
        value = mass_low * low.vel[part] + mass_high * high.vel[part] - vel[part] * total
        if part == normal:
            value = value + (low.pres + high.pres) - push - (2.0 * viscosity) * jump_along
        else:
            value = value - (shear + 2.0 * viscosity) * jump[part]
            term = vel[part] * jump[part]
            work = term if work is None else work + term
        out.append(value)
    lost = enth * both + along * push + entropy * half_sq + shear * work
    out.append(mass_low * low.enth + mass_high * high.enth - lost - (high.heat - low.heat))
    return out


def span_change(cells):
    row = row_ids()
    faces = roe_flux(cells, cells.map(lambda part: pltpu.roll(part, rows - 1, 0)), 2)
    w = cells.vel[2]
    sound_sq = (gamma_gas - 1.0) * (cells.enth - 0.5 * (cells.vel[0] * cells.vel[0] + cells.vel[1] * cells.vel[1]))
    sound = sound_sq * lax.rsqrt(sound_sq)
    still = 2.0 * (cells.dens * w * w + cells.pres)
    moving = 2.0 * w * (sound * cells.dens + 2.0 * viscosity)
    changes = []
    for part in range(5):
        top = still + moving if part == 3 else 0.0
        bottom = still - moving if part == 3 else 0.0
        upper = jnp.where(row == rows - 1, top, faces[part])
        lower = jnp.where(row == 0, bottom, pltpu.roll(faces[part], 1, 0))
        changes.append(upper - lower)
    return changes


def over_instances(values):
    out = weight_of(0) * values
    for distance in range(1, inst_count):
        out = out + weight_of(distance) * turn(values, chunk * distance)
    return out


def shift_slots(values, distance):
    owner = jnp.bitwise_and(lane_ids() // 4, 3)
    distance = distance % inst_count
    return jnp.where(owner >= distance, turn(values, 4 * distance), turn(values, 4 * distance - 16))


def over_slots(values):
    out = weight_of(0) * values
    for distance in range(1, inst_count):
        out = out + weight_of(distance) * shift_slots(values, distance)
    return out


def put(ref, place, cells):
    for number, part in enumerate(cells.parts):
        ref[place, number] = part


def get(ref, place):
    return Cells([ref[place, number] for number in range(8)])


class Pitch:
    def __init__(self, above, below, edge_faces):
        self.above, self.below, self.edge_faces = above, below, edge_faces
        self.lag = inst_count // 4
        me = lax.axis_index("inst")
        lane = lane_ids()
        self.slot = jnp.bitwise_and(lane, 3)
        self.band = lane // 16
        column = jnp.bitwise_and(lane, chunk - 1)
        self.is_first, self.is_last = column == 0, column == chunk - 1
        self.seam = self.slot == jnp.where(me == 0, 1, jnp.where(me == inst_count - 1, 3, -1))
        self.to_main = (lane // chunk) * 4 + jnp.where(self.is_first, 1, 3)
        self.from_main = jnp.bitwise_and(lane // 4, 3) * chunk + jnp.where(self.slot == 1, 0, chunk - 1)

    def mains(self, ref, places):
        out = [None] * 8
        for layer, place in places:
            for number in range(8):
                got = pick_lanes(ref[place, number], self.from_main)
                out[number] = got if out[number] is None else jnp.where(self.band == layer + 1, got, out[number])
        return Cells(out)

    def edges(self, cells, mains):
        slot = self.slot
        lower = Cells([jnp.where(slot == 3, b, a) for a, b in zip(cells.parts, mains.parts)])
        upper = []
        for a, b in zip(cells.parts, mains.parts):
            value = jnp.where(slot == 3, turn(a, 1), turn(a, -1))
            value = jnp.where(slot == 1, b, value)
            other = pick_rows(shift_slots(value, -self.lag), self.above)
            upper.append(jnp.where(self.seam, other, value))
        faces = roe_flux(lower, Cells(upper), 1)
        lower_use = [jnp.where(self.seam, pick_rows(shift_slots(face, self.lag), self.below), face) for face in faces]
        for part in range(5):
            self.edge_faces[part] = jnp.where(slot == 1, lower_use[part], faces[part])
        return faces, lower_use

    def change(self, cells, layer):
        faces = roe_flux(cells, cells.map(lambda part: turn(part, -1)), 1)
        index = (layer + 1) * 16 + self.to_main
        changes = []
        for part in range(5):
            edge = pick_lanes(self.edge_faces[part], index)
            upper = jnp.where(self.is_last, edge, faces[part])
            lower = jnp.where(self.is_first, edge, turn(faces[part], 1))
            changes.append(upper - lower)
        return changes


def inner_kernel(match, main, halo, first, edge_first, part_main, part_edge, above, below, edge_faces):
    row = row_ids()
    below_of = jnp.zeros(tile, jnp.int32)
    above_of = jnp.zeros(tile, jnp.int32)
    for k in range(rows):
        value = match[k]
        below_of = jnp.where(row == k, value, below_of)
        above_of = jnp.where(row == value, k, above_of)
    below[...], above[...] = below_of, above_of
    pitch = Pitch(above_of, below_of, edge_faces)
    slot = pitch.slot

    def start(layer, carry):
        put(first, layer, cells_of_draws([main[field, layer] for field in range(5)]))
        return carry

    unrolled(layers, start)
    cells = cells_of_draws([halo[field] for field in range(5)])
    for number, part in enumerate(cells.parts):
        edge_first[number] = part
    faces, lower_use = pitch.edges(cells, pitch.mains(first, [(layer, layer) for layer in range(layers)]))
    span = span_change(cells)
    state = cells.conserved()
    for part in range(5):
        along = jnp.where(slot == 1, faces[part] - turn(faces[part], 1), faces[part] - turn(lower_use[part], -1))
        part_edge[part] = over_slots(state[part]) + 0.5 * (along + span[part])

    def step(layer, below_faces):
        cells = get(first, layer)
        above_faces = roe_flux(cells, get(first, jnp.minimum(layer + 1, layers - 1)), 0)
        span = span_change(cells)
        along = pitch.change(cells, layer)
        state = cells.conserved()
        outs = []
        for part in range(5):
            upper = jnp.where(layer == layers - 1, 0.0, above_faces[part])
            part_main[layer, part] = over_instances(state[part]) + 0.5 * (
                (upper - below_faces[part]) + span[part] + along[part]
            )
            outs.append(upper)
        return tuple(outs)

    lax.fori_loop(0, layers, step, (jnp.zeros(tile, jnp.float32),) * 5)


def outer_kernel(first, edge_first, part_main, part_edge, above, below, halo, near_b, near_a, *refs):
    messages, (ends, second, change, edge_faces) = in_order(refs[:4]), refs[4:]
    where_on = lax.axis_index("space")
    even = jnp.bitwise_and(where_on, 1) == 0
    at_low = where_on == 0
    at_high = where_on == lax.axis_size("space") - 1
    pitch = Pitch(above[...], below[...], edge_faces)
    band = pitch.band

    for number in range(8):
        ends[2, number] = first[0, number]
        ends[3, number] = first[layers - 1, number]

    def bring(count, carry):
        high = count // 2
        place = jnp.bitwise_and(count, 1)
        from_a = jnp.logical_xor(even, high == 0)
        closed = jnp.logical_or(jnp.logical_and(at_low, high == 0), jnp.logical_and(at_high, high == 1))
        draws = [jnp.where(from_a, near_a[2 * field + place], near_b[2 * field + place]) for field in range(5)]
        cells = cells_of_draws(draws)
        own = get(first, high * (layers - 1))
        put(ends, count + 2 * high, Cells([jnp.where(closed, a, b) for a, b in zip(own.parts, cells.parts)]))
        return carry

    unrolled(4, bring)
    low_tile = jnp.where(even, near_b[10], near_a[10])
    high_tile = jnp.where(even, near_a[10], near_b[10])
    outside = []
    for field in range(5):
        inside = halo[field]
        low = jnp.where(at_low, turn(inside, -16), turn(low_tile, -16 * field))
        high = jnp.where(at_high, turn(inside, 16), turn(high_tile, 16 * (layers + 1 - field)))
        outside.append(jnp.where(band == 0, low, high))
    within = jnp.logical_and(band > 0, band < layers + 1)
    edge_cells = cells_of_draws(outside)
    edge_cells = Cells([jnp.where(within, edge_first[number], edge_cells.parts[number]) for number in range(8)])
    pitch.edges(edge_cells, pitch.mains(ends, [(-1, 1), (layers, 4)]))
    axial = roe_flux(edge_cells, edge_cells.map(lambda part: turn(part, -16)), 0)
    state = edge_cells.conserved()
    for part in range(5):
        value = part_edge[part] + 0.5 * (axial[part] - turn(axial[part], 16))
        state[part] = state[part] - pseudo_step * value
    edge_second = cells_of_conserved(state)

    def end_step(high, carry):
        base = 3 * high
        cells = get(ends, base + 1)
        lower = roe_flux(get(ends, base), cells, 0)
        upper = roe_flux(cells, get(ends, base + 2), 0)
        span = span_change(cells)
        along = pitch.change(cells, high * (layers + 1) - 1)
        state = cells.conserved()
        for part in range(5):
            value = over_instances(state[part]) + 0.5 * ((upper[part] - lower[part]) + span[part] + along[part])
            state[part] = state[part] - pseudo_step * value
            change[high, part] = jnp.where(high == 0, -upper[part], lower[part])
        put(second, high * (layers + 1), cells_of_conserved(state))
        return carry

    unrolled(2, end_step)

    def section(layer, carry):
        state = get(first, layer).conserved()
        for part in range(5):
            more = jnp.where(layer == 0, change[0, part], jnp.where(layer == layers - 1, change[1, part], 0.0))
            state[part] = state[part] - pseudo_step * (part_main[layer, part] + 0.5 * more)
        put(second, layer + 1, cells_of_conserved(state))
        return carry

    unrolled(layers, section)
    for number in range(8):
        second[0, number] = jnp.where(at_low, second[1, number], second[0, number])
        second[layers + 1, number] = jnp.where(at_high, second[layers, number], second[layers + 1, number])

    pitch.edges(edge_second, pitch.mains(second, [(layer, layer + 1) for layer in range(layers)]))

    def second_step(layer, below_faces):
        cells = get(second, layer + 1)
        above_faces = roe_flux(cells, get(second, layer + 2), 0)
        span = span_change(cells)
        along = pitch.change(cells, layer)
        state = cells.conserved()
        for part in range(5):
            value = (above_faces[part] - below_faces[part]) + span[part] + along[part]
            ends[layer, part] = over_instances(state[part]) + 0.5 * value
        return tuple(above_faces)

    lax.fori_loop(0, layers, second_step, tuple(roe_flux(get(second, 0), get(second, 1), 0)))
    me = lax.axis_index("inst")

    def send(field, carry):
        tiles = [ends[layer, field] for layer in range(layers)]
        for distance in range(inst_count):
            messages[distance][field] = pack_tile(tiles, jnp.bitwise_xor(me, distance))
        return carry

    unrolled(5, send)


def return_kernel(*refs):
    received, out = in_order(refs[:4]), refs[4]
    me = lax.axis_index("inst")

    def one_field(field, carry):
        for layer, values in enumerate(spread_tiles(received, field, me)):
            out[0, field, layer] = values
        return carry

    unrolled(5, one_field)


def call(kernel, outs, operands, scratch=(), scalars=0):
    shapes = [jax.ShapeDtypeStruct(shape, kind) for shape, kind in outs]
    return pl.pallas_call(
        kernel,
        out_shape=shapes,
        in_specs=[smem] * scalars + [vmem] * (len(operands) - scalars),
        out_specs=[vmem] * len(shapes),
        scratch_shapes=[pltpu.VMEM(shape, jnp.float32) for shape in scratch],
        compiler_params=pltpu.CompilerParams(vmem_limit_bytes=16 * 2**20),
    )(*operands)


def floats(*shape):
    return shape + tile, jnp.float32


def swap_instances(messages):
    got = []
    for distance, message in zip(order, messages):
        route = [(i, i ^ distance) for i in range(inst_count)]
        got.append(lax.ppermute(message, "inst", route) if distance else message)
    return got


def on_device_fast(flow_state, period_match):
    count = lax.axis_size("space")
    messages = call(pack_kernel, [floats(6)] * inst_count, [flow_state])
    near_b, near_a, main, halo = call(
        unpack_kernel, [floats(11), floats(11), floats(5, layers), floats(5)], swap_instances(messages)
    )
    route_a = [(i, i ^ 1) for i in range(count)]
    route_b = [(i, ((i - 1) ^ 1) + 1) if 0 < i < count - 1 else (i, count - 1 - i) for i in range(count)]
    near_b = lax.ppermute(near_b, "space", route_b)
    near_a = lax.ppermute(near_a, "space", route_a)
    integers = (tile, jnp.int32)
    inner = call(
        inner_kernel,
        [floats(layers, 8), floats(8), floats(layers, 5), floats(5), integers, integers],
        [period_match, main, halo],
        [(5,) + tile],
        scalars=1,
    )
    results = call(
        outer_kernel,
        [floats(5)] * inst_count,
        [*inner, halo, near_b, near_a],
        [(6, 8) + tile, (layers + 2, 8) + tile, (2, 5) + tile, (5,) + tile],
    )
    return call(return_kernel, [(flow_state.shape, jnp.float32)], swap_instances(results))[0]


def solution(mesh):
    in_specs = (P(("groups", "inst"), None, "space", None, None), P())
    out_specs = P(("groups", "inst"), None, "space", None, None)

    def whole(flow_state, period_match):
        block = (flow_state.shape[2] // mesh.shape["space"],) + flow_state.shape[3:]
        fits = mesh.shape["inst"] == inst_count and mesh.shape["space"] % 2 == 0
        body = on_device_fast if fits and block == (layers, rows, lanes) else on_device
        return jax.shard_map(body, mesh=mesh, in_specs=in_specs, out_specs=out_specs, check_vma=False)(
            flow_state, period_match
        )

    return whole
```

```python
import math

import jax
import jax.numpy as jnp
from jax import lax
from jax.experimental import pallas as pl
from jax.experimental.pallas import tpu as pltpu
from jax.sharding import PartitionSpec as P

gamma_gas = 1.4
prandtl = 0.72
viscosity = 0.1
pseudo_step = 0.03
entropy_share = 0.1


def from_behind(block, axis, distance):
    devices = range(lax.axis_size(axis))
    route = [((i - distance) % len(devices), i) for i in devices]
    return lax.ppermute(block, axis, route)


def extended(cells, sides, width):
    for axis, dim in sides:
        count = lax.axis_size(axis)
        ends = count - 1
        head = lax.slice_in_dim(cells, 0, width, axis=dim)
        tail = lax.slice_in_dim(cells, cells.shape[dim] - width, cells.shape[dim], axis=dim)
        cells = jnp.concatenate(
            [
                lax.ppermute(tail, axis, [(i, (i + 1) % count) for i in range(ends)]),
                cells,
                lax.ppermute(head, axis, [((i + 1) % count, i) for i in range(ends)]),
            ],
            axis=dim,
        )
    return cells


def from_draw(draws):
    shape = (5,) + (1,) * (draws.ndim - 1)
    offsets = jnp.array([1.0, 0.8, 0.0, 0.0, 0.8], jnp.float32).reshape(shape)
    spreads = jnp.array([0.3, 0.3, 0.3, 0.3, 0.2], jnp.float32).reshape(shape)
    return offsets + spreads * draws


def conserved(primitives):
    dens = primitives[0]
    velocity = primitives[1:4]
    kinetic = 0.5 * dens * jnp.sum(velocity * velocity, axis=0)
    energy = primitives[4] / (gamma_gas - 1.0) + kinetic
    return jnp.concatenate([dens[None], dens[None] * velocity, energy[None]], axis=0)


def primitive(conserved_vars):
    dens = conserved_vars[0]
    velocity = conserved_vars[1:4] / dens
    pressure = (gamma_gas - 1.0) * (
        conserved_vars[4] - 0.5 * dens * jnp.sum(velocity * velocity, axis=0)
    )
    return jnp.concatenate([dens[None], velocity, pressure[None]], axis=0)


def entropy_fix(eigen_val, sound_speed):
    spread = entropy_share * sound_speed
    magnitude = jnp.abs(eigen_val)
    return jnp.where(
        magnitude >= spread, magnitude, (eigen_val * eigen_val + spread * spread) / (2.0 * spread)
    )


def euler_flux(dens, velocity, pressure, enthalpy, normal):
    normal_vel = velocity[normal]
    values = [dens * normal_vel]
    for component in range(3):
        moment = dens * velocity[component] * normal_vel
        if component == normal:
            moment = moment + pressure
        values.append(moment)
    values.append(dens * enthalpy * normal_vel)
    return values


def face_flux(left_cells, right_cells, normal):
    dens_left, vel_left, pres_left = (left_cells[0], left_cells[1:4], left_cells[4])
    dens_right, vel_right, pres_right = (right_cells[0], right_cells[1:4], right_cells[4])
    ratio = gamma_gas / (gamma_gas - 1.0)
    sq_left = jnp.sum(vel_left * vel_left, axis=0)
    sq_right = jnp.sum(vel_right * vel_right, axis=0)
    enth_left = ratio * pres_left / dens_left + 0.5 * sq_left
    enth_right = ratio * pres_right / dens_right + 0.5 * sq_right
    flux_left = euler_flux(dens_left, vel_left, pres_left, enth_left, normal)
    flux_right = euler_flux(dens_right, vel_right, pres_right, enth_right, normal)
    root_left = jnp.sqrt(dens_left)
    root_right = jnp.sqrt(dens_right)
    root_sum = root_left + root_right
    vel_roe = (root_left * vel_left + root_right * vel_right) / root_sum
    enth_roe = (root_left * enth_left + root_right * enth_right) / root_sum
    speed_sq = jnp.sum(vel_roe * vel_roe, axis=0)
    sound_sq = (gamma_gas - 1.0) * (enth_roe - 0.5 * speed_sq)
    sound_speed = jnp.sqrt(sound_sq)
    normal_vel = vel_roe[normal]
    dens_roe = root_left * root_right
    jump_dens = dens_right - dens_left
    jump_pres = pres_right - pres_left
    jump_vel = vel_right - vel_left
    jump_normal = jump_vel[normal]
    wave_slow = (jump_pres - dens_roe * sound_speed * jump_normal) / (2.0 * sound_sq)
    wave_fast = (jump_pres + dens_roe * sound_speed * jump_normal) / (2.0 * sound_sq)
    wave_mid = jump_dens - jump_pres / sound_sq
    eigen_mid = entropy_fix(normal_vel, sound_speed)
    flux_slow = entropy_fix(normal_vel - sound_speed, sound_speed) * wave_slow
    flux_fast = entropy_fix(normal_vel + sound_speed, sound_speed) * wave_fast
    dissipation = [flux_slow + eigen_mid * wave_mid + flux_fast]
    for component in range(3):
        unit_dir = 1.0 if component == normal else 0.0
        term = flux_slow * (vel_roe[component] - unit_dir * sound_speed)
        term = term + eigen_mid * (
            wave_mid * vel_roe[component]
            + dens_roe * (jump_vel[component] - unit_dir * jump_normal)
        )
        term = term + flux_fast * (vel_roe[component] + unit_dir * sound_speed)
        dissipation.append(term)
    shear_work = jnp.sum(vel_roe * jump_vel, axis=0) - normal_vel * jump_normal
    energy_term = flux_slow * (enth_roe - normal_vel * sound_speed)
    energy_term = energy_term + eigen_mid * (wave_mid * 0.5 * speed_sq + dens_roe * shear_work)
    energy_term = energy_term + flux_fast * (enth_roe + normal_vel * sound_speed)
    dissipation.append(energy_term)
    jump_temp = pres_right / dens_right - pres_left / dens_left
    jump_kin = 0.5 * (sq_right - sq_left)
    viscous_terms = [
        jnp.zeros_like(jump_dens),
        jump_vel[0],
        jump_vel[1],
        jump_vel[2],
        jump_kin + gamma_gas / ((gamma_gas - 1.0) * prandtl) * jump_temp,
    ]
    values = []
    for component in range(5):
        values.append(
            0.5 * (flux_left[component] + flux_right[component])
            - 0.5 * dissipation[component]
            - viscosity * viscous_terms[component]
        )
    return jnp.stack(values, axis=0)


def flux_change(padded, along, normal):
    length = padded.shape[along]
    face_values = face_flux(
        lax.slice_in_dim(padded, 0, length - 1, axis=along),
        lax.slice_in_dim(padded, 1, length, axis=along),
        normal,
    )
    return lax.slice_in_dim(face_values, 1, length - 1, axis=along) - lax.slice_in_dim(
        face_values, 0, length - 2, axis=along
    )


def spectral_entry(offset, number):
    wrapped = jnp.mod(offset, number)
    parity = 1.0 - 2.0 * jnp.mod(wrapped, 2).astype(jnp.float32)
    angles = math.pi * wrapped.astype(jnp.float32) / number
    sine_val = jnp.where(wrapped == 0, 1.0, jnp.sin(angles))
    derivative = jnp.where(
        wrapped == 0, 0.0, math.pi / number * parity * jnp.cos(angles) / sine_val
    )
    return derivative + 0.5 * parity


def on_device(flow_state, period_match):
    instances = lax.axis_size("inst")
    phase_lag = instances // 4
    instance = lax.axis_index("inst")
    space_parts = lax.axis_size("space")
    position = lax.axis_index("space")
    labels = jnp.arange(period_match.shape[0], dtype=jnp.int32)
    matches = (period_match[:, None] == labels[None, :]).astype(jnp.int32)
    inverse = jnp.sum(labels[:, None] * matches, axis=0)
    mirror = jnp.array([1.0, 1.0, 1.0, -1.0, 1.0], jnp.float32).reshape(5, 1, 1, 1)

    def lagged(plane, steps):
        return from_behind(plane, "inst", steps)

    def timewise(conserved_vars):
        pieces = lax.all_gather(conserved_vars[None], "inst", axis=0, tiled=True)
        number = pieces.shape[0]
        others = jnp.arange(number, dtype=jnp.int32)
        weights = spectral_entry(instance - others, instances)
        return jnp.tensordot(weights, pieces, axes=1, precision=lax.Precision.HIGHEST)

    def evaluate(conserved_vars):
        prims = primitive(conserved_vars)
        padded = extended(prims, (("space", 1),), 1)
        lower_edge = jnp.where(position == 0, prims[:, :1], padded[:, :1])
        upper_edge = jnp.where(position == space_parts - 1, prims[:, -1:], padded[:, -1:])
        along_axial = jnp.concatenate([lower_edge, prims, upper_edge], axis=1)
        along_span = jnp.concatenate(
            [prims[:, :, :1] * mirror, prims, prims[:, :, -1:] * mirror], axis=2
        )
        ghost_below = jnp.take(lagged(prims[..., -1], phase_lag), period_match, axis=2)
        ghost_above = jnp.take(lagged(prims[..., 0], -phase_lag), inverse, axis=2)
        along_pitch = jnp.concatenate(
            [ghost_below[..., None], prims, ghost_above[..., None]], axis=3
        )
        spatial = (
            flux_change(along_axial, 1, 0)
            + flux_change(along_span, 2, 2)
            + flux_change(along_pitch, 3, 1)
        )
        return timewise(conserved_vars) + spatial

    initial = conserved(from_draw(flow_state[0]))
    section_state = initial - pseudo_step * evaluate(initial)
    return evaluate(section_state)[None]


inst_count = 4
layers = 4
chunk = 32
rows = 16
lanes = 128
tile = (rows, lanes)
vmem = pl.BlockSpec(memory_space=pltpu.VMEM)
smem = pl.BlockSpec(memory_space=pltpu.SMEM)
starts = (1.0, 0.8, 0.0, 0.0, 0.8)
spreads_of = (0.3, 0.3, 0.3, 0.3, 0.2)
ratio = gamma_gas / (gamma_gas - 1.0)


def weight_of(distance):
    parity = 1.0 - 2.0 * (distance % 2)
    if distance == 0:
        return 0.5
    if 2 * distance == inst_count:
        return 0.5 * parity
    angle = math.pi * distance / inst_count
    return math.pi / inst_count * parity * math.cos(angle) / math.sin(angle) + 0.5 * parity


order = (2, 3, 1, 0)


def in_order(items):
    return [items[order.index(distance)] for distance in range(inst_count)]


def unrolled(count, body, carry=None):
    for number in range(count):
        carry = body(number, carry)
    return carry


def lane_ids():
    return lax.broadcasted_iota(jnp.int32, tile, 1)


def row_ids():
    return lax.broadcasted_iota(jnp.int32, tile, 0)


def pick_lanes(values, index):
    return jnp.take_along_axis(values, index, axis=1, mode="promise_in_bounds")


def pick_rows(values, index):
    half = rows // 2
    low, high = values[:half], values[half:]
    parts = []
    for part in (index[:half], index[half:]):
        inner = jnp.bitwise_and(part, half - 1)
        from_low = jnp.take_along_axis(low, inner, axis=0, mode="promise_in_bounds")
        from_high = jnp.take_along_axis(high, inner, axis=0, mode="promise_in_bounds")
        parts.append(jnp.where(part < half, from_low, from_high))
    return jnp.concatenate(parts, axis=0)


def turn(values, amount):
    return pltpu.roll(values, amount % lanes if isinstance(amount, int) else amount, 1)


def mod_lanes(amount):
    return jnp.bitwise_and(amount, lanes - 1)


def pack_tile(layer_tiles, part):
    group = lane_ids() // chunk
    out = None
    for layer in range(layers):
        moved = turn(layer_tiles[layer], mod_lanes(chunk * (layer - part) + lanes))
        out = moved if out is None else jnp.where(group == layer, moved, out)
    return out


def pack_kernel(flow, *refs):
    messages = in_order(refs)
    me = lax.axis_index("inst")
    lane = lane_ids()
    slot = jnp.bitwise_and(lane, 3)
    step = jnp.where(slot < 2, slot - 2, slot + chunk - 2)
    parts = [jnp.bitwise_xor(me, distance) for distance in range(inst_count)]
    index = [mod_lanes(step + (chunk * part + lanes)) for part in parts]

    def one_field(field, edges):
        tiles = [flow[0, field, layer] for layer in range(layers)]
        edges = list(edges)
        for distance, part in enumerate(parts):
            messages[distance][field] = pack_tile(tiles, part)
            for layer in range(layers):
                here = lane // 4 == field * 4 + layer
                edges[distance] = jnp.where(here, pick_lanes(tiles[layer], index[distance]), edges[distance])
        return tuple(edges)

    edges = unrolled(5, one_field, (jnp.zeros(tile, jnp.float32),) * inst_count)
    for distance in range(inst_count):
        messages[distance][5] = edges[distance]


def spread_tiles(received, field, me):
    group = lane_ids() // chunk
    outs = [None] * layers
    for distance in range(inst_count):
        part = jnp.bitwise_xor(me, distance)
        values = received[distance][field]
        for layer in range(layers):
            moved = turn(values, mod_lanes(chunk * (part - layer) + lanes))
            outs[layer] = moved if outs[layer] is None else jnp.where(group == part, moved, outs[layer])
    return outs


def unpack_kernel(*refs):
    received, (near_b, near_a, main, halo) = in_order(refs[:4]), refs[5:]
    me = lax.axis_index("inst")
    even = jnp.bitwise_and(lax.axis_index("space"), 1) == 0
    lane = lane_ids()
    owner = jnp.bitwise_and(lane // 4, 3)
    level = lane // 16 - 1
    inner = jnp.clip(level, 0, layers - 1) * 4 + jnp.bitwise_and(lane, 3)

    def one_field(field, ends):
        tiles = spread_tiles(received, field, me)
        for layer in range(layers):
            main[field, layer] = tiles[layer]
        for place in range(2):
            near_a[2 * field + place] = jnp.where(even, tiles[2 + place], tiles[place])
            near_b[2 * field + place] = jnp.where(even, tiles[place], tiles[2 + place])
        edges = None
        for distance in range(inst_count):
            part = jnp.bitwise_xor(me, distance)
            got = pick_lanes(received[distance][5], inner + 16 * field)
            edges = got if edges is None else jnp.where(owner == part, got, edges)
        halo[field] = edges
        here = lane // 16 == field
        up = turn(edges, mod_lanes(16 * field - 16 * layers + lanes))
        down = turn(edges, mod_lanes(16 * field - 16 + lanes))
        return jnp.where(here, up, ends[0]), jnp.where(here, down, ends[1])

    up_edge, down_edge = unrolled(5, one_field, (jnp.zeros(tile, jnp.float32),) * 2)
    near_a[10] = jnp.where(even, up_edge, down_edge)
    near_b[10] = jnp.where(even, down_edge, up_edge)


class Cells:
    def __init__(self, parts):
        self.parts = list(parts)
        self.dens, self.vel, self.pres = parts[0], list(parts[1:4]), parts[4]
        self.root, self.enth, self.heat = parts[5], parts[6], parts[7]

    def map(self, change):
        return Cells([change(part) for part in self.parts])

    def conserved(self):
        dens, enth = self.dens, self.enth
        return [dens] + [dens * part for part in self.vel] + [dens * enth - self.pres]


def cells_of(dens, vel, pres):
    inverse_root = lax.rsqrt(dens)
    root = dens * inverse_root
    temp = pres * (inverse_root * inverse_root)
    kinetic = 0.5 * (vel[0] * vel[0] + vel[1] * vel[1] + vel[2] * vel[2])
    enth = ratio * temp + kinetic
    heat = 2.0 * viscosity * (kinetic + ratio / prandtl * temp)
    return Cells([dens] + list(vel) + [pres, root, enth, heat])


def cells_of_draws(draws):
    start = [base + spread * draw if base else spread * draw for base, spread, draw in zip(starts, spreads_of, draws)]
    return cells_of(start[0], start[1:4], start[4])


def cells_of_conserved(state):
    dens = state[0]
    inverse = 1.0 / dens
    vel = [part * inverse for part in state[1:4]]
    kinetic = vel[0] * vel[0] + vel[1] * vel[1] + vel[2] * vel[2]
    pres = (gamma_gas - 1.0) * (state[4] - 0.5 * dens * kinetic)
    return cells_of(dens, vel, pres)


def roe_flux(low, high, normal):
    jump_dens = high.dens - low.dens
    jump_pres = high.pres - low.pres
    jump = [b - a for a, b in zip(low.vel, high.vel)]
    share = high.root / (low.root + high.root)
    vel = [a + share * d for a, d in zip(low.vel, jump)]
    enth = low.enth + share * (high.enth - low.enth)
    half_sq = 0.5 * (vel[0] * vel[0] + vel[1] * vel[1] + vel[2] * vel[2])
    sound_sq = (gamma_gas - 1.0) * (enth - half_sq)
    inverse = lax.rsqrt(sound_sq)
    sound = sound_sq * inverse
    dens_roe = low.root * high.root
    along = vel[normal]
    jump_along = jump[normal]
    press_part = jump_pres * (inverse * inverse)
    speed_part = dens_roe * inverse * jump_along
    bound = entropy_share * sound
    curve = (0.5 / entropy_share) * inverse
    floor = 0.5 * bound

    def fixed(speed):
        size = jnp.abs(speed)
        return jnp.where(size >= bound, size, speed * speed * curve + floor)

    slow = 0.5 * fixed(along - sound) * (press_part - speed_part)
    fast = 0.5 * fixed(along + sound) * (press_part + speed_part)
    middle = fixed(along)
    entropy = middle * (jump_dens - press_part)
    both = slow + fast
    total = both + entropy
    push = sound * (fast - slow)
    shear = middle * dens_roe
    mass_low = low.dens * low.vel[normal]
    mass_high = high.dens * high.vel[normal]
    out = [mass_low + mass_high - total]
    work = None
    for part in range(3):
        value = mass_low * low.vel[part] + mass_high * high.vel[part] - vel[part] * total
        if part == normal:
            value = value + (low.pres + high.pres) - push - (2.0 * viscosity) * jump_along
        else:
            value = value - (shear + 2.0 * viscosity) * jump[part]
            term = vel[part] * jump[part]
            work = term if work is None else work + term
        out.append(value)
    lost = enth * both + along * push + entropy * half_sq + shear * work
    out.append(mass_low * low.enth + mass_high * high.enth - lost - (high.heat - low.heat))
    return out


def span_change(cells):
    row = row_ids()
    faces = roe_flux(cells, cells.map(lambda part: pltpu.roll(part, rows - 1, 0)), 2)
    w = cells.vel[2]
    sound_sq = (gamma_gas - 1.0) * (cells.enth - 0.5 * (cells.vel[0] * cells.vel[0] + cells.vel[1] * cells.vel[1]))
    sound = sound_sq * lax.rsqrt(sound_sq)
    still = 2.0 * (cells.dens * w * w + cells.pres)
    moving = 2.0 * w * (sound * cells.dens + 2.0 * viscosity)
    changes = []
    for part in range(5):
        top = still + moving if part == 3 else 0.0
        bottom = still - moving if part == 3 else 0.0
        upper = jnp.where(row == rows - 1, top, faces[part])
        lower = jnp.where(row == 0, bottom, pltpu.roll(faces[part], 1, 0))
        changes.append(upper - lower)
    return changes


def over_instances(values):
    out = weight_of(0) * values
    for distance in range(1, inst_count):
        out = out + weight_of(distance) * turn(values, chunk * distance)
    return out


def shift_slots(values, distance):
    owner = jnp.bitwise_and(lane_ids() // 4, 3)
    distance = distance % inst_count
    return jnp.where(owner >= distance, turn(values, 4 * distance), turn(values, 4 * distance - 16))


def over_slots(values):
    out = weight_of(0) * values
    for distance in range(1, inst_count):
        out = out + weight_of(distance) * shift_slots(values, distance)
    return out


def put(ref, place, cells):
    for number, part in enumerate(cells.parts):
        ref[place, number] = part


def get(ref, place):
    return Cells([ref[place, number] for number in range(8)])


class Pitch:
    def __init__(self, above, below, edge_faces):
        self.above, self.below, self.edge_faces = above, below, edge_faces
        self.lag = inst_count // 4
        me = lax.axis_index("inst")
        lane = lane_ids()
        self.slot = jnp.bitwise_and(lane, 3)
        self.band = lane // 16
        column = jnp.bitwise_and(lane, chunk - 1)
        self.is_first, self.is_last = column == 0, column == chunk - 1
        self.seam = self.slot == jnp.where(me == 0, 1, jnp.where(me == inst_count - 1, 3, -1))
        self.to_main = (lane // chunk) * 4 + jnp.where(self.is_first, 1, 3)
        self.from_main = jnp.bitwise_and(lane // 4, 3) * chunk + jnp.where(self.slot == 1, 0, chunk - 1)

    def mains(self, ref, places):
        out = [None] * 8
        for layer, place in places:
            for number in range(8):
                got = pick_lanes(ref[place, number], self.from_main)
                out[number] = got if out[number] is None else jnp.where(self.band == layer + 1, got, out[number])
        return Cells(out)

    def edges(self, cells, mains):
        slot = self.slot
        lower = Cells([jnp.where(slot == 3, b, a) for a, b in zip(cells.parts, mains.parts)])
        upper = []
        for a, b in zip(cells.parts, mains.parts):
            value = jnp.where(slot == 3, turn(a, 1), turn(a, -1))
            value = jnp.where(slot == 1, b, value)
            other = pick_rows(shift_slots(value, -self.lag), self.above)
            upper.append(jnp.where(self.seam, other, value))
        faces = roe_flux(lower, Cells(upper), 1)
        lower_use = [jnp.where(self.seam, pick_rows(shift_slots(face, self.lag), self.below), face) for face in faces]
        for part in range(5):
            self.edge_faces[part] = jnp.where(slot == 1, lower_use[part], faces[part])
        return faces, lower_use

    def change(self, cells, layer):
        faces = roe_flux(cells, cells.map(lambda part: turn(part, -1)), 1)
        index = (layer + 1) * 16 + self.to_main
        changes = []
        for part in range(5):
            edge = pick_lanes(self.edge_faces[part], index)
            upper = jnp.where(self.is_last, edge, faces[part])
            lower = jnp.where(self.is_first, edge, turn(faces[part], 1))
            changes.append(upper - lower)
        return changes


def index_kernel(match, behind, above, below):
    row = row_ids()
    below_of = jnp.zeros(tile, jnp.int32)
    above_of = jnp.zeros(tile, jnp.int32)
    for k in range(rows):
        value = match[k]
        below_of = jnp.where(row == k, value, below_of)
        above_of = jnp.where(row == value, k, above_of)
    below[...], above[...] = below_of, above_of


def inner_kernel(above, below, main, halo, first, edge_first, part_first, part_edge, second, part_second, edge_faces):
    pitch = Pitch(above[...], below[...], edge_faces)
    slot = pitch.slot
    middle = range(1, layers - 1)
    for layer in range(layers):
        put(first, layer, cells_of_draws([main[field, layer] for field in range(5)]))
    cells = cells_of_draws([halo[field] for field in range(5)])
    for number, part in enumerate(cells.parts):
        edge_first[number] = part
    faces, lower_use = pitch.edges(cells, pitch.mains(first, [(layer, layer) for layer in range(layers)]))
    span = span_change(cells)
    axial = roe_flux(cells, cells.map(lambda part: turn(part, -16)), 0)
    state = cells.conserved()
    for part in range(5):
        along = jnp.where(slot == 1, faces[part] - turn(faces[part], 1), faces[part] - turn(lower_use[part], -1))
        value = over_slots(state[part]) + 0.5 * (along + span[part])
        part_edge[part] = value
        value = value + 0.5 * (axial[part] - turn(axial[part], 16))
        state[part] = state[part] - pseudo_step * value
    edge_second = cells_of_conserved(state)

    def step(layer, below_faces):
        cells = get(first, layer)
        above_faces = roe_flux(cells, get(first, jnp.minimum(layer + 1, layers - 1)), 0)
        span = span_change(cells)
        along = pitch.change(cells, layer)
        state = cells.conserved()
        outs = []
        for part in range(5):
            upper = jnp.where(layer == layers - 1, 0.0, above_faces[part])
            part_first[layer, part] = over_instances(state[part]) + 0.5 * (
                (upper - below_faces[part]) + span[part] + along[part]
            )
            outs.append(upper)
        return tuple(outs)

    lax.fori_loop(0, layers, step, (jnp.zeros(tile, jnp.float32),) * 5)

    for place, layer in enumerate(middle):
        state = get(first, layer).conserved()
        state = [value - pseudo_step * part_first[layer, part] for part, value in enumerate(state)]
        put(second, place, cells_of_conserved(state))
    pitch.edges(edge_second, pitch.mains(second, [(layer, place) for place, layer in enumerate(middle)]))
    between = roe_flux(get(second, 0), get(second, 1), 0)
    for part in range(5):
        part_second[0, part] = between[part]
        part_second[1, part] = -between[part]

    def second_step(place, carry):
        cells = get(second, place)
        span = span_change(cells)
        along = pitch.change(cells, place + 1)
        state = cells.conserved()
        for part in range(5):
            value = part_second[place, part] + span[part] + along[part]
            part_second[place, part] = over_instances(state[part]) + 0.5 * value
        return carry

    lax.fori_loop(0, layers - 2, second_step, 0)


def outer_kernel(
    first, edge_first, part_first, part_edge, second_middle, part_second, above, below, halo, near_b, near_a, *refs
):
    messages, (ends, second, change, edge_faces) = in_order(refs[:4]), refs[4:]
    where_on = lax.axis_index("space")
    even = jnp.bitwise_and(where_on, 1) == 0
    at_low = where_on == 0
    at_high = where_on == lax.axis_size("space") - 1
    pitch = Pitch(above[...], below[...], edge_faces)
    band = pitch.band

    for number in range(8):
        ends[2, number] = first[0, number]
        ends[3, number] = first[layers - 1, number]
        second[2, number] = second_middle[0, number]
        second[layers - 1, number] = second_middle[layers - 3, number]

    for high in range(2):
        own = get(first, high * (layers - 1))
        closed, from_a = (at_high, even) if high else (at_low, jnp.logical_not(even))
        for place in range(2):
            draws = [jnp.where(from_a, near_a[2 * field + place], near_b[2 * field + place]) for field in range(5)]
            cells = cells_of_draws(draws)
            pairs = zip(own.parts, cells.parts)
            put(ends, place + 4 * high, Cells([jnp.where(closed, a, b) for a, b in pairs]))

    low_tile = jnp.where(even, near_b[10], near_a[10])
    high_tile = jnp.where(even, near_a[10], near_b[10])
    outside = []
    for field in range(5):
        inside = halo[field]
        low = jnp.where(at_low, turn(inside, -16), turn(low_tile, -16 * field))
        high = jnp.where(at_high, turn(inside, 16), turn(high_tile, 16 * (layers + 1 - field)))
        outside.append(jnp.where(band == 0, low, high))
    within = jnp.logical_and(band > 0, band < layers + 1)
    edge_cells = cells_of_draws(outside)
    edge_cells = Cells([jnp.where(within, edge_first[number], edge_cells.parts[number]) for number in range(8)])
    pitch.edges(edge_cells, pitch.mains(ends, [(-1, 1), (layers, 4)]))
    axial = roe_flux(edge_cells, edge_cells.map(lambda part: turn(part, -16)), 0)
    state = edge_cells.conserved()
    for part in range(5):
        value = part_edge[part] + 0.5 * (axial[part] - turn(axial[part], 16))
        state[part] = state[part] - pseudo_step * value
    edge_second = cells_of_conserved(state)

    def end_values(ref, high, layer):
        base = 3 * high
        cells = get(ref, base + 1)
        lower = roe_flux(get(ref, base), cells, 0)
        upper = roe_flux(cells, get(ref, base + 2), 0)
        span = span_change(cells)
        along = pitch.change(cells, layer)
        state = cells.conserved()
        values = []
        for part in range(5):
            value = (upper[part] - lower[part]) + span[part] + along[part]
            values.append(over_instances(state[part]) + 0.5 * value)
            change[high, part] = jnp.where(high == 0, -upper[part], lower[part])
        return state, values

    def first_step(high, carry):
        state, values = end_values(ends, high, high * (layers + 1) - 1)
        state = [a - pseudo_step * b for a, b in zip(state, values)]
        put(second, high * (layers + 1), cells_of_conserved(state))
        return carry

    unrolled(2, first_step)

    for high in range(2):
        layer = high * (layers - 1)
        state = get(first, layer).conserved()
        for part in range(5):
            state[part] = state[part] - pseudo_step * (part_first[layer, part] + 0.5 * change[high, part])
        put(second, layer + 1, cells_of_conserved(state))
    for number in range(8):
        second[0, number] = jnp.where(at_low, second[1, number], second[0, number])
        second[layers + 1, number] = jnp.where(at_high, second[layers, number], second[layers + 1, number])

    pitch.edges(edge_second, pitch.mains(second, [(0, 1), (layers - 1, layers)]))

    def second_step(high, carry):
        _, values = end_values(second, high, high * (layers - 1))
        for part in range(5):
            ends[high, part] = values[part]
        return carry

    lax.fori_loop(0, 2, second_step, 0)

    me = lax.axis_index("inst")
    for field in range(5):
        tiles = [ends[0, field], part_second[0, field] + 0.5 * change[0, field]]
        tiles += [part_second[1, field] + 0.5 * change[1, field], ends[1, field]]
        for distance in range(inst_count):
            messages[distance][field] = pack_tile(tiles, jnp.bitwise_xor(me, distance))


def return_kernel(*refs):
    received, out = in_order(refs[:4]), refs[4]
    me = lax.axis_index("inst")

    def one_field(field, carry):
        for layer, values in enumerate(spread_tiles(received, field, me)):
            out[0, field, layer] = values
        return carry

    unrolled(5, one_field)


def call(kernel, outs, operands, scratch=(), scalars=0):
    shapes = [jax.ShapeDtypeStruct(shape, kind) for shape, kind in outs]
    return pl.pallas_call(
        kernel,
        out_shape=shapes,
        in_specs=[smem] * scalars + [vmem] * (len(operands) - scalars),
        out_specs=[vmem] * len(shapes),
        scratch_shapes=[pltpu.VMEM(shape, jnp.float32) for shape in scratch],
        compiler_params=pltpu.CompilerParams(vmem_limit_bytes=16 * 2**20),
    )(*operands)


def floats(*shape):
    return shape + tile, jnp.float32


def swap_instances(messages):
    got = []
    for distance, message in zip(order, messages):
        route = [(i, i ^ distance) for i in range(inst_count)]
        got.append(lax.ppermute(message, "inst", route) if distance else message)
    return got


def on_device_fast(flow_state, period_match):
    count = lax.axis_size("space")
    messages = call(pack_kernel, [floats(6)] * inst_count, [flow_state])
    integers = (tile, jnp.int32)
    above, below = call(index_kernel, [integers, integers], [period_match, messages[-1]], scalars=1)
    near_b, near_a, main, halo = call(
        unpack_kernel, [floats(11), floats(11), floats(5, layers), floats(5)], [*swap_instances(messages), above]
    )
    route_a = [(i, i ^ 1) for i in range(count)]
    route_b = []
    for n in range(inst_count):
        for i in range(count):
            far = (n, ((i - 1) ^ 1) + 1) if 0 < i < count - 1 else (n ^ 1, i)
            route_b.append((n * count + i, far[0] * count + far[1]))
    near_b = lax.ppermute(near_b, ("inst", "space"), route_b)
    near_a = lax.ppermute(near_a, "space", route_a)
    inner = call(
        inner_kernel,
        [floats(layers, 8), floats(8), floats(layers, 5), floats(5), floats(layers - 2, 8), floats(layers - 2, 5)],
        [above, below, main, halo],
        [(5,) + tile],
    )
    results = call(
        outer_kernel,
        [floats(5)] * inst_count,
        [*inner, above, below, halo, near_b, near_a],
        [(6, 8) + tile, (layers + 2, 8) + tile, (2, 5) + tile, (5,) + tile],
    )
    return call(return_kernel, [(flow_state.shape, jnp.float32)], swap_instances(results))[0]


def solution(mesh):
    in_specs = (P(("groups", "inst"), None, "space", None, None), P())
    out_specs = P(("groups", "inst"), None, "space", None, None)

    def whole(flow_state, period_match):
        block = (flow_state.shape[2] // mesh.shape["space"],) + flow_state.shape[3:]
        fits = mesh.shape["inst"] == inst_count and mesh.shape["space"] % 2 == 0
        body = on_device_fast if fits and block == (layers, rows, lanes) else on_device
        return jax.shard_map(body, mesh=mesh, in_specs=in_specs, out_specs=out_specs, check_vma=False)(
            flow_state, period_match
        )

    return whole
```

```python
import math

import jax
import jax.numpy as jnp
from jax import lax
from jax.experimental import pallas as pl
from jax.experimental.pallas import tpu as pltpu
from jax.sharding import PartitionSpec as P

gamma_gas = 1.4
prandtl = 0.72
viscosity = 0.1
pseudo_step = 0.03
entropy_share = 0.1


def from_behind(block, axis, distance):
    devices = range(lax.axis_size(axis))
    route = [((i - distance) % len(devices), i) for i in devices]
    return lax.ppermute(block, axis, route)


def extended(cells, sides, width):
    for axis, dim in sides:
        count = lax.axis_size(axis)
        ends = count - 1
        head = lax.slice_in_dim(cells, 0, width, axis=dim)
        tail = lax.slice_in_dim(cells, cells.shape[dim] - width, cells.shape[dim], axis=dim)
        cells = jnp.concatenate(
            [
                lax.ppermute(tail, axis, [(i, (i + 1) % count) for i in range(ends)]),
                cells,
                lax.ppermute(head, axis, [((i + 1) % count, i) for i in range(ends)]),
            ],
            axis=dim,
        )
    return cells


def from_draw(draws):
    shape = (5,) + (1,) * (draws.ndim - 1)
    offsets = jnp.array([1.0, 0.8, 0.0, 0.0, 0.8], jnp.float32).reshape(shape)
    spreads = jnp.array([0.3, 0.3, 0.3, 0.3, 0.2], jnp.float32).reshape(shape)
    return offsets + spreads * draws


def conserved(primitives):
    dens = primitives[0]
    velocity = primitives[1:4]
    kinetic = 0.5 * dens * jnp.sum(velocity * velocity, axis=0)
    energy = primitives[4] / (gamma_gas - 1.0) + kinetic
    return jnp.concatenate([dens[None], dens[None] * velocity, energy[None]], axis=0)


def primitive(conserved_vars):
    dens = conserved_vars[0]
    velocity = conserved_vars[1:4] / dens
    pressure = (gamma_gas - 1.0) * (
        conserved_vars[4] - 0.5 * dens * jnp.sum(velocity * velocity, axis=0)
    )
    return jnp.concatenate([dens[None], velocity, pressure[None]], axis=0)


def entropy_fix(eigen_val, sound_speed):
    spread = entropy_share * sound_speed
    magnitude = jnp.abs(eigen_val)
    return jnp.where(
        magnitude >= spread, magnitude, (eigen_val * eigen_val + spread * spread) / (2.0 * spread)
    )


def euler_flux(dens, velocity, pressure, enthalpy, normal):
    normal_vel = velocity[normal]
    values = [dens * normal_vel]
    for component in range(3):
        moment = dens * velocity[component] * normal_vel
        if component == normal:
            moment = moment + pressure
        values.append(moment)
    values.append(dens * enthalpy * normal_vel)
    return values


def face_flux(left_cells, right_cells, normal):
    dens_left, vel_left, pres_left = (left_cells[0], left_cells[1:4], left_cells[4])
    dens_right, vel_right, pres_right = (right_cells[0], right_cells[1:4], right_cells[4])
    ratio = gamma_gas / (gamma_gas - 1.0)
    sq_left = jnp.sum(vel_left * vel_left, axis=0)
    sq_right = jnp.sum(vel_right * vel_right, axis=0)
    enth_left = ratio * pres_left / dens_left + 0.5 * sq_left
    enth_right = ratio * pres_right / dens_right + 0.5 * sq_right
    flux_left = euler_flux(dens_left, vel_left, pres_left, enth_left, normal)
    flux_right = euler_flux(dens_right, vel_right, pres_right, enth_right, normal)
    root_left = jnp.sqrt(dens_left)
    root_right = jnp.sqrt(dens_right)
    root_sum = root_left + root_right
    vel_roe = (root_left * vel_left + root_right * vel_right) / root_sum
    enth_roe = (root_left * enth_left + root_right * enth_right) / root_sum
    speed_sq = jnp.sum(vel_roe * vel_roe, axis=0)
    sound_sq = (gamma_gas - 1.0) * (enth_roe - 0.5 * speed_sq)
    sound_speed = jnp.sqrt(sound_sq)
    normal_vel = vel_roe[normal]
    dens_roe = root_left * root_right
    jump_dens = dens_right - dens_left
    jump_pres = pres_right - pres_left
    jump_vel = vel_right - vel_left
    jump_normal = jump_vel[normal]
    wave_slow = (jump_pres - dens_roe * sound_speed * jump_normal) / (2.0 * sound_sq)
    wave_fast = (jump_pres + dens_roe * sound_speed * jump_normal) / (2.0 * sound_sq)
    wave_mid = jump_dens - jump_pres / sound_sq
    eigen_mid = entropy_fix(normal_vel, sound_speed)
    flux_slow = entropy_fix(normal_vel - sound_speed, sound_speed) * wave_slow
    flux_fast = entropy_fix(normal_vel + sound_speed, sound_speed) * wave_fast
    dissipation = [flux_slow + eigen_mid * wave_mid + flux_fast]
    for component in range(3):
        unit_dir = 1.0 if component == normal else 0.0
        term = flux_slow * (vel_roe[component] - unit_dir * sound_speed)
        term = term + eigen_mid * (
            wave_mid * vel_roe[component]
            + dens_roe * (jump_vel[component] - unit_dir * jump_normal)
        )
        term = term + flux_fast * (vel_roe[component] + unit_dir * sound_speed)
        dissipation.append(term)
    shear_work = jnp.sum(vel_roe * jump_vel, axis=0) - normal_vel * jump_normal
    energy_term = flux_slow * (enth_roe - normal_vel * sound_speed)
    energy_term = energy_term + eigen_mid * (wave_mid * 0.5 * speed_sq + dens_roe * shear_work)
    energy_term = energy_term + flux_fast * (enth_roe + normal_vel * sound_speed)
    dissipation.append(energy_term)
    jump_temp = pres_right / dens_right - pres_left / dens_left
    jump_kin = 0.5 * (sq_right - sq_left)
    viscous_terms = [
        jnp.zeros_like(jump_dens),
        jump_vel[0],
        jump_vel[1],
        jump_vel[2],
        jump_kin + gamma_gas / ((gamma_gas - 1.0) * prandtl) * jump_temp,
    ]
    values = []
    for component in range(5):
        values.append(
            0.5 * (flux_left[component] + flux_right[component])
            - 0.5 * dissipation[component]
            - viscosity * viscous_terms[component]
        )
    return jnp.stack(values, axis=0)


def flux_change(padded, along, normal):
    length = padded.shape[along]
    face_values = face_flux(
        lax.slice_in_dim(padded, 0, length - 1, axis=along),
        lax.slice_in_dim(padded, 1, length, axis=along),
        normal,
    )
    return lax.slice_in_dim(face_values, 1, length - 1, axis=along) - lax.slice_in_dim(
        face_values, 0, length - 2, axis=along
    )


def spectral_entry(offset, number):
    wrapped = jnp.mod(offset, number)
    parity = 1.0 - 2.0 * jnp.mod(wrapped, 2).astype(jnp.float32)
    angles = math.pi * wrapped.astype(jnp.float32) / number
    sine_val = jnp.where(wrapped == 0, 1.0, jnp.sin(angles))
    derivative = jnp.where(
        wrapped == 0, 0.0, math.pi / number * parity * jnp.cos(angles) / sine_val
    )
    return derivative + 0.5 * parity


def on_device(flow_state, period_match):
    instances = lax.axis_size("inst")
    phase_lag = instances // 4
    instance = lax.axis_index("inst")
    space_parts = lax.axis_size("space")
    position = lax.axis_index("space")
    labels = jnp.arange(period_match.shape[0], dtype=jnp.int32)
    matches = (period_match[:, None] == labels[None, :]).astype(jnp.int32)
    inverse = jnp.sum(labels[:, None] * matches, axis=0)
    mirror = jnp.array([1.0, 1.0, 1.0, -1.0, 1.0], jnp.float32).reshape(5, 1, 1, 1)

    def lagged(plane, steps):
        return from_behind(plane, "inst", steps)

    def timewise(conserved_vars):
        pieces = lax.all_gather(conserved_vars[None], "inst", axis=0, tiled=True)
        number = pieces.shape[0]
        others = jnp.arange(number, dtype=jnp.int32)
        weights = spectral_entry(instance - others, instances)
        return jnp.tensordot(weights, pieces, axes=1, precision=lax.Precision.HIGHEST)

    def evaluate(conserved_vars):
        prims = primitive(conserved_vars)
        padded = extended(prims, (("space", 1),), 1)
        lower_edge = jnp.where(position == 0, prims[:, :1], padded[:, :1])
        upper_edge = jnp.where(position == space_parts - 1, prims[:, -1:], padded[:, -1:])
        along_axial = jnp.concatenate([lower_edge, prims, upper_edge], axis=1)
        along_span = jnp.concatenate(
            [prims[:, :, :1] * mirror, prims, prims[:, :, -1:] * mirror], axis=2
        )
        ghost_below = jnp.take(lagged(prims[..., -1], phase_lag), period_match, axis=2)
        ghost_above = jnp.take(lagged(prims[..., 0], -phase_lag), inverse, axis=2)
        along_pitch = jnp.concatenate(
            [ghost_below[..., None], prims, ghost_above[..., None]], axis=3
        )
        spatial = (
            flux_change(along_axial, 1, 0)
            + flux_change(along_span, 2, 2)
            + flux_change(along_pitch, 3, 1)
        )
        return timewise(conserved_vars) + spatial

    initial = conserved(from_draw(flow_state[0]))
    section_state = initial - pseudo_step * evaluate(initial)
    return evaluate(section_state)[None]


inst_count = 4
layers = 4
chunk = 32
rows = 16
lanes = 128
tile = (rows, lanes)
vmem = pl.BlockSpec(memory_space=pltpu.VMEM)
smem = pl.BlockSpec(memory_space=pltpu.SMEM)
starts = (1.0, 0.8, 0.0, 0.0, 0.8)
spreads_of = (0.3, 0.3, 0.3, 0.3, 0.2)
ratio = gamma_gas / (gamma_gas - 1.0)


def weight_of(distance):
    parity = 1.0 - 2.0 * (distance % 2)
    if distance == 0:
        return 0.5
    if 2 * distance == inst_count:
        return 0.5 * parity
    angle = math.pi * distance / inst_count
    return math.pi / inst_count * parity * math.cos(angle) / math.sin(angle) + 0.5 * parity


order = (2, 3, 1, 0)


def in_order(items):
    return [items[order.index(distance)] for distance in range(inst_count)]


def unrolled(count, body, carry=None):
    for number in range(count):
        carry = body(number, carry)
    return carry


def lane_ids():
    return lax.broadcasted_iota(jnp.int32, tile, 1)


def row_ids():
    return lax.broadcasted_iota(jnp.int32, tile, 0)


def band_ids():
    return jnp.bitwise_and(lane_ids() // 4, 7)


def pick_lanes(values, index):
    return jnp.take_along_axis(values, index, axis=1, mode="promise_in_bounds")


def pick_rows(values, index):
    half = rows // 2
    low, high = values[:half], values[half:]
    parts = []
    for part in (index[:half], index[half:]):
        inner = jnp.bitwise_and(part, half - 1)
        from_low = jnp.take_along_axis(low, inner, axis=0, mode="promise_in_bounds")
        from_high = jnp.take_along_axis(high, inner, axis=0, mode="promise_in_bounds")
        parts.append(jnp.where(part < half, from_low, from_high))
    return jnp.concatenate(parts, axis=0)


def turn(values, amount):
    return pltpu.roll(values, amount % lanes if isinstance(amount, int) else amount, 1)


def mod_lanes(amount):
    return jnp.bitwise_and(amount, lanes - 1)


def group_ids():
    return lane_ids() // chunk


def turn_groups(tiles):
    low_half = lane_ids() < lanes // 2
    even_group = jnp.bitwise_and(group_ids(), 1) == 0
    out = list(tiles)
    for a, b, mask, width in ((0, 2, low_half, 2), (1, 3, low_half, 2), (0, 1, even_group, 1), (2, 3, even_group, 1)):
        first, second = out[a], out[b]
        out[a] = jnp.where(mask, first, turn(second, chunk * width))
        out[b] = jnp.where(mask, turn(first, -chunk * width), second)
    return out


def by_distance(items, me):
    out = list(items)
    for bit, pairs in ((1, ((0, 1), (2, 3))), (2, ((0, 2), (1, 3)))):
        is_set = jnp.bitwise_and(me, bit) != 0
        for a, b in pairs:
            out[a], out[b] = jnp.where(is_set, out[b], out[a]), jnp.where(is_set, out[a], out[b])
    return out


def pack_kernel(flow, *refs):
    messages = in_order(refs)
    me = lax.axis_index("inst")
    lane = lane_ids()
    place = lane // 4
    slot = jnp.bitwise_and(lane, 3)
    step = jnp.where(slot < 2, slot - 2, slot + chunk - 2)
    part_at = jnp.bitwise_and(place, 3)
    index = [mod_lanes(step + (chunk * jnp.bitwise_xor(part_at, layer) + lanes)) for layer in range(layers)]
    edges = [jnp.zeros(tile, jnp.float32)] * inst_count
    for field in range(5):
        tiles = [flow[0, field, layer] for layer in range(layers)]
        for distance, values in enumerate(by_distance(turn_groups(tiles), me)):
            messages[distance][field] = values
        for layer in range(layers):
            got = pick_lanes(tiles[layer], index[layer])
            for distance in range(inst_count):
                here = place == field * 4 + jnp.bitwise_xor(me, distance ^ layer)
                edges[distance] = jnp.where(here, got, edges[distance])
    for distance in range(inst_count):
        messages[distance][5] = edges[distance]


def spread_tiles(received, field, me):
    return turn_groups(by_distance([message[field] for message in received], me))


def unpack_kernel(*refs):
    received, (near_b, near_a, main, halo) = in_order(refs[:4]), refs[5:]
    me = lax.axis_index("inst")
    even = jnp.bitwise_and(lax.axis_index("space"), 1) == 0
    lane = lane_ids()
    owner = group_ids()
    band = band_ids()
    level = jnp.clip(band - 1, 0, layers - 1)
    inner = jnp.bitwise_xor(level, me) * 4 + jnp.bitwise_and(lane, 3)
    up_edge = down_edge = jnp.zeros(tile, jnp.float32)
    for field in range(5):
        tiles = spread_tiles(received, field, me)
        for layer in range(layers):
            main[field, layer] = tiles[layer]
        for place in range(2):
            near_a[2 * field + place] = jnp.where(even, tiles[2 + place], tiles[place])
            near_b[2 * field + place] = jnp.where(even, tiles[place], tiles[2 + place])
        edges = None
        for distance in range(inst_count):
            got = pick_lanes(received[distance][5], inner + 16 * field)
            edges = got if edges is None else jnp.where(owner == jnp.bitwise_xor(me, distance), got, edges)
        halo[field] = edges
        up_edge = jnp.where(band == field, turn(edges, 4 * (field - layers)), up_edge)
        down_edge = jnp.where(band == field, turn(edges, 4 * (field - 1)), down_edge)
    near_a[10] = jnp.where(even, up_edge, down_edge)
    near_b[10] = jnp.where(even, down_edge, up_edge)


class Cells:
    def __init__(self, parts):
        self.parts = list(parts)
        self.root, self.vel, self.temp = parts[0], list(parts[1:4]), parts[4]
        if len(parts) == 5:
            dens = self.root * self.root
            kinetic = 0.5 * (self.vel[0] * self.vel[0] + self.vel[1] * self.vel[1] + self.vel[2] * self.vel[2])
            enth = ratio * self.temp + kinetic
            heat = 2.0 * viscosity * (kinetic + ratio / prandtl * self.temp)
            self.parts += [dens, dens * self.temp, enth, heat]
        self.dens, self.pres, self.enth, self.heat = self.parts[5:]
        self.base = self.parts[:5]

    def map(self, change):
        return Cells([change(part) for part in self.base])

    def conserved(self):
        dens, enth = self.dens, self.enth
        return [dens] + [dens * part for part in self.vel] + [dens * enth - self.pres]


fields_kept = 9


def cells_of(dens, vel, pres):
    inverse_root = lax.rsqrt(dens)
    return Cells([dens * inverse_root] + list(vel) + [pres * (inverse_root * inverse_root)])


def cells_of_draws(draws):
    start = [base + spread * draw if base else spread * draw for base, spread, draw in zip(starts, spreads_of, draws)]
    return cells_of(start[0], start[1:4], start[4])


def cells_of_conserved(state):
    dens = state[0]
    inverse = 1.0 / dens
    vel = [part * inverse for part in state[1:4]]
    kinetic = vel[0] * vel[0] + vel[1] * vel[1] + vel[2] * vel[2]
    pres = (gamma_gas - 1.0) * (state[4] - 0.5 * dens * kinetic)
    return cells_of(dens, vel, pres)


def roe_flux(low, high, normal):
    jump_dens = high.dens - low.dens
    jump_pres = high.pres - low.pres
    jump = [b - a for a, b in zip(low.vel, high.vel)]
    share = high.root / (low.root + high.root)
    vel = [a + share * d for a, d in zip(low.vel, jump)]
    enth = low.enth + share * (high.enth - low.enth)
    half_sq = 0.5 * (vel[0] * vel[0] + vel[1] * vel[1] + vel[2] * vel[2])
    sound_sq = (gamma_gas - 1.0) * (enth - half_sq)
    inverse = lax.rsqrt(sound_sq)
    sound = sound_sq * inverse
    dens_roe = low.root * high.root
    along = vel[normal]
    jump_along = jump[normal]
    press_part = jump_pres * (inverse * inverse)
    speed_part = dens_roe * inverse * jump_along
    bound = entropy_share * sound
    curve = (0.5 / entropy_share) * inverse
    floor = 0.5 * bound

    def fixed(speed):
        size = jnp.abs(speed)
        return jnp.where(size >= bound, size, speed * speed * curve + floor)

    slow = 0.5 * fixed(along - sound) * (press_part - speed_part)
    fast = 0.5 * fixed(along + sound) * (press_part + speed_part)
    middle = fixed(along)
    entropy = middle * (jump_dens - press_part)
    both = slow + fast
    total = both + entropy
    push = sound * (fast - slow)
    shear = middle * dens_roe
    mass_low = low.dens * low.vel[normal]
    mass_high = high.dens * high.vel[normal]
    out = [mass_low + mass_high - total]
    work = None
    for part in range(3):
        value = mass_low * low.vel[part] + mass_high * high.vel[part] - vel[part] * total
        if part == normal:
            value = value + (low.pres + high.pres) - push - (2.0 * viscosity) * jump_along
        else:
            value = value - (shear + 2.0 * viscosity) * jump[part]
            term = vel[part] * jump[part]
            work = term if work is None else work + term
        out.append(value)
    lost = enth * both + along * push + entropy * half_sq + shear * work
    out.append(mass_low * low.enth + mass_high * high.enth - lost - (high.heat - low.heat))
    return out


def span_change(cells):
    row = row_ids()
    faces = roe_flux(cells, cells.map(lambda part: pltpu.roll(part, rows - 1, 0)), 2)
    w = cells.vel[2]
    sound_sq = (gamma_gas - 1.0) * (cells.enth - 0.5 * (cells.vel[0] * cells.vel[0] + cells.vel[1] * cells.vel[1]))
    sound = sound_sq * lax.rsqrt(sound_sq)
    still = 2.0 * (cells.dens * w * w + cells.pres)
    moving = 2.0 * w * (sound * cells.dens + 2.0 * viscosity)
    changes = []
    for part in range(5):
        top = still + moving if part == 3 else 0.0
        bottom = still - moving if part == 3 else 0.0
        upper = jnp.where(row == rows - 1, top, faces[part])
        lower = jnp.where(row == 0, bottom, pltpu.roll(faces[part], 1, 0))
        changes.append(upper - lower)
    return changes


def over_instances(values):
    weights = [weight_of(distance) for distance in range(inst_count)]
    across = turn(values, 2 * chunk)
    return (weights[0] * values + weights[2] * across) + turn(weights[1] * values + weights[3] * across, chunk)


def put(ref, place, cells):
    for number, part in enumerate(cells.parts):
        ref[place, number] = part


def get(ref, place):
    return Cells([ref[place, number] for number in range(fields_kept)])


class Pitch:
    def __init__(self, above, below, edge_faces):
        self.above, self.below, self.edge_faces = above, below, edge_faces
        self.lag = inst_count // 4
        me = lax.axis_index("inst")
        lane = lane_ids()
        self.slot = jnp.bitwise_and(lane, 3)
        self.band = band_ids()
        column = jnp.bitwise_and(lane, chunk - 1)
        self.is_first, self.is_last = column == 0, column == chunk - 1
        self.seam = self.slot == jnp.where(me == 0, 1, jnp.where(me == inst_count - 1, 3, -1))
        start = group_ids() * chunk
        self.to_main = start + jnp.where(self.is_first, 1, 3)
        self.from_main = start + jnp.where(self.slot == 1, 0, chunk - 1)
        self.beside = lane + jnp.where(self.slot == 3, -1, 1)

    def mains(self, ref, places):
        out = [None] * 5
        for layer, place in places:
            for number in range(5):
                got = pick_lanes(ref[place, number], self.from_main)
                out[number] = got if out[number] is None else jnp.where(self.band == layer + 1, got, out[number])
        return out

    def edges(self, cells, mains):
        slot = self.slot
        lower = Cells([jnp.where(slot == 3, b, a) for a, b in zip(cells.base, mains)])
        upper = []
        for a, b in zip(cells.base, mains):
            value = jnp.where(slot == 1, b, pick_lanes(a, self.beside))
            other = pick_rows(turn(value, -chunk * self.lag), self.above)
            upper.append(jnp.where(self.seam, other, value))
        faces = roe_flux(lower, Cells(upper), 1)
        lower_use = [jnp.where(self.seam, pick_rows(turn(face, chunk * self.lag), self.below), face) for face in faces]
        for part in range(5):
            self.edge_faces[part] = jnp.where(slot == 1, lower_use[part], faces[part])
        return faces, lower_use

    def change(self, cells, layer):
        faces = roe_flux(cells, cells.map(lambda part: turn(part, -1)), 1)
        index = (layer + 1) * 4 + self.to_main
        changes = []
        for part in range(5):
            edge = pick_lanes(self.edge_faces[part], index)
            upper = jnp.where(self.is_last, edge, faces[part])
            lower = jnp.where(self.is_first, edge, turn(faces[part], 1))
            changes.append(upper - lower)
        return changes


def index_kernel(match, behind, above, below):
    row = row_ids()
    below_of = jnp.zeros(tile, jnp.int32)
    above_of = jnp.zeros(tile, jnp.int32)
    for k in range(rows):
        value = match[k]
        below_of = jnp.where(row == k, value, below_of)
        above_of = jnp.where(row == value, k, above_of)
    below[...], above[...] = below_of, above_of


def inner_kernel(above, below, main, halo, first, edge_first, part_first, part_edge, second, part_second, edge_faces):
    pitch = Pitch(above[...], below[...], edge_faces)
    slot = pitch.slot
    middle = range(1, layers - 1)
    for layer in range(layers):
        put(first, layer, cells_of_draws([main[field, layer] for field in range(5)]))
    cells = cells_of_draws([halo[field] for field in range(5)])
    for number, part in enumerate(cells.parts):
        edge_first[number] = part
    faces, lower_use = pitch.edges(cells, pitch.mains(first, [(layer, layer) for layer in range(layers)]))
    span = span_change(cells)
    axial = roe_flux(cells, cells.map(lambda part: turn(part, -4)), 0)
    state = cells.conserved()
    for part in range(5):
        along = jnp.where(slot == 1, faces[part] - turn(faces[part], 1), faces[part] - turn(lower_use[part], -1))
        value = over_instances(state[part]) + 0.5 * (along + span[part])
        part_edge[part] = value
        value = value + 0.5 * (axial[part] - turn(axial[part], 4))
        state[part] = state[part] - pseudo_step * value
    edge_second = cells_of_conserved(state)

    def step(layer, below_faces):
        cells = get(first, layer)
        above_faces = roe_flux(cells, get(first, jnp.minimum(layer + 1, layers - 1)), 0)
        span = span_change(cells)
        along = pitch.change(cells, layer)
        state = cells.conserved()
        outs = []
        for part in range(5):
            upper = jnp.where(layer == layers - 1, 0.0, above_faces[part])
            part_first[layer, part] = over_instances(state[part]) + 0.5 * (
                (upper - below_faces[part]) + span[part] + along[part]
            )
            outs.append(upper)
        return tuple(outs)

    lax.fori_loop(0, layers, step, (jnp.zeros(tile, jnp.float32),) * 5)

    for place, layer in enumerate(middle):
        state = get(first, layer).conserved()
        state = [value - pseudo_step * part_first[layer, part] for part, value in enumerate(state)]
        put(second, place, cells_of_conserved(state))
    pitch.edges(edge_second, pitch.mains(second, [(layer, place) for place, layer in enumerate(middle)]))
    between = roe_flux(get(second, 0), get(second, 1), 0)
    for part in range(5):
        part_second[0, part] = between[part]
        part_second[1, part] = -between[part]

    def second_step(place, carry):
        cells = get(second, place)
        span = span_change(cells)
        along = pitch.change(cells, place + 1)
        state = cells.conserved()
        for part in range(5):
            value = part_second[place, part] + span[part] + along[part]
            part_second[place, part] = over_instances(state[part]) + 0.5 * value
        return carry

    lax.fori_loop(0, layers - 2, second_step, 0)


def outer_kernel(
    first, edge_first, part_first, part_edge, second_middle, part_second, above, below, halo, near_b, near_a, *refs
):
    messages, (ends, second, change, edge_faces) = in_order(refs[:4]), refs[4:]
    where_on = lax.axis_index("space")
    even = jnp.bitwise_and(where_on, 1) == 0
    at_low = where_on == 0
    at_high = where_on == lax.axis_size("space") - 1
    pitch = Pitch(above[...], below[...], edge_faces)
    band = pitch.band

    for number in range(fields_kept):
        ends[2, number] = first[0, number]
        ends[3, number] = first[layers - 1, number]
        second[2, number] = second_middle[0, number]
        second[layers - 1, number] = second_middle[layers - 3, number]

    for high in range(2):
        own = get(first, high * (layers - 1))
        closed, from_a = (at_high, even) if high else (at_low, jnp.logical_not(even))
        for place in range(2):
            draws = [jnp.where(from_a, near_a[2 * field + place], near_b[2 * field + place]) for field in range(5)]
            cells = cells_of_draws(draws)
            pairs = zip(own.parts, cells.parts)
            put(ends, place + 4 * high, Cells([jnp.where(closed, a, b) for a, b in pairs]))

    low_tile = jnp.where(even, near_b[10], near_a[10])
    high_tile = jnp.where(even, near_a[10], near_b[10])
    outside = []
    for field in range(5):
        inside = halo[field]
        low = jnp.where(at_low, inside, turn(low_tile, -4 * field))
        high = jnp.where(at_high, inside, turn(high_tile, 4 * (layers + 1 - field)))
        outside.append(jnp.where(band == 0, low, high))
    within = jnp.logical_and(band > 0, band < layers + 1)
    edge_cells = cells_of_draws(outside)
    edge_cells = Cells([jnp.where(within, edge_first[number], edge_cells.parts[number]) for number in range(fields_kept)])
    pitch.edges(edge_cells, pitch.mains(ends, [(-1, 1), (layers, 4)]))
    axial = roe_flux(edge_cells, edge_cells.map(lambda part: turn(part, -4)), 0)
    state = edge_cells.conserved()
    for part in range(5):
        value = part_edge[part] + 0.5 * (axial[part] - turn(axial[part], 4))
        state[part] = state[part] - pseudo_step * value
    edge_second = cells_of_conserved(state)

    def end_values(ref, high, layer):
        base = 3 * high
        cells = get(ref, base + 1)
        lower = roe_flux(get(ref, base), cells, 0)
        upper = roe_flux(cells, get(ref, base + 2), 0)
        span = span_change(cells)
        along = pitch.change(cells, layer)
        state = cells.conserved()
        values = []
        for part in range(5):
            value = (upper[part] - lower[part]) + span[part] + along[part]
            values.append(over_instances(state[part]) + 0.5 * value)
            change[high, part] = jnp.where(high == 0, -upper[part], lower[part])
        return state, values

    def first_step(high, carry):
        state, values = end_values(ends, high, high * (layers + 1) - 1)
        state = [a - pseudo_step * b for a, b in zip(state, values)]
        put(second, high * (layers + 1), cells_of_conserved(state))
        return carry

    unrolled(2, first_step)

    for high in range(2):
        layer = high * (layers - 1)
        state = get(first, layer).conserved()
        for part in range(5):
            state[part] = state[part] - pseudo_step * (part_first[layer, part] + 0.5 * change[high, part])
        put(second, layer + 1, cells_of_conserved(state))
    for number in range(fields_kept):
        second[0, number] = jnp.where(at_low, second[1, number], second[0, number])
        second[layers + 1, number] = jnp.where(at_high, second[layers, number], second[layers + 1, number])

    pitch.edges(edge_second, pitch.mains(second, [(0, 1), (layers - 1, layers)]))

    def second_step(high, carry):
        _, values = end_values(second, high, high * (layers - 1))
        for part in range(5):
            ends[high, part] = values[part]
        return carry

    lax.fori_loop(0, 2, second_step, 0)

    me = lax.axis_index("inst")
    for field in range(5):
        tiles = [ends[0, field], part_second[0, field] + 0.5 * change[0, field]]
        tiles += [part_second[1, field] + 0.5 * change[1, field], ends[1, field]]
        for distance, values in enumerate(by_distance(turn_groups(tiles), me)):
            messages[distance][field] = values


def return_kernel(*refs):
    received, out = in_order(refs[:4]), refs[4]
    me = lax.axis_index("inst")

    def one_field(field, carry):
        for layer, values in enumerate(spread_tiles(received, field, me)):
            out[0, field, layer] = values
        return carry

    unrolled(5, one_field)


def call(kernel, outs, operands, scratch=(), scalars=0):
    shapes = [jax.ShapeDtypeStruct(shape, kind) for shape, kind in outs]
    return pl.pallas_call(
        kernel,
        out_shape=shapes,
        in_specs=[smem] * scalars + [vmem] * (len(operands) - scalars),
        out_specs=[vmem] * len(shapes),
        scratch_shapes=[pltpu.VMEM(shape, jnp.float32) for shape in scratch],
        compiler_params=pltpu.CompilerParams(vmem_limit_bytes=16 * 2**20),
    )(*operands)


def floats(*shape):
    return shape + tile, jnp.float32


def swap_instances(messages):
    got = []
    for distance, message in zip(order, messages):
        route = [(i, i ^ distance) for i in range(inst_count)]
        got.append(lax.ppermute(message, "inst", route) if distance else message)
    return got


def on_device_fast(flow_state, period_match):
    count = lax.axis_size("space")
    messages = call(pack_kernel, [floats(6)] * inst_count, [flow_state])
    integers = (tile, jnp.int32)
    above, below = call(index_kernel, [integers, integers], [period_match, messages[-1]], scalars=1)
    near_b, near_a, main, halo = call(
        unpack_kernel, [floats(11), floats(11), floats(5, layers), floats(5)], [*swap_instances(messages), above]
    )
    route_a = [(i, i ^ 1) for i in range(count)]
    route_b = []
    for n in range(inst_count):
        for i in range(count):
            far = (n, ((i - 1) ^ 1) + 1) if 0 < i < count - 1 else (n ^ 1, i)
            route_b.append((n * count + i, far[0] * count + far[1]))
    near_b = lax.ppermute(near_b, ("inst", "space"), route_b)
    near_a = lax.ppermute(near_a, "space", route_a)
    inner = call(
        inner_kernel,
        [
            floats(layers, fields_kept),
            floats(fields_kept),
            floats(layers, 5),
            floats(5),
            floats(layers - 2, fields_kept),
            floats(layers - 2, 5),
        ],
        [above, below, main, halo],
        [(5,) + tile],
    )
    results = call(
        outer_kernel,
        [floats(5)] * inst_count,
        [*inner, above, below, halo, near_b, near_a],
        [(6, fields_kept) + tile, (layers + 2, fields_kept) + tile, (2, 5) + tile, (5,) + tile],
    )
    return call(return_kernel, [(flow_state.shape, jnp.float32)], swap_instances(results))[0]


def solution(mesh):
    in_specs = (P(("groups", "inst"), None, "space", None, None), P())
    out_specs = P(("groups", "inst"), None, "space", None, None)

    def whole(flow_state, period_match):
        block = (flow_state.shape[2] // mesh.shape["space"],) + flow_state.shape[3:]
        fits = mesh.shape["inst"] == inst_count and mesh.shape["space"] % 2 == 0
        body = on_device_fast if fits and block == (layers, rows, lanes) else on_device
        return jax.shard_map(body, mesh=mesh, in_specs=in_specs, out_specs=out_specs, check_vma=False)(
            flow_state, period_match
        )

    return whole
```

```python
import math

import jax
import jax.numpy as jnp
from jax import lax
from jax.experimental import pallas as pl
from jax.experimental.pallas import tpu as pltpu
from jax.sharding import PartitionSpec as P

gamma_gas = 1.4
prandtl = 0.72
viscosity = 0.1
pseudo_step = 0.03
entropy_share = 0.1


def from_behind(block, axis, distance):
    devices = range(lax.axis_size(axis))
    route = [((i - distance) % len(devices), i) for i in devices]
    return lax.ppermute(block, axis, route)


def extended(cells, sides, width):
    for axis, dim in sides:
        count = lax.axis_size(axis)
        ends = count - 1
        head = lax.slice_in_dim(cells, 0, width, axis=dim)
        tail = lax.slice_in_dim(cells, cells.shape[dim] - width, cells.shape[dim], axis=dim)
        cells = jnp.concatenate(
            [
                lax.ppermute(tail, axis, [(i, (i + 1) % count) for i in range(ends)]),
                cells,
                lax.ppermute(head, axis, [((i + 1) % count, i) for i in range(ends)]),
            ],
            axis=dim,
        )
    return cells


def from_draw(draws):
    shape = (5,) + (1,) * (draws.ndim - 1)
    offsets = jnp.array([1.0, 0.8, 0.0, 0.0, 0.8], jnp.float32).reshape(shape)
    spreads = jnp.array([0.3, 0.3, 0.3, 0.3, 0.2], jnp.float32).reshape(shape)
    return offsets + spreads * draws


def conserved(primitives):
    dens = primitives[0]
    velocity = primitives[1:4]
    kinetic = 0.5 * dens * jnp.sum(velocity * velocity, axis=0)
    energy = primitives[4] / (gamma_gas - 1.0) + kinetic
    return jnp.concatenate([dens[None], dens[None] * velocity, energy[None]], axis=0)


def primitive(conserved_vars):
    dens = conserved_vars[0]
    velocity = conserved_vars[1:4] / dens
    pressure = (gamma_gas - 1.0) * (
        conserved_vars[4] - 0.5 * dens * jnp.sum(velocity * velocity, axis=0)
    )
    return jnp.concatenate([dens[None], velocity, pressure[None]], axis=0)


def entropy_fix(eigen_val, sound_speed):
    spread = entropy_share * sound_speed
    magnitude = jnp.abs(eigen_val)
    return jnp.where(
        magnitude >= spread, magnitude, (eigen_val * eigen_val + spread * spread) / (2.0 * spread)
    )


def euler_flux(dens, velocity, pressure, enthalpy, normal):
    normal_vel = velocity[normal]
    values = [dens * normal_vel]
    for component in range(3):
        moment = dens * velocity[component] * normal_vel
        if component == normal:
            moment = moment + pressure
        values.append(moment)
    values.append(dens * enthalpy * normal_vel)
    return values


def face_flux(left_cells, right_cells, normal):
    dens_left, vel_left, pres_left = (left_cells[0], left_cells[1:4], left_cells[4])
    dens_right, vel_right, pres_right = (right_cells[0], right_cells[1:4], right_cells[4])
    ratio = gamma_gas / (gamma_gas - 1.0)
    sq_left = jnp.sum(vel_left * vel_left, axis=0)
    sq_right = jnp.sum(vel_right * vel_right, axis=0)
    enth_left = ratio * pres_left / dens_left + 0.5 * sq_left
    enth_right = ratio * pres_right / dens_right + 0.5 * sq_right
    flux_left = euler_flux(dens_left, vel_left, pres_left, enth_left, normal)
    flux_right = euler_flux(dens_right, vel_right, pres_right, enth_right, normal)
    root_left = jnp.sqrt(dens_left)
    root_right = jnp.sqrt(dens_right)
    root_sum = root_left + root_right
    vel_roe = (root_left * vel_left + root_right * vel_right) / root_sum
    enth_roe = (root_left * enth_left + root_right * enth_right) / root_sum
    speed_sq = jnp.sum(vel_roe * vel_roe, axis=0)
    sound_sq = (gamma_gas - 1.0) * (enth_roe - 0.5 * speed_sq)
    sound_speed = jnp.sqrt(sound_sq)
    normal_vel = vel_roe[normal]
    dens_roe = root_left * root_right
    jump_dens = dens_right - dens_left
    jump_pres = pres_right - pres_left
    jump_vel = vel_right - vel_left
    jump_normal = jump_vel[normal]
    wave_slow = (jump_pres - dens_roe * sound_speed * jump_normal) / (2.0 * sound_sq)
    wave_fast = (jump_pres + dens_roe * sound_speed * jump_normal) / (2.0 * sound_sq)
    wave_mid = jump_dens - jump_pres / sound_sq
    eigen_mid = entropy_fix(normal_vel, sound_speed)
    flux_slow = entropy_fix(normal_vel - sound_speed, sound_speed) * wave_slow
    flux_fast = entropy_fix(normal_vel + sound_speed, sound_speed) * wave_fast
    dissipation = [flux_slow + eigen_mid * wave_mid + flux_fast]
    for component in range(3):
        unit_dir = 1.0 if component == normal else 0.0
        term = flux_slow * (vel_roe[component] - unit_dir * sound_speed)
        term = term + eigen_mid * (
            wave_mid * vel_roe[component]
            + dens_roe * (jump_vel[component] - unit_dir * jump_normal)
        )
        term = term + flux_fast * (vel_roe[component] + unit_dir * sound_speed)
        dissipation.append(term)
    shear_work = jnp.sum(vel_roe * jump_vel, axis=0) - normal_vel * jump_normal
    energy_term = flux_slow * (enth_roe - normal_vel * sound_speed)
    energy_term = energy_term + eigen_mid * (wave_mid * 0.5 * speed_sq + dens_roe * shear_work)
    energy_term = energy_term + flux_fast * (enth_roe + normal_vel * sound_speed)
    dissipation.append(energy_term)
    jump_temp = pres_right / dens_right - pres_left / dens_left
    jump_kin = 0.5 * (sq_right - sq_left)
    viscous_terms = [
        jnp.zeros_like(jump_dens),
        jump_vel[0],
        jump_vel[1],
        jump_vel[2],
        jump_kin + gamma_gas / ((gamma_gas - 1.0) * prandtl) * jump_temp,
    ]
    values = []
    for component in range(5):
        values.append(
            0.5 * (flux_left[component] + flux_right[component])
            - 0.5 * dissipation[component]
            - viscosity * viscous_terms[component]
        )
    return jnp.stack(values, axis=0)


def flux_change(padded, along, normal):
    length = padded.shape[along]
    face_values = face_flux(
        lax.slice_in_dim(padded, 0, length - 1, axis=along),
        lax.slice_in_dim(padded, 1, length, axis=along),
        normal,
    )
    return lax.slice_in_dim(face_values, 1, length - 1, axis=along) - lax.slice_in_dim(
        face_values, 0, length - 2, axis=along
    )


def spectral_entry(offset, number):
    wrapped = jnp.mod(offset, number)
    parity = 1.0 - 2.0 * jnp.mod(wrapped, 2).astype(jnp.float32)
    angles = math.pi * wrapped.astype(jnp.float32) / number
    sine_val = jnp.where(wrapped == 0, 1.0, jnp.sin(angles))
    derivative = jnp.where(
        wrapped == 0, 0.0, math.pi / number * parity * jnp.cos(angles) / sine_val
    )
    return derivative + 0.5 * parity


def on_device(flow_state, period_match):
    instances = lax.axis_size("inst")
    phase_lag = instances // 4
    instance = lax.axis_index("inst")
    space_parts = lax.axis_size("space")
    position = lax.axis_index("space")
    labels = jnp.arange(period_match.shape[0], dtype=jnp.int32)
    matches = (period_match[:, None] == labels[None, :]).astype(jnp.int32)
    inverse = jnp.sum(labels[:, None] * matches, axis=0)
    mirror = jnp.array([1.0, 1.0, 1.0, -1.0, 1.0], jnp.float32).reshape(5, 1, 1, 1)

    def lagged(plane, steps):
        return from_behind(plane, "inst", steps)

    def timewise(conserved_vars):
        pieces = lax.all_gather(conserved_vars[None], "inst", axis=0, tiled=True)
        number = pieces.shape[0]
        others = jnp.arange(number, dtype=jnp.int32)
        weights = spectral_entry(instance - others, instances)
        return jnp.tensordot(weights, pieces, axes=1, precision=lax.Precision.HIGHEST)

    def evaluate(conserved_vars):
        prims = primitive(conserved_vars)
        padded = extended(prims, (("space", 1),), 1)
        lower_edge = jnp.where(position == 0, prims[:, :1], padded[:, :1])
        upper_edge = jnp.where(position == space_parts - 1, prims[:, -1:], padded[:, -1:])
        along_axial = jnp.concatenate([lower_edge, prims, upper_edge], axis=1)
        along_span = jnp.concatenate(
            [prims[:, :, :1] * mirror, prims, prims[:, :, -1:] * mirror], axis=2
        )
        ghost_below = jnp.take(lagged(prims[..., -1], phase_lag), period_match, axis=2)
        ghost_above = jnp.take(lagged(prims[..., 0], -phase_lag), inverse, axis=2)
        along_pitch = jnp.concatenate(
            [ghost_below[..., None], prims, ghost_above[..., None]], axis=3
        )
        spatial = (
            flux_change(along_axial, 1, 0)
            + flux_change(along_span, 2, 2)
            + flux_change(along_pitch, 3, 1)
        )
        return timewise(conserved_vars) + spatial

    initial = conserved(from_draw(flow_state[0]))
    section_state = initial - pseudo_step * evaluate(initial)
    return evaluate(section_state)[None]


inst_count = 4
layers = 4
chunk = 32
rows = 16
lanes = 128
tile = (rows, lanes)
vmem = pl.BlockSpec(memory_space=pltpu.VMEM)
smem = pl.BlockSpec(memory_space=pltpu.SMEM)
starts = (1.0, 0.8, 0.0, 0.0, 0.8)
spreads_of = (0.3, 0.3, 0.3, 0.3, 0.2)
ratio = gamma_gas / (gamma_gas - 1.0)


def weight_of(distance):
    parity = 1.0 - 2.0 * (distance % 2)
    if distance == 0:
        return 0.5
    if 2 * distance == inst_count:
        return 0.5 * parity
    angle = math.pi * distance / inst_count
    return math.pi / inst_count * parity * math.cos(angle) / math.sin(angle) + 0.5 * parity


order = (2, 3, 1, 0)


def in_order(items):
    return [items[order.index(distance)] for distance in range(inst_count)]


def unrolled(count, body, carry=None):
    for number in range(count):
        carry = body(number, carry)
    return carry


def lane_ids():
    return lax.broadcasted_iota(jnp.int32, tile, 1)


def row_ids():
    return lax.broadcasted_iota(jnp.int32, tile, 0)


def band_ids():
    return jnp.bitwise_and(lane_ids() // 4, 7)


def pick_lanes(values, index):
    return jnp.take_along_axis(values, index, axis=1, mode="promise_in_bounds")


def pick_rows(values, index):
    half = rows // 2
    low, high = values[:half], values[half:]
    parts = []
    for part in (index[:half], index[half:]):
        inner = jnp.bitwise_and(part, half - 1)
        from_low = jnp.take_along_axis(low, inner, axis=0, mode="promise_in_bounds")
        from_high = jnp.take_along_axis(high, inner, axis=0, mode="promise_in_bounds")
        parts.append(jnp.where(part < half, from_low, from_high))
    return jnp.concatenate(parts, axis=0)


def turn(values, amount):
    return pltpu.roll(values, amount % lanes if isinstance(amount, int) else amount, 1)


def mod_lanes(amount):
    return jnp.bitwise_and(amount, lanes - 1)


def group_ids():
    return lane_ids() // chunk


def turn_groups(tiles):
    low_half = lane_ids() < lanes // 2
    even_group = jnp.bitwise_and(group_ids(), 1) == 0
    out = list(tiles)
    for a, b, mask, width in ((0, 2, low_half, 2), (1, 3, low_half, 2), (0, 1, even_group, 1), (2, 3, even_group, 1)):
        first, second = out[a], out[b]
        out[a] = jnp.where(mask, first, turn(second, chunk * width))
        out[b] = jnp.where(mask, turn(first, -chunk * width), second)
    return out


def by_distance(items, me):
    out = list(items)
    for bit, pairs in ((1, ((0, 1), (2, 3))), (2, ((0, 2), (1, 3)))):
        is_set = jnp.bitwise_and(me, bit) != 0
        for a, b in pairs:
            out[a], out[b] = jnp.where(is_set, out[b], out[a]), jnp.where(is_set, out[a], out[b])
    return out


def pack_kernel(flow, *refs):
    messages = in_order(refs)
    me = lax.axis_index("inst")
    lane = lane_ids()
    place = lane // 4
    slot = jnp.bitwise_and(lane, 3)
    step = jnp.where(slot < 2, slot - 2, slot + chunk - 2)
    part_at = jnp.bitwise_and(place, 3)
    index = [mod_lanes(step + (chunk * jnp.bitwise_xor(part_at, layer) + lanes)) for layer in range(layers)]
    edges = [jnp.zeros(tile, jnp.float32)] * inst_count
    for field in range(5):
        tiles = [flow[0, field, layer] for layer in range(layers)]
        for distance, values in enumerate(by_distance(turn_groups(tiles), me)):
            messages[distance][field] = values
        for layer in range(layers):
            got = pick_lanes(tiles[layer], index[layer])
            for distance in range(inst_count):
                here = place == field * 4 + jnp.bitwise_xor(me, distance ^ layer)
                edges[distance] = jnp.where(here, got, edges[distance])
    for distance in range(inst_count):
        messages[distance][5] = edges[distance]


def spread_tiles(received, field, me):
    return turn_groups(by_distance([message[field] for message in received], me))


def unpack_kernel(*refs):
    received, (near_a, near_b, main, halo) = in_order(refs[:4]), refs[5:]
    me = lax.axis_index("inst")
    even = jnp.bitwise_and(lax.axis_index("space"), 1) == 0
    lane = lane_ids()
    owner = group_ids()
    band = band_ids()
    level = jnp.clip(band - 1, 0, layers - 1)
    inner = jnp.bitwise_xor(level, me) * 4 + jnp.bitwise_and(lane, 3)
    up_edge = down_edge = jnp.zeros(tile, jnp.float32)
    for field in range(5):
        tiles = spread_tiles(received, field, me)
        for layer in range(layers):
            main[field, layer] = tiles[layer]
        for place in range(2):
            near_a[2 * field + place] = jnp.where(even, tiles[2 + place], tiles[place])
            near_b[2 * field + place] = jnp.where(even, tiles[place], tiles[2 + place])
        edges = None
        for distance in range(inst_count):
            got = pick_lanes(received[distance][5], inner + 16 * field)
            edges = got if edges is None else jnp.where(owner == jnp.bitwise_xor(me, distance), got, edges)
        halo[field] = edges
        up_edge = jnp.where(band == field, turn(edges, 4 * (field - layers)), up_edge)
        down_edge = jnp.where(band == field, turn(edges, 4 * (field - 1)), down_edge)
    near_a[10] = jnp.where(even, up_edge, down_edge)
    near_b[10] = jnp.where(even, down_edge, up_edge)


class Cells:
    def __init__(self, parts):
        self.parts = list(parts)
        self.root, self.vel, self.temp = parts[0], list(parts[1:4]), parts[4]
        if len(parts) == 5:
            dens = self.root * self.root
            kinetic = 0.5 * (self.vel[0] * self.vel[0] + self.vel[1] * self.vel[1] + self.vel[2] * self.vel[2])
            enth = ratio * self.temp + kinetic
            heat = 2.0 * viscosity * (kinetic + ratio / prandtl * self.temp)
            self.parts += [dens, dens * self.temp, enth, heat]
        self.dens, self.pres, self.enth, self.heat = self.parts[5:]
        self.base = self.parts[:5]

    def map(self, change):
        return Cells([change(part) for part in self.base])

    def conserved(self):
        dens, enth = self.dens, self.enth
        return [dens] + [dens * part for part in self.vel] + [dens * enth - self.pres]


fields_kept = 9


def cells_of(dens, vel, pres):
    inverse_root = lax.rsqrt(dens)
    return Cells([dens * inverse_root] + list(vel) + [pres * (inverse_root * inverse_root)])


def cells_of_draws(draws):
    start = [base + spread * draw if base else spread * draw for base, spread, draw in zip(starts, spreads_of, draws)]
    return cells_of(start[0], start[1:4], start[4])


def cells_of_conserved(state):
    dens = state[0]
    inverse_root = lax.rsqrt(dens)
    inverse = inverse_root * inverse_root
    vel = [part * inverse for part in state[1:4]]
    kinetic = 0.5 * (vel[0] * vel[0] + vel[1] * vel[1] + vel[2] * vel[2])
    return Cells([dens * inverse_root] + vel + [(gamma_gas - 1.0) * (state[4] * inverse - kinetic)])


def roe_flux(low, high, normal):
    jump_dens = high.dens - low.dens
    jump_pres = high.pres - low.pres
    jump = [b - a for a, b in zip(low.vel, high.vel)]
    share = high.root / (low.root + high.root)
    vel = [a + share * d for a, d in zip(low.vel, jump)]
    enth = low.enth + share * (high.enth - low.enth)
    half_sq = 0.5 * (vel[0] * vel[0] + vel[1] * vel[1] + vel[2] * vel[2])
    sound_sq = (gamma_gas - 1.0) * (enth - half_sq)
    inverse = lax.rsqrt(sound_sq)
    sound = sound_sq * inverse
    dens_roe = low.root * high.root
    along = vel[normal]
    jump_along = jump[normal]
    press_part = jump_pres * (inverse * inverse)
    speed_part = dens_roe * inverse * jump_along
    bound = entropy_share * sound
    curve = (0.5 / entropy_share) * inverse
    floor = 0.5 * bound

    def fixed(speed):
        size = jnp.abs(speed)
        return jnp.where(size >= bound, size, speed * speed * curve + floor)

    slow = 0.5 * fixed(along - sound) * (press_part - speed_part)
    fast = 0.5 * fixed(along + sound) * (press_part + speed_part)
    middle = fixed(along)
    entropy = middle * (jump_dens - press_part)
    both = slow + fast
    total = both + entropy
    push = sound * (fast - slow)
    shear = middle * dens_roe
    mass_low = low.dens * low.vel[normal]
    mass_high = high.dens * high.vel[normal]
    out = [mass_low + mass_high - total]
    work = None
    for part in range(3):
        value = mass_low * low.vel[part] + mass_high * high.vel[part] - vel[part] * total
        if part == normal:
            value = value + (low.pres + high.pres) - push - (2.0 * viscosity) * jump_along
        else:
            value = value - (shear + 2.0 * viscosity) * jump[part]
            term = vel[part] * jump[part]
            work = term if work is None else work + term
        out.append(value)
    lost = enth * both + along * push + entropy * half_sq + shear * work
    out.append(mass_low * low.enth + mass_high * high.enth - lost - (high.heat - low.heat))
    return out


def span_change(cells):
    row = row_ids()
    faces = roe_flux(cells, cells.map(lambda part: pltpu.roll(part, rows - 1, 0)), 2)
    w = cells.vel[2]
    sound_sq = (gamma_gas - 1.0) * (cells.enth - 0.5 * (cells.vel[0] * cells.vel[0] + cells.vel[1] * cells.vel[1]))
    sound = sound_sq * lax.rsqrt(sound_sq)
    still = 2.0 * (cells.dens * w * w + cells.pres)
    moving = 2.0 * w * (sound * cells.dens + 2.0 * viscosity)
    changes = []
    for part in range(5):
        top = still + moving if part == 3 else 0.0
        bottom = still - moving if part == 3 else 0.0
        upper = jnp.where(row == rows - 1, top, faces[part])
        lower = jnp.where(row == 0, bottom, pltpu.roll(faces[part], 1, 0))
        changes.append(upper - lower)
    return changes


def over_instances(values):
    weights = [weight_of(distance) for distance in range(inst_count)]
    across = turn(values, 2 * chunk)
    return (weights[0] * values + weights[2] * across) + turn(weights[1] * values + weights[3] * across, chunk)


def put(ref, place, cells):
    for number, part in enumerate(cells.parts):
        ref[place, number] = part


def get(ref, place):
    return Cells([ref[place, number] for number in range(fields_kept)])


class Pitch:
    def __init__(self, above, below, edge_faces):
        self.above, self.below, self.edge_faces = above, below, edge_faces
        self.lag = inst_count // 4
        me = lax.axis_index("inst")
        lane = lane_ids()
        self.slot = jnp.bitwise_and(lane, 3)
        self.band = band_ids()
        column = jnp.bitwise_and(lane, chunk - 1)
        self.is_first, self.is_last = column == 0, column == chunk - 1
        self.seam = self.slot == jnp.where(me == 0, 1, jnp.where(me == inst_count - 1, 3, -1))
        start = group_ids() * chunk
        ahead = chunk * self.lag
        low_seam, high_seam = me == 0, me == inst_count - 1
        self.to_main = start + jnp.where(self.is_first, jnp.where(low_seam, 1 - ahead, 1), 3)
        self.from_main = mod_lanes(start + jnp.where(self.slot == 1, jnp.where(low_seam, ahead, 0), chunk - 1))
        self.beside = mod_lanes(lane + jnp.where(self.slot == 3, jnp.where(high_seam, ahead - 1, -1), 1))

    def mains(self, ref, places):
        out = [None] * 5
        for layer, place in places:
            for number in range(5):
                got = pick_lanes(ref[place, number], self.from_main)
                out[number] = got if out[number] is None else jnp.where(self.band == layer + 1, got, out[number])
        return out

    def edges(self, cells, mains):
        slot = self.slot
        lower = Cells([jnp.where(slot == 3, b, a) for a, b in zip(cells.base, mains)])
        upper = []
        for a, b in zip(cells.base, mains):
            value = jnp.where(slot == 1, b, pick_lanes(a, self.beside))
            upper.append(jnp.where(self.seam, pick_rows(value, self.above), value))
        faces = roe_flux(lower, Cells(upper), 1)
        moved = [pick_rows(face, self.below) for face in faces]
        at_low = jnp.logical_and(self.seam, slot == 1)
        for part in range(5):
            self.edge_faces[part] = jnp.where(at_low, moved[part], faces[part])
        return faces, moved

    def as_upper(self, face, moved):
        return jnp.where(self.seam, turn(moved, chunk * self.lag), face)

    def change(self, cells, layer):
        faces = roe_flux(cells, cells.map(lambda part: turn(part, -1)), 1)
        index = mod_lanes((layer + 1) * 4 + self.to_main + lanes)
        changes = []
        for part in range(5):
            edge = pick_lanes(self.edge_faces[part], index)
            upper = jnp.where(self.is_last, edge, faces[part])
            lower = jnp.where(self.is_first, edge, turn(faces[part], 1))
            changes.append(upper - lower)
        return changes


def index_kernel(match, behind, above, below):
    row = row_ids()
    below_of = jnp.zeros(tile, jnp.int32)
    above_of = jnp.zeros(tile, jnp.int32)
    for k in range(rows):
        value = match[k]
        below_of = jnp.where(row == k, value, below_of)
        above_of = jnp.where(row == value, k, above_of)
    below[...], above[...] = below_of, above_of


def inner_kernel(above, below, main, halo, first, edge_first, part_first, part_edge, second, part_second, edge_faces):
    pitch = Pitch(above[...], below[...], edge_faces)
    slot = pitch.slot
    middle = range(1, layers - 1)
    for layer in range(layers):
        put(first, layer, cells_of_draws([main[field, layer] for field in range(5)]))
    cells = cells_of_draws([halo[field] for field in range(5)])
    for number, part in enumerate(cells.parts):
        edge_first[number] = part
    faces, moved = pitch.edges(cells, pitch.mains(first, [(layer, layer) for layer in range(layers)]))
    span = span_change(cells)
    axial = roe_flux(cells, cells.map(lambda part: turn(part, -4)), 0)
    state = cells.conserved()
    for part in range(5):
        lower_use = pitch.as_upper(faces[part], moved[part])
        along = jnp.where(slot == 1, faces[part] - turn(faces[part], 1), faces[part] - turn(lower_use, -1))
        value = over_instances(state[part]) + 0.5 * (along + span[part])
        part_edge[part] = value
        value = value + 0.5 * (axial[part] - turn(axial[part], 4))
        state[part] = state[part] - pseudo_step * value
    edge_second = cells_of_conserved(state)

    def step(layer, below_faces):
        cells = get(first, layer)
        above_faces = roe_flux(cells, get(first, jnp.minimum(layer + 1, layers - 1)), 0)
        span = span_change(cells)
        along = pitch.change(cells, layer)
        state = cells.conserved()
        outs = []
        for part in range(5):
            upper = jnp.where(layer == layers - 1, 0.0, above_faces[part])
            part_first[layer, part] = over_instances(state[part]) + 0.5 * (
                (upper - below_faces[part]) + span[part] + along[part]
            )
            outs.append(upper)
        return tuple(outs)

    lax.fori_loop(0, layers, step, (jnp.zeros(tile, jnp.float32),) * 5)

    for place, layer in enumerate(middle):
        state = get(first, layer).conserved()
        state = [value - pseudo_step * part_first[layer, part] for part, value in enumerate(state)]
        put(second, place, cells_of_conserved(state))
    pitch.edges(edge_second, pitch.mains(second, [(layer, place) for place, layer in enumerate(middle)]))
    between = roe_flux(get(second, 0), get(second, 1), 0)
    for part in range(5):
        part_second[0, part] = between[part]
        part_second[1, part] = -between[part]

    def second_step(place, carry):
        cells = get(second, place)
        span = span_change(cells)
        along = pitch.change(cells, place + 1)
        state = cells.conserved()
        for part in range(5):
            value = part_second[place, part] + span[part] + along[part]
            part_second[place, part] = over_instances(state[part]) + 0.5 * value
        return carry

    unrolled(layers - 2, second_step)


def side_values(high, closed, near, shared, scratch):
    first, edge_first, part_first, part_edge, second_middle, part_second, above, below, halo = shared
    ends, second, edge_faces = scratch
    pitch = Pitch(above[...], below[...], edge_faces)
    is_high = high == 1
    own = high * (layers - 1)
    outer_band = high * (layers + 1)

    own_cells = get(first, own)
    put(ends, 2 - 2 * high, own_cells)
    put(second, 2 - 2 * high, get(second_middle, high))
    for place, part in ((2 * high, high), (1, 1 - high)):
        cells = cells_of_draws([near[2 * field + part] for field in range(5)])
        if closed is not None:
            cells = Cells([jnp.where(closed, a, b) for a, b in zip(own_cells.parts, cells.parts)])
        put(ends, place, cells)
    outside = []
    for field in range(5):
        value = turn(near[10], mod_lanes(4 * (outer_band - field) + lanes))
        outside.append(value if closed is None else jnp.where(closed, halo[field], value))
    outside = cells_of_draws(outside).parts
    in_outer = pitch.band == outer_band
    edge_cells = Cells([jnp.where(in_outer, part, edge_first[number]) for number, part in enumerate(outside)])
    pitch.edges(edge_cells, pitch.mains(ends, [(0, 1)]))
    axial = roe_flux(edge_cells, edge_cells.map(lambda part: turn(part, -4)), 0)
    state = edge_cells.conserved()
    for part in range(5):
        value = part_edge[part] + 0.5 * (axial[part] - turn(axial[part], 4))
        state[part] = state[part] - pseudo_step * value
    edge_second = cells_of_conserved(state)

    def middle_values(ref, layer):
        cells = get(ref, 1)
        lower = roe_flux(get(ref, 0), cells, 0)
        upper = roe_flux(cells, get(ref, 2), 0)
        span = span_change(cells)
        along = pitch.change(cells, layer)
        state = cells.conserved()
        values, inward = [], []
        for part in range(5):
            value = (upper[part] - lower[part]) + span[part] + along[part]
            values.append(over_instances(state[part]) + 0.5 * value)
            inward.append(0.5 * jnp.where(is_high, lower[part], -upper[part]))
        return state, values, inward

    state, values, inward = middle_values(ends, outer_band - 1)
    beyond = cells_of_conserved([a - pseudo_step * b for a, b in zip(state, values)])
    state = own_cells.conserved()
    state = [a - pseudo_step * (part_first[own, part] + inward[part]) for part, a in enumerate(state)]
    own_second = cells_of_conserved(state)
    if closed is not None:
        beyond = Cells([jnp.where(closed, a, b) for a, b in zip(own_second.parts, beyond.parts)])
    put(second, 1, own_second)
    put(second, 2 * high, beyond)
    pitch.edges(edge_second, pitch.mains(second, [(0, 1)]))
    _, values, inward = middle_values(second, own)
    return values, [part_second[high, part] + inward[part] for part in range(5)]


def near_side_kernel(near, *refs):
    shared, out, scratch = refs[:9], refs[9], refs[10:]
    high = 1 - jnp.bitwise_and(lax.axis_index("space"), 1)
    for place, values in enumerate(side_values(high, None, near, shared, scratch)):
        for part in range(5):
            out[place, part] = values[part]


def far_side_kernel(near, other, *refs):
    shared, messages, scratch = refs[:9], in_order(refs[9:13]), refs[13:]
    where_on = lax.axis_index("space")
    high = jnp.bitwise_and(where_on, 1)
    closed = jnp.logical_or(where_on == 0, where_on == lax.axis_size("space") - 1)
    end, inner = side_values(high, closed, near, shared, scratch)
    me = lax.axis_index("inst")
    is_high = high == 1
    for field in range(5):
        low_side = [jnp.where(is_high, other[place, field], mine[field]) for place, mine in ((0, end), (1, inner))]
        high_side = [jnp.where(is_high, mine[field], other[place, field]) for place, mine in ((1, inner), (0, end))]
        for distance, values in enumerate(by_distance(turn_groups(low_side + high_side), me)):
            messages[distance][field] = values


def return_kernel(*refs):
    received, out = in_order(refs[:4]), refs[4]
    me = lax.axis_index("inst")

    def one_field(field, carry):
        for layer, values in enumerate(spread_tiles(received, field, me)):
            out[0, field, layer] = values
        return carry

    unrolled(5, one_field)


def call(kernel, outs, operands, scratch=(), scalars=0):
    shapes = [jax.ShapeDtypeStruct(shape, kind) for shape, kind in outs]
    return pl.pallas_call(
        kernel,
        out_shape=shapes,
        in_specs=[smem] * scalars + [vmem] * (len(operands) - scalars),
        out_specs=[vmem] * len(shapes),
        scratch_shapes=[pltpu.VMEM(shape, jnp.float32) for shape in scratch],
        compiler_params=pltpu.CompilerParams(vmem_limit_bytes=16 * 2**20),
    )(*operands)


def floats(*shape):
    return shape + tile, jnp.float32


def swap_instances(messages):
    got = []
    for distance, message in zip(order, messages):
        route = [(i, i ^ distance) for i in range(inst_count)]
        got.append(lax.ppermute(message, "inst", route) if distance else message)
    return got


def on_device_fast(flow_state, period_match):
    count = lax.axis_size("space")
    messages = call(pack_kernel, [floats(6)] * inst_count, [flow_state])
    integers = (tile, jnp.int32)
    above, below = call(index_kernel, [integers, integers], [period_match, messages[-1]], scalars=1)
    near_a, near_b, main, halo = call(
        unpack_kernel, [floats(11), floats(11), floats(5, layers), floats(5)], [*swap_instances(messages), above]
    )
    route_a = [(i, i ^ 1) for i in range(count)]
    route_b = []
    for n in range(inst_count):
        for i in range(count):
            far = (n, ((i - 1) ^ 1) + 1) if 0 < i < count - 1 else (n ^ 1, i)
            route_b.append((n * count + i, far[0] * count + far[1]))
    near_a = lax.ppermute(near_a, "space", route_a)
    near_b = lax.ppermute(near_b, ("inst", "space"), route_b)
    inner = call(
        inner_kernel,
        [
            floats(layers, fields_kept),
            floats(fields_kept),
            floats(layers, 5),
            floats(5),
            floats(layers - 2, fields_kept),
            floats(layers - 2, 5),
        ],
        [above, below, main, halo],
        [(5,) + tile],
    )
    shared = [*inner, above, below, halo]
    scratch = [(3, fields_kept) + tile, (3, fields_kept) + tile, (5,) + tile]
    (other,) = call(near_side_kernel, [floats(2, 5)], [near_a, *shared], scratch)
    results = call(far_side_kernel, [floats(5)] * inst_count, [near_b, other, *shared], scratch)
    return call(return_kernel, [(flow_state.shape, jnp.float32)], swap_instances(results))[0]


def solution(mesh):
    in_specs = (P(("groups", "inst"), None, "space", None, None), P())
    out_specs = P(("groups", "inst"), None, "space", None, None)

    def whole(flow_state, period_match):
        block = (flow_state.shape[2] // mesh.shape["space"],) + flow_state.shape[3:]
        fits = mesh.shape["inst"] == inst_count and mesh.shape["space"] % 2 == 0
        body = on_device_fast if fits and block == (layers, rows, lanes) else on_device
        return jax.shard_map(body, mesh=mesh, in_specs=in_specs, out_specs=out_specs, check_vma=False)(
            flow_state, period_match
        )

    return whole
```

```python
import math

import jax
import jax.numpy as jnp
from jax import lax
from jax.experimental import pallas as pl
from jax.experimental.pallas import tpu as pltpu
from jax.sharding import PartitionSpec as P

gamma_gas = 1.4
prandtl = 0.72
viscosity = 0.1
pseudo_step = 0.03
entropy_share = 0.1


def from_behind(block, axis, distance):
    devices = range(lax.axis_size(axis))
    route = [((i - distance) % len(devices), i) for i in devices]
    return lax.ppermute(block, axis, route)


def extended(cells, sides, width):
    for axis, dim in sides:
        count = lax.axis_size(axis)
        ends = count - 1
        head = lax.slice_in_dim(cells, 0, width, axis=dim)
        tail = lax.slice_in_dim(cells, cells.shape[dim] - width, cells.shape[dim], axis=dim)
        cells = jnp.concatenate(
            [
                lax.ppermute(tail, axis, [(i, (i + 1) % count) for i in range(ends)]),
                cells,
                lax.ppermute(head, axis, [((i + 1) % count, i) for i in range(ends)]),
            ],
            axis=dim,
        )
    return cells


def from_draw(draws):
    shape = (5,) + (1,) * (draws.ndim - 1)
    offsets = jnp.array([1.0, 0.8, 0.0, 0.0, 0.8], jnp.float32).reshape(shape)
    spreads = jnp.array([0.3, 0.3, 0.3, 0.3, 0.2], jnp.float32).reshape(shape)
    return offsets + spreads * draws


def conserved(primitives):
    dens = primitives[0]
    velocity = primitives[1:4]
    kinetic = 0.5 * dens * jnp.sum(velocity * velocity, axis=0)
    energy = primitives[4] / (gamma_gas - 1.0) + kinetic
    return jnp.concatenate([dens[None], dens[None] * velocity, energy[None]], axis=0)


def primitive(conserved_vars):
    dens = conserved_vars[0]
    velocity = conserved_vars[1:4] / dens
    pressure = (gamma_gas - 1.0) * (
        conserved_vars[4] - 0.5 * dens * jnp.sum(velocity * velocity, axis=0)
    )
    return jnp.concatenate([dens[None], velocity, pressure[None]], axis=0)


def entropy_fix(eigen_val, sound_speed):
    spread = entropy_share * sound_speed
    magnitude = jnp.abs(eigen_val)
    return jnp.where(
        magnitude >= spread, magnitude, (eigen_val * eigen_val + spread * spread) / (2.0 * spread)
    )


def euler_flux(dens, velocity, pressure, enthalpy, normal):
    normal_vel = velocity[normal]
    values = [dens * normal_vel]
    for component in range(3):
        moment = dens * velocity[component] * normal_vel
        if component == normal:
            moment = moment + pressure
        values.append(moment)
    values.append(dens * enthalpy * normal_vel)
    return values


def face_flux(left_cells, right_cells, normal):
    dens_left, vel_left, pres_left = (left_cells[0], left_cells[1:4], left_cells[4])
    dens_right, vel_right, pres_right = (right_cells[0], right_cells[1:4], right_cells[4])
    ratio = gamma_gas / (gamma_gas - 1.0)
    sq_left = jnp.sum(vel_left * vel_left, axis=0)
    sq_right = jnp.sum(vel_right * vel_right, axis=0)
    enth_left = ratio * pres_left / dens_left + 0.5 * sq_left
    enth_right = ratio * pres_right / dens_right + 0.5 * sq_right
    flux_left = euler_flux(dens_left, vel_left, pres_left, enth_left, normal)
    flux_right = euler_flux(dens_right, vel_right, pres_right, enth_right, normal)
    root_left = jnp.sqrt(dens_left)
    root_right = jnp.sqrt(dens_right)
    root_sum = root_left + root_right
    vel_roe = (root_left * vel_left + root_right * vel_right) / root_sum
    enth_roe = (root_left * enth_left + root_right * enth_right) / root_sum
    speed_sq = jnp.sum(vel_roe * vel_roe, axis=0)
    sound_sq = (gamma_gas - 1.0) * (enth_roe - 0.5 * speed_sq)
    sound_speed = jnp.sqrt(sound_sq)
    normal_vel = vel_roe[normal]
    dens_roe = root_left * root_right
    jump_dens = dens_right - dens_left
    jump_pres = pres_right - pres_left
    jump_vel = vel_right - vel_left
    jump_normal = jump_vel[normal]
    wave_slow = (jump_pres - dens_roe * sound_speed * jump_normal) / (2.0 * sound_sq)
    wave_fast = (jump_pres + dens_roe * sound_speed * jump_normal) / (2.0 * sound_sq)
    wave_mid = jump_dens - jump_pres / sound_sq
    eigen_mid = entropy_fix(normal_vel, sound_speed)
    flux_slow = entropy_fix(normal_vel - sound_speed, sound_speed) * wave_slow
    flux_fast = entropy_fix(normal_vel + sound_speed, sound_speed) * wave_fast
    dissipation = [flux_slow + eigen_mid * wave_mid + flux_fast]
    for component in range(3):
        unit_dir = 1.0 if component == normal else 0.0
        term = flux_slow * (vel_roe[component] - unit_dir * sound_speed)
        term = term + eigen_mid * (
            wave_mid * vel_roe[component]
            + dens_roe * (jump_vel[component] - unit_dir * jump_normal)
        )
        term = term + flux_fast * (vel_roe[component] + unit_dir * sound_speed)
        dissipation.append(term)
    shear_work = jnp.sum(vel_roe * jump_vel, axis=0) - normal_vel * jump_normal
    energy_term = flux_slow * (enth_roe - normal_vel * sound_speed)
    energy_term = energy_term + eigen_mid * (wave_mid * 0.5 * speed_sq + dens_roe * shear_work)
    energy_term = energy_term + flux_fast * (enth_roe + normal_vel * sound_speed)
    dissipation.append(energy_term)
    jump_temp = pres_right / dens_right - pres_left / dens_left
    jump_kin = 0.5 * (sq_right - sq_left)
    viscous_terms = [
        jnp.zeros_like(jump_dens),
        jump_vel[0],
        jump_vel[1],
        jump_vel[2],
        jump_kin + gamma_gas / ((gamma_gas - 1.0) * prandtl) * jump_temp,
    ]
    values = []
    for component in range(5):
        values.append(
            0.5 * (flux_left[component] + flux_right[component])
            - 0.5 * dissipation[component]
            - viscosity * viscous_terms[component]
        )
    return jnp.stack(values, axis=0)


def flux_change(padded, along, normal):
    length = padded.shape[along]
    face_values = face_flux(
        lax.slice_in_dim(padded, 0, length - 1, axis=along),
        lax.slice_in_dim(padded, 1, length, axis=along),
        normal,
    )
    return lax.slice_in_dim(face_values, 1, length - 1, axis=along) - lax.slice_in_dim(
        face_values, 0, length - 2, axis=along
    )


def spectral_entry(offset, number):
    wrapped = jnp.mod(offset, number)
    parity = 1.0 - 2.0 * jnp.mod(wrapped, 2).astype(jnp.float32)
    angles = math.pi * wrapped.astype(jnp.float32) / number
    sine_val = jnp.where(wrapped == 0, 1.0, jnp.sin(angles))
    derivative = jnp.where(
        wrapped == 0, 0.0, math.pi / number * parity * jnp.cos(angles) / sine_val
    )
    return derivative + 0.5 * parity


def on_device(flow_state, period_match):
    instances = lax.axis_size("inst")
    phase_lag = instances // 4
    instance = lax.axis_index("inst")
    space_parts = lax.axis_size("space")
    position = lax.axis_index("space")
    labels = jnp.arange(period_match.shape[0], dtype=jnp.int32)
    matches = (period_match[:, None] == labels[None, :]).astype(jnp.int32)
    inverse = jnp.sum(labels[:, None] * matches, axis=0)
    mirror = jnp.array([1.0, 1.0, 1.0, -1.0, 1.0], jnp.float32).reshape(5, 1, 1, 1)

    def lagged(plane, steps):
        return from_behind(plane, "inst", steps)

    def timewise(conserved_vars):
        pieces = lax.all_gather(conserved_vars[None], "inst", axis=0, tiled=True)
        number = pieces.shape[0]
        others = jnp.arange(number, dtype=jnp.int32)
        weights = spectral_entry(instance - others, instances)
        return jnp.tensordot(weights, pieces, axes=1, precision=lax.Precision.HIGHEST)

    def evaluate(conserved_vars):
        prims = primitive(conserved_vars)
        padded = extended(prims, (("space", 1),), 1)
        lower_edge = jnp.where(position == 0, prims[:, :1], padded[:, :1])
        upper_edge = jnp.where(position == space_parts - 1, prims[:, -1:], padded[:, -1:])
        along_axial = jnp.concatenate([lower_edge, prims, upper_edge], axis=1)
        along_span = jnp.concatenate(
            [prims[:, :, :1] * mirror, prims, prims[:, :, -1:] * mirror], axis=2
        )
        ghost_below = jnp.take(lagged(prims[..., -1], phase_lag), period_match, axis=2)
        ghost_above = jnp.take(lagged(prims[..., 0], -phase_lag), inverse, axis=2)
        along_pitch = jnp.concatenate(
            [ghost_below[..., None], prims, ghost_above[..., None]], axis=3
        )
        spatial = (
            flux_change(along_axial, 1, 0)
            + flux_change(along_span, 2, 2)
            + flux_change(along_pitch, 3, 1)
        )
        return timewise(conserved_vars) + spatial

    initial = conserved(from_draw(flow_state[0]))
    section_state = initial - pseudo_step * evaluate(initial)
    return evaluate(section_state)[None]


inst_count = 4
layers = 4
chunk = 32
rows = 16
lanes = 128
tile = (rows, lanes)
vmem = pl.BlockSpec(memory_space=pltpu.VMEM)
smem = pl.BlockSpec(memory_space=pltpu.SMEM)
starts = (1.0, 0.8, 0.0, 0.0, 0.8)
spreads_of = (0.3, 0.3, 0.3, 0.3, 0.2)
ratio = gamma_gas / (gamma_gas - 1.0)


def weight_of(distance):
    parity = 1.0 - 2.0 * (distance % 2)
    if distance == 0:
        return 0.5
    if 2 * distance == inst_count:
        return 0.5 * parity
    angle = math.pi * distance / inst_count
    return math.pi / inst_count * parity * math.cos(angle) / math.sin(angle) + 0.5 * parity


order = (2, 3, 1, 0)


def in_order(items):
    return [items[order.index(distance)] for distance in range(inst_count)]


def unrolled(count, body, carry=None):
    for number in range(count):
        carry = body(number, carry)
    return carry


def lane_ids():
    return lax.broadcasted_iota(jnp.int32, tile, 1)


def row_ids():
    return lax.broadcasted_iota(jnp.int32, tile, 0)


def band_ids():
    return jnp.bitwise_and(lane_ids() // 4, 7)


def pick_lanes(values, index):
    return jnp.take_along_axis(values, index, axis=1, mode="promise_in_bounds")


def pick_rows(values, index):
    half = rows // 2
    low, high = values[:half], values[half:]
    parts = []
    for part in (index[:half], index[half:]):
        inner = jnp.bitwise_and(part, half - 1)
        from_low = jnp.take_along_axis(low, inner, axis=0, mode="promise_in_bounds")
        from_high = jnp.take_along_axis(high, inner, axis=0, mode="promise_in_bounds")
        parts.append(jnp.where(part < half, from_low, from_high))
    return jnp.concatenate(parts, axis=0)


def turn(values, amount):
    return pltpu.roll(values, amount % lanes if isinstance(amount, int) else amount, 1)


def mod_lanes(amount):
    return jnp.bitwise_and(amount, lanes - 1)


def group_ids():
    return lane_ids() // chunk


class Groups:
    def __init__(self, me):
        group = group_ids()
        self.amounts = [chunk * (me + layer) for layer in range(layers)]
        self.masks = []
        for distance in range(inst_count):
            total = jnp.bitwise_xor(me, distance) + me
            self.masks.append([group == jnp.bitwise_and(total + layer, 3) for layer in range(layers)])

    def send(self, tiles):
        turned = [turn(values, mod_lanes(amount)) for values, amount in zip(tiles, self.amounts)]
        messages = []
        for masks in self.masks:
            out = turned[0]
            for layer in range(1, layers):
                out = jnp.where(masks[layer], turned[layer], out)
            messages.append(out)
        return messages

    def receive(self, messages):
        tiles = []
        for layer, amount in enumerate(self.amounts):
            out = messages[0]
            for distance in range(1, inst_count):
                out = jnp.where(self.masks[distance][layer], messages[distance], out)
            tiles.append(turn(out, mod_lanes(4 * lanes - amount)))
        return tiles


def pack_kernel(flow, *refs):
    messages = in_order(refs)
    me = lax.axis_index("inst")
    lane = lane_ids()
    place = lane // 4
    slot = jnp.bitwise_and(lane, 3)
    step = jnp.where(slot < 2, slot - 2, slot + chunk - 2)
    part_at = jnp.bitwise_and(place, 3)
    index = [mod_lanes(step + (chunk * jnp.bitwise_xor(part_at, layer) + lanes)) for layer in range(layers)]
    edges = [jnp.zeros(tile, jnp.float32)] * inst_count
    groups = Groups(me)
    for field in range(5):
        tiles = [flow[0, field, layer] for layer in range(layers)]
        for distance, values in enumerate(groups.send(tiles)):
            messages[distance][field] = values
        for layer in range(layers):
            got = pick_lanes(tiles[layer], index[layer])
            for distance in range(inst_count):
                here = place == field * 4 + jnp.bitwise_xor(me, distance ^ layer)
                edges[distance] = jnp.where(here, got, edges[distance])
    for distance in range(inst_count):
        messages[distance][5] = edges[distance]


def unpack_kernel(*refs):
    received, (near_a, near_b, main, halo) = in_order(refs[:4]), refs[5:]
    me = lax.axis_index("inst")
    even = jnp.bitwise_and(lax.axis_index("space"), 1) == 0
    lane = lane_ids()
    owner = group_ids()
    band = band_ids()
    level = jnp.clip(band - 1, 0, layers - 1)
    inner = jnp.bitwise_xor(level, me) * 4 + jnp.bitwise_and(lane, 3)
    up_edge = down_edge = jnp.zeros(tile, jnp.float32)
    groups = Groups(me)
    for field in range(5):
        tiles = groups.receive([message[field] for message in received])
        for layer in range(layers):
            main[field, layer] = tiles[layer]
        for place in range(2):
            near_a[2 * field + place] = jnp.where(even, tiles[2 + place], tiles[place])
            near_b[2 * field + place] = jnp.where(even, tiles[place], tiles[2 + place])
        edges = None
        for distance in range(inst_count):
            got = pick_lanes(received[distance][5], inner + 16 * field)
            edges = got if edges is None else jnp.where(owner == jnp.bitwise_xor(me, distance), got, edges)
        halo[field] = edges
        up_edge = jnp.where(band == field, turn(edges, 4 * (field - layers)), up_edge)
        down_edge = jnp.where(band == field, turn(edges, 4 * (field - 1)), down_edge)
    near_a[10] = jnp.where(even, up_edge, down_edge)
    near_b[10] = jnp.where(even, down_edge, up_edge)


class Cells:
    def __init__(self, parts):
        self.parts = list(parts)
        self.root, self.vel, self.temp = parts[0], list(parts[1:4]), parts[4]
        if len(parts) == 5:
            dens = self.root * self.root
            kinetic = 0.5 * (self.vel[0] * self.vel[0] + self.vel[1] * self.vel[1] + self.vel[2] * self.vel[2])
            enth = ratio * self.temp + kinetic
            heat = 2.0 * viscosity * (kinetic + ratio / prandtl * self.temp)
            self.parts += [dens, dens * self.temp, enth, heat]
        self.dens, self.pres, self.enth, self.heat = self.parts[5:]
        self.base = self.parts[:5]

    def map(self, change):
        return Cells([change(part) for part in self.base])

    def conserved(self):
        dens, enth = self.dens, self.enth
        return [dens] + [dens * part for part in self.vel] + [dens * enth - self.pres]


fields_kept = 9


def cells_of(dens, vel, pres):
    inverse_root = lax.rsqrt(dens)
    return Cells([dens * inverse_root] + list(vel) + [pres * (inverse_root * inverse_root)])


def cells_of_draws(draws):
    start = [base + spread * draw if base else spread * draw for base, spread, draw in zip(starts, spreads_of, draws)]
    return cells_of(start[0], start[1:4], start[4])


def cells_of_conserved(state):
    dens = state[0]
    inverse_root = lax.rsqrt(dens)
    inverse = inverse_root * inverse_root
    vel = [part * inverse for part in state[1:4]]
    kinetic = 0.5 * (vel[0] * vel[0] + vel[1] * vel[1] + vel[2] * vel[2])
    return Cells([dens * inverse_root] + vel + [(gamma_gas - 1.0) * (state[4] * inverse - kinetic)])


def roe_flux(low, high, normal):
    jump_dens = high.dens - low.dens
    jump_pres = high.pres - low.pres
    jump = [b - a for a, b in zip(low.vel, high.vel)]
    share = high.root / (low.root + high.root)
    vel = [a + share * d for a, d in zip(low.vel, jump)]
    enth = low.enth + share * (high.enth - low.enth)
    half_sq = 0.5 * (vel[0] * vel[0] + vel[1] * vel[1] + vel[2] * vel[2])
    sound_sq = (gamma_gas - 1.0) * (enth - half_sq)
    inverse = lax.rsqrt(sound_sq)
    sound = sound_sq * inverse
    dens_roe = low.root * high.root
    along = vel[normal]
    jump_along = jump[normal]
    press_part = jump_pres * (inverse * inverse)
    speed_part = dens_roe * inverse * jump_along
    bound = entropy_share * sound
    curve = (0.5 / entropy_share) * inverse
    floor = 0.5 * bound

    def fixed(speed):
        size = jnp.abs(speed)
        return jnp.where(size >= bound, size, speed * speed * curve + floor)

    slow = 0.5 * fixed(along - sound) * (press_part - speed_part)
    fast = 0.5 * fixed(along + sound) * (press_part + speed_part)
    middle = fixed(along)
    entropy = middle * (jump_dens - press_part)
    both = slow + fast
    total = both + entropy
    push = sound * (fast - slow)
    shear = middle * dens_roe
    mass_low = low.dens * low.vel[normal]
    mass_high = high.dens * high.vel[normal]
    out = [mass_low + mass_high - total]
    work = None
    for part in range(3):
        value = mass_low * low.vel[part] + mass_high * high.vel[part] - vel[part] * total
        if part == normal:
            value = value + (low.pres + high.pres) - push - (2.0 * viscosity) * jump_along
        else:
            value = value - (shear + 2.0 * viscosity) * jump[part]
            term = vel[part] * jump[part]
            work = term if work is None else work + term
        out.append(value)
    lost = enth * both + along * push + entropy * half_sq + shear * work
    out.append(mass_low * low.enth + mass_high * high.enth - lost - (high.heat - low.heat))
    return out


def span_change(cells):
    row = row_ids()
    faces = roe_flux(cells, cells.map(lambda part: pltpu.roll(part, rows - 1, 0)), 2)
    w = cells.vel[2]
    sound_sq = (gamma_gas - 1.0) * (cells.enth - 0.5 * (cells.vel[0] * cells.vel[0] + cells.vel[1] * cells.vel[1]))
    sound = sound_sq * lax.rsqrt(sound_sq)
    still = 2.0 * (cells.dens * w * w + cells.pres)
    moving = 2.0 * w * (sound * cells.dens + 2.0 * viscosity)
    changes = []
    for part in range(5):
        top = still + moving if part == 3 else 0.0
        bottom = still - moving if part == 3 else 0.0
        upper = jnp.where(row == rows - 1, top, faces[part])
        lower = jnp.where(row == 0, bottom, pltpu.roll(faces[part], 1, 0))
        changes.append(upper - lower)
    return changes


def over_instances(values):
    weights = [weight_of(distance) for distance in range(inst_count)]
    across = turn(values, 2 * chunk)
    return (weights[0] * values + weights[2] * across) + turn(weights[1] * values + weights[3] * across, chunk)


def put(ref, place, cells):
    for number, part in enumerate(cells.parts):
        ref[place, number] = part


def get(ref, place):
    return Cells([ref[place, number] for number in range(fields_kept)])


class Pitch:
    def __init__(self, above, below, edge_faces):
        self.above, self.below, self.edge_faces = above, below, edge_faces
        self.lag = inst_count // 4
        me = lax.axis_index("inst")
        lane = lane_ids()
        self.slot = jnp.bitwise_and(lane, 3)
        self.band = band_ids()
        column = jnp.bitwise_and(lane, chunk - 1)
        self.is_first, self.is_last = column == 0, column == chunk - 1
        self.seam = self.slot == jnp.where(me == 0, 1, jnp.where(me == inst_count - 1, 3, -1))
        start = group_ids() * chunk
        ahead = chunk * self.lag
        low_seam, high_seam = me == 0, me == inst_count - 1
        self.to_main = start + jnp.where(self.is_first, jnp.where(low_seam, 1 - ahead, 1), 3)
        self.from_main = mod_lanes(start + jnp.where(self.slot == 1, jnp.where(low_seam, ahead, 0), chunk - 1))
        self.beside = mod_lanes(lane + jnp.where(self.slot == 3, jnp.where(high_seam, ahead - 1, -1), 1))

    def mains(self, ref, places):
        out = [None] * 5
        for layer, place in places:
            for number in range(5):
                got = pick_lanes(ref[place, number], self.from_main)
                out[number] = got if out[number] is None else jnp.where(self.band == layer + 1, got, out[number])
        return out

    def edges(self, cells, mains):
        slot = self.slot
        lower = Cells([jnp.where(slot == 3, b, a) for a, b in zip(cells.base, mains)])
        upper = []
        for a, b in zip(cells.base, mains):
            value = jnp.where(slot == 1, b, pick_lanes(a, self.beside))
            upper.append(jnp.where(self.seam, pick_rows(value, self.above), value))
        faces = roe_flux(lower, Cells(upper), 1)
        moved = [pick_rows(face, self.below) for face in faces]
        at_low = jnp.logical_and(self.seam, slot == 1)
        for part in range(5):
            self.edge_faces[part] = jnp.where(at_low, moved[part], faces[part])
        return faces, moved

    def as_upper(self, face, moved):
        return jnp.where(self.seam, turn(moved, chunk * self.lag), face)

    def change(self, cells, layer):
        faces = roe_flux(cells, cells.map(lambda part: turn(part, -1)), 1)
        index = mod_lanes((layer + 1) * 4 + self.to_main + lanes)
        changes = []
        for part in range(5):
            edge = pick_lanes(self.edge_faces[part], index)
            upper = jnp.where(self.is_last, edge, faces[part])
            lower = jnp.where(self.is_first, edge, turn(faces[part], 1))
            changes.append(upper - lower)
        return changes


def index_kernel(match, behind, above, below):
    row = row_ids()
    below_of = jnp.zeros(tile, jnp.int32)
    above_of = jnp.zeros(tile, jnp.int32)
    for k in range(rows):
        value = match[k]
        below_of = jnp.where(row == k, value, below_of)
        above_of = jnp.where(row == value, k, above_of)
    below[...], above[...] = below_of, above_of


def inner_kernel(above, below, main, halo, first, edge_first, part_first, part_edge, second, part_second, edge_faces):
    pitch = Pitch(above[...], below[...], edge_faces)
    slot = pitch.slot
    middle = range(1, layers - 1)
    for layer in range(layers):
        put(first, layer, cells_of_draws([main[field, layer] for field in range(5)]))
    cells = cells_of_draws([halo[field] for field in range(5)])
    for number, part in enumerate(cells.parts):
        edge_first[number] = part
    faces, moved = pitch.edges(cells, pitch.mains(first, [(layer, layer) for layer in range(layers)]))
    span = span_change(cells)
    axial = roe_flux(cells, cells.map(lambda part: turn(part, -4)), 0)
    state = cells.conserved()
    for part in range(5):
        lower_use = pitch.as_upper(faces[part], moved[part])
        along = jnp.where(slot == 1, faces[part] - turn(faces[part], 1), faces[part] - turn(lower_use, -1))
        value = over_instances(state[part]) + 0.5 * (along + span[part])
        part_edge[part] = value
        value = value + 0.5 * (axial[part] - turn(axial[part], 4))
        state[part] = state[part] - pseudo_step * value
    edge_second = cells_of_conserved(state)

    def step(layer, below_faces):
        cells = get(first, layer)
        above_faces = roe_flux(cells, get(first, jnp.minimum(layer + 1, layers - 1)), 0)
        span = span_change(cells)
        along = pitch.change(cells, layer)
        state = cells.conserved()
        outs = []
        for part in range(5):
            upper = jnp.where(layer == layers - 1, 0.0, above_faces[part])
            part_first[layer, part] = over_instances(state[part]) + 0.5 * (
                (upper - below_faces[part]) + span[part] + along[part]
            )
            outs.append(upper)
        return tuple(outs)

    lax.fori_loop(0, layers, step, (jnp.zeros(tile, jnp.float32),) * 5)

    for place, layer in enumerate(middle):
        state = get(first, layer).conserved()
        state = [value - pseudo_step * part_first[layer, part] for part, value in enumerate(state)]
        put(second, place, cells_of_conserved(state))
    pitch.edges(edge_second, pitch.mains(second, [(layer, place) for place, layer in enumerate(middle)]))
    between = roe_flux(get(second, 0), get(second, 1), 0)
    for part in range(5):
        part_second[0, part] = between[part]
        part_second[1, part] = -between[part]

    def second_step(place, carry):
        cells = get(second, place)
        span = span_change(cells)
        along = pitch.change(cells, place + 1)
        state = cells.conserved()
        for part in range(5):
            value = part_second[place, part] + span[part] + along[part]
            part_second[place, part] = over_instances(state[part]) + 0.5 * value
        return carry

    unrolled(layers - 2, second_step)


def side_values(high, closed, near, shared, scratch):
    first, edge_first, part_first, part_edge, second_middle, part_second, above, below, halo = shared
    ends, second, edge_faces = scratch
    pitch = Pitch(above[...], below[...], edge_faces)
    is_high = high == 1
    own = high * (layers - 1)
    outer_band = high * (layers + 1)

    own_cells = get(first, own)
    put(ends, 2 - 2 * high, own_cells)
    put(second, 2 - 2 * high, get(second_middle, high))
    for place, part in ((2 * high, high), (1, 1 - high)):
        cells = cells_of_draws([near[2 * field + part] for field in range(5)])
        if closed is not None:
            cells = Cells([jnp.where(closed, a, b) for a, b in zip(own_cells.parts, cells.parts)])
        put(ends, place, cells)
    outside = []
    for field in range(5):
        value = turn(near[10], mod_lanes(4 * (outer_band - field) + lanes))
        outside.append(value if closed is None else jnp.where(closed, halo[field], value))
    outside = cells_of_draws(outside).parts
    in_outer = pitch.band == outer_band
    edge_cells = Cells([jnp.where(in_outer, part, edge_first[number]) for number, part in enumerate(outside)])
    pitch.edges(edge_cells, pitch.mains(ends, [(0, 1)]))
    axial = roe_flux(edge_cells, edge_cells.map(lambda part: turn(part, -4)), 0)
    state = edge_cells.conserved()
    for part in range(5):
        value = part_edge[part] + 0.5 * (axial[part] - turn(axial[part], 4))
        state[part] = state[part] - pseudo_step * value
    edge_second = cells_of_conserved(state)

    def middle_values(ref, layer):
        cells = get(ref, 1)
        lower = roe_flux(get(ref, 0), cells, 0)
        upper = roe_flux(cells, get(ref, 2), 0)
        span = span_change(cells)
        along = pitch.change(cells, layer)
        state = cells.conserved()
        values, inward = [], []
        for part in range(5):
            value = (upper[part] - lower[part]) + span[part] + along[part]
            values.append(over_instances(state[part]) + 0.5 * value)
            inward.append(0.5 * jnp.where(is_high, lower[part], -upper[part]))
        return state, values, inward

    state, values, inward = middle_values(ends, outer_band - 1)
    beyond = cells_of_conserved([a - pseudo_step * b for a, b in zip(state, values)])
    state = own_cells.conserved()
    state = [a - pseudo_step * (part_first[own, part] + inward[part]) for part, a in enumerate(state)]
    own_second = cells_of_conserved(state)
    if closed is not None:
        beyond = Cells([jnp.where(closed, a, b) for a, b in zip(own_second.parts, beyond.parts)])
    put(second, 1, own_second)
    put(second, 2 * high, beyond)
    pitch.edges(edge_second, pitch.mains(second, [(0, 1)]))
    _, values, inward = middle_values(second, own)
    return values, [part_second[high, part] + inward[part] for part in range(5)]


def near_side_kernel(near, *refs):
    shared, out, scratch = refs[:9], refs[9], refs[10:]
    high = 1 - jnp.bitwise_and(lax.axis_index("space"), 1)
    for place, values in enumerate(side_values(high, None, near, shared, scratch)):
        for part in range(5):
            out[place, part] = values[part]


def far_side_kernel(near, other, *refs):
    shared, messages, scratch = refs[:9], in_order(refs[9:13]), refs[13:]
    where_on = lax.axis_index("space")
    high = jnp.bitwise_and(where_on, 1)
    closed = jnp.logical_or(where_on == 0, where_on == lax.axis_size("space") - 1)
    end, inner = side_values(high, closed, near, shared, scratch)
    groups = Groups(lax.axis_index("inst"))
    is_high = high == 1
    for field in range(5):
        low_side = [jnp.where(is_high, other[place, field], mine[field]) for place, mine in ((0, end), (1, inner))]
        high_side = [jnp.where(is_high, mine[field], other[place, field]) for place, mine in ((1, inner), (0, end))]
        for distance, values in enumerate(groups.send(low_side + high_side)):
            messages[distance][field] = values


def return_kernel(*refs):
    received, out = in_order(refs[:4]), refs[4]
    groups = Groups(lax.axis_index("inst"))
    for field in range(5):
        for layer, values in enumerate(groups.receive([message[field] for message in received])):
            out[0, field, layer] = values


def call(kernel, outs, operands, scratch=(), scalars=0):
    shapes = [jax.ShapeDtypeStruct(shape, kind) for shape, kind in outs]
    return pl.pallas_call(
        kernel,
        out_shape=shapes,
        in_specs=[smem] * scalars + [vmem] * (len(operands) - scalars),
        out_specs=[vmem] * len(shapes),
        scratch_shapes=[pltpu.VMEM(shape, jnp.float32) for shape in scratch],
        compiler_params=pltpu.CompilerParams(vmem_limit_bytes=16 * 2**20),
    )(*operands)


def floats(*shape):
    return shape + tile, jnp.float32


def swap_instances(messages):
    got = []
    for distance, message in zip(order, messages):
        route = [(i, i ^ distance) for i in range(inst_count)]
        got.append(lax.ppermute(message, "inst", route) if distance else message)
    return got


def on_device_fast(flow_state, period_match):
    count = lax.axis_size("space")
    messages = call(pack_kernel, [floats(6)] * inst_count, [flow_state])
    integers = (tile, jnp.int32)
    above, below = call(index_kernel, [integers, integers], [period_match, messages[-1]], scalars=1)
    near_a, near_b, main, halo = call(
        unpack_kernel, [floats(11), floats(11), floats(5, layers), floats(5)], [*swap_instances(messages), above]
    )
    route_a = [(i, i ^ 1) for i in range(count)]
    route_b = []
    for n in range(inst_count):
        for i in range(count):
            far = (n, ((i - 1) ^ 1) + 1) if 0 < i < count - 1 else (n ^ 1, i)
            route_b.append((n * count + i, far[0] * count + far[1]))
    near_a = lax.ppermute(near_a, "space", route_a)
    near_b = lax.ppermute(near_b, ("inst", "space"), route_b)
    inner = call(
        inner_kernel,
        [
            floats(layers, fields_kept),
            floats(fields_kept),
            floats(layers, 5),
            floats(5),
            floats(layers - 2, fields_kept),
            floats(layers - 2, 5),
        ],
        [above, below, main, halo],
        [(5,) + tile],
    )
    shared = [*inner, above, below, halo]
    scratch = [(3, fields_kept) + tile, (3, fields_kept) + tile, (5,) + tile]
    (other,) = call(near_side_kernel, [floats(2, 5)], [near_a, *shared], scratch)
    results = call(far_side_kernel, [floats(5)] * inst_count, [near_b, other, *shared], scratch)
    return call(return_kernel, [(flow_state.shape, jnp.float32)], swap_instances(results))[0]


def solution(mesh):
    in_specs = (P(("groups", "inst"), None, "space", None, None), P())
    out_specs = P(("groups", "inst"), None, "space", None, None)

    def whole(flow_state, period_match):
        block = (flow_state.shape[2] // mesh.shape["space"],) + flow_state.shape[3:]
        fits = mesh.shape["inst"] == inst_count and mesh.shape["space"] % 2 == 0
        body = on_device_fast if fits and block == (layers, rows, lanes) else on_device
        return jax.shard_map(body, mesh=mesh, in_specs=in_specs, out_specs=out_specs, check_vma=False)(
            flow_state, period_match
        )

    return whole
```

```python
import math

import jax
import jax.numpy as jnp
from jax import lax
from jax.experimental import pallas as pl
from jax.experimental.pallas import tpu as pltpu
from jax.sharding import PartitionSpec as P

gamma_gas = 1.4
prandtl = 0.72
viscosity = 0.1
pseudo_step = 0.03
entropy_share = 0.1


def from_behind(block, axis, distance):
    devices = range(lax.axis_size(axis))
    route = [((i - distance) % len(devices), i) for i in devices]
    return lax.ppermute(block, axis, route)


def extended(cells, sides, width):
    for axis, dim in sides:
        count = lax.axis_size(axis)
        ends = count - 1
        head = lax.slice_in_dim(cells, 0, width, axis=dim)
        tail = lax.slice_in_dim(cells, cells.shape[dim] - width, cells.shape[dim], axis=dim)
        cells = jnp.concatenate(
            [
                lax.ppermute(tail, axis, [(i, (i + 1) % count) for i in range(ends)]),
                cells,
                lax.ppermute(head, axis, [((i + 1) % count, i) for i in range(ends)]),
            ],
            axis=dim,
        )
    return cells


def from_draw(draws):
    shape = (5,) + (1,) * (draws.ndim - 1)
    offsets = jnp.array([1.0, 0.8, 0.0, 0.0, 0.8], jnp.float32).reshape(shape)
    spreads = jnp.array([0.3, 0.3, 0.3, 0.3, 0.2], jnp.float32).reshape(shape)
    return offsets + spreads * draws


def conserved(primitives):
    dens = primitives[0]
    velocity = primitives[1:4]
    kinetic = 0.5 * dens * jnp.sum(velocity * velocity, axis=0)
    energy = primitives[4] / (gamma_gas - 1.0) + kinetic
    return jnp.concatenate([dens[None], dens[None] * velocity, energy[None]], axis=0)


def primitive(conserved_vars):
    dens = conserved_vars[0]
    velocity = conserved_vars[1:4] / dens
    pressure = (gamma_gas - 1.0) * (
        conserved_vars[4] - 0.5 * dens * jnp.sum(velocity * velocity, axis=0)
    )
    return jnp.concatenate([dens[None], velocity, pressure[None]], axis=0)


def entropy_fix(eigen_val, sound_speed):
    spread = entropy_share * sound_speed
    magnitude = jnp.abs(eigen_val)
    return jnp.where(
        magnitude >= spread, magnitude, (eigen_val * eigen_val + spread * spread) / (2.0 * spread)
    )


def euler_flux(dens, velocity, pressure, enthalpy, normal):
    normal_vel = velocity[normal]
    values = [dens * normal_vel]
    for component in range(3):
        moment = dens * velocity[component] * normal_vel
        if component == normal:
            moment = moment + pressure
        values.append(moment)
    values.append(dens * enthalpy * normal_vel)
    return values


def face_flux(left_cells, right_cells, normal):
    dens_left, vel_left, pres_left = (left_cells[0], left_cells[1:4], left_cells[4])
    dens_right, vel_right, pres_right = (right_cells[0], right_cells[1:4], right_cells[4])
    ratio = gamma_gas / (gamma_gas - 1.0)
    sq_left = jnp.sum(vel_left * vel_left, axis=0)
    sq_right = jnp.sum(vel_right * vel_right, axis=0)
    enth_left = ratio * pres_left / dens_left + 0.5 * sq_left
    enth_right = ratio * pres_right / dens_right + 0.5 * sq_right
    flux_left = euler_flux(dens_left, vel_left, pres_left, enth_left, normal)
    flux_right = euler_flux(dens_right, vel_right, pres_right, enth_right, normal)
    root_left = jnp.sqrt(dens_left)
    root_right = jnp.sqrt(dens_right)
    root_sum = root_left + root_right
    vel_roe = (root_left * vel_left + root_right * vel_right) / root_sum
    enth_roe = (root_left * enth_left + root_right * enth_right) / root_sum
    speed_sq = jnp.sum(vel_roe * vel_roe, axis=0)
    sound_sq = (gamma_gas - 1.0) * (enth_roe - 0.5 * speed_sq)
    sound_speed = jnp.sqrt(sound_sq)
    normal_vel = vel_roe[normal]
    dens_roe = root_left * root_right
    jump_dens = dens_right - dens_left
    jump_pres = pres_right - pres_left
    jump_vel = vel_right - vel_left
    jump_normal = jump_vel[normal]
    wave_slow = (jump_pres - dens_roe * sound_speed * jump_normal) / (2.0 * sound_sq)
    wave_fast = (jump_pres + dens_roe * sound_speed * jump_normal) / (2.0 * sound_sq)
    wave_mid = jump_dens - jump_pres / sound_sq
    eigen_mid = entropy_fix(normal_vel, sound_speed)
    flux_slow = entropy_fix(normal_vel - sound_speed, sound_speed) * wave_slow
    flux_fast = entropy_fix(normal_vel + sound_speed, sound_speed) * wave_fast
    dissipation = [flux_slow + eigen_mid * wave_mid + flux_fast]
    for component in range(3):
        unit_dir = 1.0 if component == normal else 0.0
        term = flux_slow * (vel_roe[component] - unit_dir * sound_speed)
        term = term + eigen_mid * (
            wave_mid * vel_roe[component]
            + dens_roe * (jump_vel[component] - unit_dir * jump_normal)
        )
        term = term + flux_fast * (vel_roe[component] + unit_dir * sound_speed)
        dissipation.append(term)
    shear_work = jnp.sum(vel_roe * jump_vel, axis=0) - normal_vel * jump_normal
    energy_term = flux_slow * (enth_roe - normal_vel * sound_speed)
    energy_term = energy_term + eigen_mid * (wave_mid * 0.5 * speed_sq + dens_roe * shear_work)
    energy_term = energy_term + flux_fast * (enth_roe + normal_vel * sound_speed)
    dissipation.append(energy_term)
    jump_temp = pres_right / dens_right - pres_left / dens_left
    jump_kin = 0.5 * (sq_right - sq_left)
    viscous_terms = [
        jnp.zeros_like(jump_dens),
        jump_vel[0],
        jump_vel[1],
        jump_vel[2],
        jump_kin + gamma_gas / ((gamma_gas - 1.0) * prandtl) * jump_temp,
    ]
    values = []
    for component in range(5):
        values.append(
            0.5 * (flux_left[component] + flux_right[component])
            - 0.5 * dissipation[component]
            - viscosity * viscous_terms[component]
        )
    return jnp.stack(values, axis=0)


def flux_change(padded, along, normal):
    length = padded.shape[along]
    face_values = face_flux(
        lax.slice_in_dim(padded, 0, length - 1, axis=along),
        lax.slice_in_dim(padded, 1, length, axis=along),
        normal,
    )
    return lax.slice_in_dim(face_values, 1, length - 1, axis=along) - lax.slice_in_dim(
        face_values, 0, length - 2, axis=along
    )


def spectral_entry(offset, number):
    wrapped = jnp.mod(offset, number)
    parity = 1.0 - 2.0 * jnp.mod(wrapped, 2).astype(jnp.float32)
    angles = math.pi * wrapped.astype(jnp.float32) / number
    sine_val = jnp.where(wrapped == 0, 1.0, jnp.sin(angles))
    derivative = jnp.where(
        wrapped == 0, 0.0, math.pi / number * parity * jnp.cos(angles) / sine_val
    )
    return derivative + 0.5 * parity


def on_device(flow_state, period_match):
    instances = lax.axis_size("inst")
    phase_lag = instances // 4
    instance = lax.axis_index("inst")
    space_parts = lax.axis_size("space")
    position = lax.axis_index("space")
    labels = jnp.arange(period_match.shape[0], dtype=jnp.int32)
    matches = (period_match[:, None] == labels[None, :]).astype(jnp.int32)
    inverse = jnp.sum(labels[:, None] * matches, axis=0)
    mirror = jnp.array([1.0, 1.0, 1.0, -1.0, 1.0], jnp.float32).reshape(5, 1, 1, 1)

    def lagged(plane, steps):
        return from_behind(plane, "inst", steps)

    def timewise(conserved_vars):
        pieces = lax.all_gather(conserved_vars[None], "inst", axis=0, tiled=True)
        number = pieces.shape[0]
        others = jnp.arange(number, dtype=jnp.int32)
        weights = spectral_entry(instance - others, instances)
        return jnp.tensordot(weights, pieces, axes=1, precision=lax.Precision.HIGHEST)

    def evaluate(conserved_vars):
        prims = primitive(conserved_vars)
        padded = extended(prims, (("space", 1),), 1)
        lower_edge = jnp.where(position == 0, prims[:, :1], padded[:, :1])
        upper_edge = jnp.where(position == space_parts - 1, prims[:, -1:], padded[:, -1:])
        along_axial = jnp.concatenate([lower_edge, prims, upper_edge], axis=1)
        along_span = jnp.concatenate(
            [prims[:, :, :1] * mirror, prims, prims[:, :, -1:] * mirror], axis=2
        )
        ghost_below = jnp.take(lagged(prims[..., -1], phase_lag), period_match, axis=2)
        ghost_above = jnp.take(lagged(prims[..., 0], -phase_lag), inverse, axis=2)
        along_pitch = jnp.concatenate(
            [ghost_below[..., None], prims, ghost_above[..., None]], axis=3
        )
        spatial = (
            flux_change(along_axial, 1, 0)
            + flux_change(along_span, 2, 2)
            + flux_change(along_pitch, 3, 1)
        )
        return timewise(conserved_vars) + spatial

    initial = conserved(from_draw(flow_state[0]))
    section_state = initial - pseudo_step * evaluate(initial)
    return evaluate(section_state)[None]


inst_count = 4
layers = 4
chunk = 32
rows = 16
lanes = 128
tile = (rows, lanes)
vmem = pl.BlockSpec(memory_space=pltpu.VMEM)
smem = pl.BlockSpec(memory_space=pltpu.SMEM)
starts = (1.0, 0.8, 0.0, 0.0, 0.8)
spreads_of = (0.3, 0.3, 0.3, 0.3, 0.2)
ratio = gamma_gas / (gamma_gas - 1.0)


def weight_of(distance):
    parity = 1.0 - 2.0 * (distance % 2)
    if distance == 0:
        return 0.5
    if 2 * distance == inst_count:
        return 0.5 * parity
    angle = math.pi * distance / inst_count
    return math.pi / inst_count * parity * math.cos(angle) / math.sin(angle) + 0.5 * parity


order = (2, 3, 1, 0)
back = (3, 2, 1, 0)


def in_order(items, order=order):
    return [items[order.index(distance)] for distance in range(inst_count)]


def unrolled(count, body, carry=None):
    for number in range(count):
        carry = body(number, carry)
    return carry


def lane_ids():
    return lax.broadcasted_iota(jnp.int32, tile, 1)


def row_ids():
    return lax.broadcasted_iota(jnp.int32, tile, 0)


def band_ids():
    return jnp.bitwise_and(lane_ids() // 4, 7)


def pick_lanes(values, index):
    return jnp.take_along_axis(values, index, axis=1, mode="promise_in_bounds")


def pick_rows(values, index):
    half = rows // 2
    low, high = values[:half], values[half:]
    parts = []
    for part in (index[:half], index[half:]):
        inner = jnp.bitwise_and(part, half - 1)
        from_low = jnp.take_along_axis(low, inner, axis=0, mode="promise_in_bounds")
        from_high = jnp.take_along_axis(high, inner, axis=0, mode="promise_in_bounds")
        parts.append(jnp.where(part < half, from_low, from_high))
    return jnp.concatenate(parts, axis=0)


def turn(values, amount):
    return pltpu.roll(values, amount % lanes if isinstance(amount, int) else amount, 1)


def mod_lanes(amount):
    return jnp.bitwise_and(amount, lanes - 1)


def group_ids():
    return lane_ids() // chunk


class Groups:
    def __init__(self, me):
        group = group_ids()
        self.me = me
        self.amounts = [chunk * (me + layer) for layer in range(layers)]
        self.masks = []
        for distance in range(inst_count):
            total = jnp.bitwise_xor(me, distance) + me
            self.masks.append([group == jnp.bitwise_and(total + layer, 3) for layer in range(layers)])

    def send(self, tiles):
        return self.share([self.turned(values, layer) for layer, values in enumerate(tiles)])

    def turned(self, values, layer):
        return turn(values, mod_lanes(chunk * (self.me + layer)))

    def share(self, turned):
        messages = []
        for masks in self.masks:
            out = turned[0]
            for layer in range(1, layers):
                out = jnp.where(masks[layer], turned[layer], out)
            messages.append(out)
        return messages

    def receive(self, messages):
        tiles = []
        for layer, amount in enumerate(self.amounts):
            out = messages[0]
            for distance in range(1, inst_count):
                out = jnp.where(self.masks[distance][layer], messages[distance], out)
            tiles.append(turn(out, mod_lanes(4 * lanes - amount)))
        return tiles


def pack_kernel(flow, *refs):
    messages = in_order(refs)
    me = lax.axis_index("inst")
    lane = lane_ids()
    place = lane // 4
    slot = jnp.bitwise_and(lane, 3)
    step = jnp.where(slot < 2, slot - 2, slot + chunk - 2)
    part_at = jnp.bitwise_and(place, 3)
    index = [mod_lanes(step + (chunk * jnp.bitwise_xor(part_at, layer) + lanes)) for layer in range(layers)]
    edges = [jnp.zeros(tile, jnp.float32)] * inst_count
    groups = Groups(me)
    for field in range(5):
        tiles = [flow[0, field, layer] for layer in range(layers)]
        for distance, values in enumerate(groups.send(tiles)):
            messages[distance][field] = values
        for layer in range(layers):
            got = pick_lanes(tiles[layer], index[layer])
            for distance in range(inst_count):
                here = place == field * 4 + jnp.bitwise_xor(me, distance ^ layer)
                edges[distance] = jnp.where(here, got, edges[distance])
    for distance in range(inst_count):
        messages[distance][5] = edges[distance]


def unpack_kernel(*refs):
    received, (near_a, near_b, main, halo) = in_order(refs[:4]), refs[5:]
    me = lax.axis_index("inst")
    even = jnp.bitwise_and(lax.axis_index("space"), 1) == 0
    lane = lane_ids()
    owner = group_ids()
    band = band_ids()
    level = jnp.clip(band - 1, 0, layers - 1)
    inner = jnp.bitwise_xor(level, me) * 4 + jnp.bitwise_and(lane, 3)
    up_edge = down_edge = jnp.zeros(tile, jnp.float32)
    groups = Groups(me)
    for field in range(5):
        tiles = groups.receive([message[field] for message in received])
        for layer in range(layers):
            main[field, layer] = tiles[layer]
        for place in range(2):
            near_a[2 * field + place] = jnp.where(even, tiles[2 + place], tiles[place])
            near_b[2 * field + place] = jnp.where(even, tiles[place], tiles[2 + place])
        edges = None
        for distance in range(inst_count):
            got = pick_lanes(received[distance][5], inner + 16 * field)
            edges = got if edges is None else jnp.where(owner == jnp.bitwise_xor(me, distance), got, edges)
        halo[field] = edges
        up_edge = jnp.where(band == field, turn(edges, 4 * (field - layers)), up_edge)
        down_edge = jnp.where(band == field, turn(edges, 4 * (field - 1)), down_edge)
    near_a[10] = jnp.where(even, up_edge, down_edge)
    near_b[10] = jnp.where(even, down_edge, up_edge)


class Cells:
    def __init__(self, parts):
        self.parts = list(parts)
        self.root, self.vel, self.temp = parts[0], list(parts[1:4]), parts[4]
        if len(parts) == 5:
            dens = self.root * self.root
            kinetic = 0.5 * (self.vel[0] * self.vel[0] + self.vel[1] * self.vel[1] + self.vel[2] * self.vel[2])
            enth = ratio * self.temp + kinetic
            heat = 2.0 * viscosity * (kinetic + ratio / prandtl * self.temp)
            self.parts += [dens, dens * self.temp, enth, heat]
        self.dens, self.pres, self.enth, self.heat = self.parts[5:]
        self.base = self.parts[:5]

    def map(self, change):
        return Cells([change(part) for part in self.base])

    def conserved(self):
        dens, enth = self.dens, self.enth
        return [dens] + [dens * part for part in self.vel] + [dens * enth - self.pres]


fields_kept = 9


def cells_of(dens, vel, pres):
    inverse_root = lax.rsqrt(dens)
    return Cells([dens * inverse_root] + list(vel) + [pres * (inverse_root * inverse_root)])


def cells_of_draws(draws):
    start = [base + spread * draw if base else spread * draw for base, spread, draw in zip(starts, spreads_of, draws)]
    return cells_of(start[0], start[1:4], start[4])


def cells_of_conserved(state):
    dens = state[0]
    inverse_root = lax.rsqrt(dens)
    inverse = inverse_root * inverse_root
    vel = [part * inverse for part in state[1:4]]
    kinetic = 0.5 * (vel[0] * vel[0] + vel[1] * vel[1] + vel[2] * vel[2])
    return Cells([dens * inverse_root] + vel + [(gamma_gas - 1.0) * (state[4] * inverse - kinetic)])


def roe_flux(low, high, normal):
    jump_dens = high.dens - low.dens
    jump_pres = high.pres - low.pres
    jump = [b - a for a, b in zip(low.vel, high.vel)]
    share = high.root / (low.root + high.root)
    vel = [a + share * d for a, d in zip(low.vel, jump)]
    enth = low.enth + share * (high.enth - low.enth)
    half_sq = 0.5 * (vel[0] * vel[0] + vel[1] * vel[1] + vel[2] * vel[2])
    sound_sq = (gamma_gas - 1.0) * (enth - half_sq)
    inverse = lax.rsqrt(sound_sq)
    sound = sound_sq * inverse
    dens_roe = low.root * high.root
    along = vel[normal]
    jump_along = jump[normal]
    press_part = jump_pres * (inverse * inverse)
    speed_part = dens_roe * inverse * jump_along
    bound = entropy_share * sound
    curve = (0.5 / entropy_share) * inverse
    floor = 0.5 * bound

    def fixed(speed):
        size = jnp.abs(speed)
        return jnp.where(size >= bound, size, speed * speed * curve + floor)

    slow = 0.5 * fixed(along - sound) * (press_part - speed_part)
    fast = 0.5 * fixed(along + sound) * (press_part + speed_part)
    middle = fixed(along)
    entropy = middle * (jump_dens - press_part)
    both = slow + fast
    total = both + entropy
    push = sound * (fast - slow)
    shear = middle * dens_roe
    mass_low = low.dens * low.vel[normal]
    mass_high = high.dens * high.vel[normal]
    out = [mass_low + mass_high - total]
    work = None
    for part in range(3):
        value = mass_low * low.vel[part] + mass_high * high.vel[part] - vel[part] * total
        if part == normal:
            value = value + (low.pres + high.pres) - push - (2.0 * viscosity) * jump_along
        else:
            value = value - (shear + 2.0 * viscosity) * jump[part]
            term = vel[part] * jump[part]
            work = term if work is None else work + term
        out.append(value)
    lost = enth * both + along * push + entropy * half_sq + shear * work
    out.append(mass_low * low.enth + mass_high * high.enth - lost - (high.heat - low.heat))
    return out


def span_change(cells):
    row = row_ids()
    faces = roe_flux(cells, cells.map(lambda part: pltpu.roll(part, rows - 1, 0)), 2)
    w = cells.vel[2]
    sound_sq = (gamma_gas - 1.0) * (cells.enth - 0.5 * (cells.vel[0] * cells.vel[0] + cells.vel[1] * cells.vel[1]))
    sound = sound_sq * lax.rsqrt(sound_sq)
    still = 2.0 * (cells.dens * w * w + cells.pres)
    moving = 2.0 * w * (sound * cells.dens + 2.0 * viscosity)
    changes = []
    for part in range(5):
        top = still + moving if part == 3 else 0.0
        bottom = still - moving if part == 3 else 0.0
        upper = jnp.where(row == rows - 1, top, faces[part])
        lower = jnp.where(row == 0, bottom, pltpu.roll(faces[part], 1, 0))
        changes.append(upper - lower)
    return changes


def over_instances(values):
    weights = [weight_of(distance) for distance in range(inst_count)]
    across = turn(values, 2 * chunk)
    return (weights[0] * values + weights[2] * across) + turn(weights[1] * values + weights[3] * across, chunk)


def put(ref, place, cells):
    for number, part in enumerate(cells.parts):
        ref[place, number] = part


def get(ref, place):
    return Cells([ref[place, number] for number in range(fields_kept)])


class Pitch:
    def __init__(self, above, below, edge_faces):
        self.above, self.below, self.edge_faces = above, below, edge_faces
        self.lag = inst_count // 4
        me = lax.axis_index("inst")
        lane = lane_ids()
        self.slot = jnp.bitwise_and(lane, 3)
        self.band = band_ids()
        column = jnp.bitwise_and(lane, chunk - 1)
        self.is_first, self.is_last = column == 0, column == chunk - 1
        self.seam = self.slot == jnp.where(me == 0, 1, jnp.where(me == inst_count - 1, 3, -1))
        start = group_ids() * chunk
        ahead = chunk * self.lag
        low_seam, high_seam = me == 0, me == inst_count - 1
        self.to_main = start + jnp.where(self.is_first, jnp.where(low_seam, 1 - ahead, 1), 3)
        self.from_main = mod_lanes(start + jnp.where(self.slot == 1, jnp.where(low_seam, ahead, 0), chunk - 1))
        self.beside_end = start + jnp.where(self.slot == 3, jnp.where(high_seam, ahead + 2, 2), 1)
        self.beside = mod_lanes(lane + jnp.where(self.slot == 3, jnp.where(high_seam, ahead - 1, -1), 1))

    def mains(self, ref, places):
        out = [None] * 5
        for layer, place in places:
            for number in range(5):
                got = pick_lanes(ref[place, number], self.from_main)
                out[number] = got if out[number] is None else jnp.where(self.band == layer + 1, got, out[number])
        return out

    def edges(self, cells, mains):
        slot = self.slot
        lower = Cells([jnp.where(slot == 3, b, a) for a, b in zip(cells.base, mains)])
        upper = []
        for a, b in zip(cells.base, mains):
            value = jnp.where(slot == 1, b, pick_lanes(a, self.beside))
            upper.append(jnp.where(self.seam, pick_rows(value, self.above), value))
        faces = roe_flux(lower, Cells(upper), 1)
        moved = [pick_rows(face, self.below) for face in faces]
        at_low = jnp.logical_and(self.seam, slot == 1)
        for part in range(5):
            self.edge_faces[part] = jnp.where(at_low, moved[part], faces[part])
        return faces, moved

    def as_upper(self, face, moved):
        return jnp.where(self.seam, turn(moved, chunk * self.lag), face)

    def end_faces(self, cells, band, mains):
        slot = self.slot
        index = mod_lanes(self.beside_end + band * 4)
        halo = [pick_lanes(part, index) for part in cells.base]
        lower = Cells([jnp.where(slot == 3, b, a) for a, b in zip(halo, mains)])
        upper = [jnp.where(slot == 1, b, a) for a, b in zip(halo, mains)]
        upper = Cells([jnp.where(self.seam, pick_rows(part, self.above), part) for part in upper])
        faces = roe_flux(lower, upper, 1)
        packed = faces[0]
        for part in range(1, 5):
            packed = jnp.where(self.band == part, faces[part], packed)
        at_low = jnp.logical_and(self.seam, slot == 1)
        return jnp.where(at_low, pick_rows(packed, self.below), packed)

    def change(self, cells, layer, packed=None):
        faces = roe_flux(cells, cells.map(lambda part: turn(part, -1)), 1)
        changes = []
        for part in range(5):
            tile_of, band = (self.edge_faces[part], layer + 1) if packed is None else (packed, part)
            edge = pick_lanes(tile_of, mod_lanes(band * 4 + self.to_main + lanes))
            upper = jnp.where(self.is_last, edge, faces[part])
            lower = jnp.where(self.is_first, edge, turn(faces[part], 1))
            changes.append(upper - lower)
        return changes


def index_kernel(match, behind, above, below):
    row = row_ids()
    below_of = jnp.zeros(tile, jnp.int32)
    above_of = jnp.zeros(tile, jnp.int32)
    for k in range(rows):
        value = match[k]
        below_of = jnp.where(row == k, value, below_of)
        above_of = jnp.where(row == value, k, above_of)
    below[...], above[...] = below_of, above_of


def inner_kernel(above, below, main, halo, first, edge_first, part_first, part_edge, second, part_second, edge_faces):
    pitch = Pitch(above[...], below[...], edge_faces)
    slot = pitch.slot
    middle = range(1, layers - 1)
    for layer in range(layers):
        put(first, layer, cells_of_draws([main[field, layer] for field in range(5)]))
    cells = cells_of_draws([halo[field] for field in range(5)])
    for number, part in enumerate(cells.parts):
        edge_first[number] = part
    faces, moved = pitch.edges(cells, pitch.mains(first, [(layer, layer) for layer in range(layers)]))
    span = span_change(cells)
    axial = roe_flux(cells, cells.map(lambda part: turn(part, -4)), 0)
    state = cells.conserved()
    for part in range(5):
        lower_use = pitch.as_upper(faces[part], moved[part])
        along = jnp.where(slot == 1, faces[part] - turn(faces[part], 1), faces[part] - turn(lower_use, -1))
        between = jnp.where(jnp.logical_and(pitch.band > 0, pitch.band < layers), axial[part], 0.0)
        value = over_instances(state[part]) + 0.5 * (along + span[part] + (between - turn(between, 4)))
        part_edge[part] = value
        state[part] = state[part] - pseudo_step * value
    edge_second = cells_of_conserved(state)

    def step(layer, below_faces):
        cells = get(first, layer)
        above_faces = roe_flux(cells, get(first, jnp.minimum(layer + 1, layers - 1)), 0)
        span = span_change(cells)
        along = pitch.change(cells, layer)
        state = cells.conserved()
        outs = []
        for part in range(5):
            upper = jnp.where(layer == layers - 1, 0.0, above_faces[part])
            part_first[layer, part] = over_instances(state[part]) + 0.5 * (
                (upper - below_faces[part]) + span[part] + along[part]
            )
            outs.append(upper)
        return tuple(outs)

    lax.fori_loop(0, layers, step, (jnp.zeros(tile, jnp.float32),) * 5)

    for place, layer in enumerate(middle):
        state = get(first, layer).conserved()
        state = [value - pseudo_step * part_first[layer, part] for part, value in enumerate(state)]
        put(second, place, cells_of_conserved(state))
    pitch.edges(edge_second, pitch.mains(second, [(layer, place) for place, layer in enumerate(middle)]))
    between = roe_flux(get(second, 0), get(second, 1), 0)
    for part in range(5):
        part_second[0, part] = between[part]
        part_second[1, part] = -between[part]

    def second_step(place, carry):
        cells = get(second, place)
        span = span_change(cells)
        along = pitch.change(cells, place + 1)
        state = cells.conserved()
        for part in range(5):
            value = part_second[place, part] + span[part] + along[part]
            part_second[place, part] = over_instances(state[part]) + 0.5 * value
        return carry

    unrolled(layers - 2, second_step)


def side_values(high, closed, near, shared, scratch):
    first, edge_first, part_first, part_edge, second_middle, part_second, above, below, halo = shared
    ends, second = scratch
    pitch = Pitch(above[...], below[...], None)
    is_high = high == 1
    own = high * (layers - 1)

    own_cells = get(first, own)
    put(ends, 2 - 2 * high, own_cells)
    put(second, 2 - 2 * high, get(second_middle, high))
    for place, part in ((2 * high, high), (1, 1 - high)):
        cells = cells_of_draws([near[2 * field + part] for field in range(5)])
        if closed is not None:
            cells = Cells([jnp.where(closed, a, b) for a, b in zip(own_cells.parts, cells.parts)])
        put(ends, place, cells)
    draws = []
    for field in range(5):
        value = turn(near[10], mod_lanes(4 * (own + 1 - field) + lanes))
        draws.append(value if closed is None else jnp.where(closed, halo[field], value))
    outside = cells_of_draws(draws)
    inside = Cells([edge_first[number] for number in range(fields_kept)])
    pairs = list(zip(inside.base, outside.base))
    lower = Cells([jnp.where(is_high, a, b) for a, b in pairs])
    upper = Cells([jnp.where(is_high, b, a) for a, b in pairs])
    axial = roe_flux(lower, upper, 0)
    state = inside.conserved()
    for part in range(5):
        value = part_edge[part] + 0.5 * jnp.where(is_high, axial[part], -axial[part])
        state[part] = state[part] - pseudo_step * value
    edge_second = cells_of_conserved(state)

    def middle_values(ref, edge_cells):
        cells = get(ref, 1)
        packed = pitch.end_faces(edge_cells, own + 1, pitch.mains(ref, [(0, 1)]))
        lower = roe_flux(get(ref, 0), cells, 0)
        upper = roe_flux(cells, get(ref, 2), 0)
        span = span_change(cells)
        along = pitch.change(cells, None, packed)
        state = cells.conserved()
        values, inward = [], []
        for part in range(5):
            value = (upper[part] - lower[part]) + span[part] + along[part]
            values.append(over_instances(state[part]) + 0.5 * value)
            inward.append(0.5 * jnp.where(is_high, lower[part], -upper[part]))
        return state, values, inward

    state, values, inward = middle_values(ends, outside)
    beyond = cells_of_conserved([a - pseudo_step * b for a, b in zip(state, values)])
    state = own_cells.conserved()
    state = [a - pseudo_step * (part_first[own, part] + inward[part]) for part, a in enumerate(state)]
    own_second = cells_of_conserved(state)
    if closed is not None:
        beyond = Cells([jnp.where(closed, a, b) for a, b in zip(own_second.parts, beyond.parts)])
    put(second, 1, own_second)
    put(second, 2 * high, beyond)
    _, values, inward = middle_values(second, edge_second)
    groups = Groups(lax.axis_index("inst"))
    inner = [part_second[high, part] + inward[part] for part in range(5)]
    return [groups.turned(part, own) for part in values], [groups.turned(part, 1 + high) for part in inner]


def near_side_kernel(near, *refs):
    shared, out, scratch = refs[:9], refs[9], refs[10:]
    high = 1 - jnp.bitwise_and(lax.axis_index("space"), 1)
    for place, values in enumerate(side_values(high, None, near, shared, scratch)):
        for part in range(5):
            out[place, part] = values[part]


def far_side_kernel(near, other, *refs):
    shared, messages, scratch = refs[:9], in_order(refs[9:13], back), refs[13:]
    where_on = lax.axis_index("space")
    high = jnp.bitwise_and(where_on, 1)
    closed = jnp.logical_or(where_on == 0, where_on == lax.axis_size("space") - 1)
    end, inner = side_values(high, closed, near, shared, scratch)
    groups = Groups(lax.axis_index("inst"))
    is_high = high == 1
    for field in range(5):
        low_side = [jnp.where(is_high, other[place, field], mine[field]) for place, mine in ((0, end), (1, inner))]
        high_side = [jnp.where(is_high, mine[field], other[place, field]) for place, mine in ((1, inner), (0, end))]
        for distance, values in enumerate(groups.share(low_side + high_side)):
            messages[distance][field] = values


def return_kernel(*refs):
    received, out = in_order(refs[:4], back), refs[4]
    groups = Groups(lax.axis_index("inst"))
    for field in range(5):
        for layer, values in enumerate(groups.receive([message[field] for message in received])):
            out[0, field, layer] = values


def call(kernel, outs, operands, scratch=(), scalars=0):
    shapes = [jax.ShapeDtypeStruct(shape, kind) for shape, kind in outs]
    return pl.pallas_call(
        kernel,
        out_shape=shapes,
        in_specs=[smem] * scalars + [vmem] * (len(operands) - scalars),
        out_specs=[vmem] * len(shapes),
        scratch_shapes=[pltpu.VMEM(shape, jnp.float32) for shape in scratch],
        compiler_params=pltpu.CompilerParams(vmem_limit_bytes=16 * 2**20),
    )(*operands)


def floats(*shape):
    return shape + tile, jnp.float32


def swap_instances(messages, order=order):
    got = []
    for distance, message in zip(order, messages):
        route = [(i, i ^ distance) for i in range(inst_count)]
        got.append(lax.ppermute(message, "inst", route) if distance else message)
    return got


def on_device_fast(flow_state, period_match):
    count = lax.axis_size("space")
    messages = call(pack_kernel, [floats(6)] * inst_count, [flow_state])
    integers = (tile, jnp.int32)
    above, below = call(index_kernel, [integers, integers], [period_match, messages[-1]], scalars=1)
    near_a, near_b, main, halo = call(
        unpack_kernel, [floats(11), floats(11), floats(5, layers), floats(5)], [*swap_instances(messages), above]
    )
    route_a = [(i, i ^ 1) for i in range(count)]
    route_b = []
    for n in range(inst_count):
        for i in range(count):
            far = (n, ((i - 1) ^ 1) + 1) if 0 < i < count - 1 else (n ^ 1, i)
            route_b.append((n * count + i, far[0] * count + far[1]))
    near_a = lax.ppermute(near_a, "space", route_a)
    near_b = lax.ppermute(near_b, ("inst", "space"), route_b)
    inner = call(
        inner_kernel,
        [
            floats(layers, fields_kept),
            floats(fields_kept),
            floats(layers, 5),
            floats(5),
            floats(layers - 2, fields_kept),
            floats(layers - 2, 5),
        ],
        [above, below, main, halo],
        [(5,) + tile],
    )
    shared = [*inner, above, below, halo]
    scratch = [(3, fields_kept) + tile, (3, fields_kept) + tile]
    (other,) = call(near_side_kernel, [floats(2, 5)], [near_a, *shared], scratch)
    results = call(far_side_kernel, [floats(5)] * inst_count, [near_b, other, *shared], scratch)
    return call(return_kernel, [(flow_state.shape, jnp.float32)], swap_instances(results, back))[0]


def solution(mesh):
    in_specs = (P(("groups", "inst"), None, "space", None, None), P())
    out_specs = P(("groups", "inst"), None, "space", None, None)

    def whole(flow_state, period_match):
        block = (flow_state.shape[2] // mesh.shape["space"],) + flow_state.shape[3:]
        fits = mesh.shape["inst"] == inst_count and mesh.shape["space"] % 2 == 0
        body = on_device_fast if fits and block == (layers, rows, lanes) else on_device
        return jax.shard_map(body, mesh=mesh, in_specs=in_specs, out_specs=out_specs, check_vma=False)(
            flow_state, period_match
        )

    return whole
```

```python
import math

import jax
import jax.numpy as jnp
from jax import lax
from jax.experimental import pallas as pl
from jax.experimental.pallas import tpu as pltpu
from jax.sharding import PartitionSpec as P

gamma_gas = 1.4
prandtl = 0.72
viscosity = 0.1
pseudo_step = 0.03
entropy_share = 0.1


def from_behind(block, axis, distance):
    devices = range(lax.axis_size(axis))
    route = [((i - distance) % len(devices), i) for i in devices]
    return lax.ppermute(block, axis, route)


def extended(cells, sides, width):
    for axis, dim in sides:
        count = lax.axis_size(axis)
        ends = count - 1
        head = lax.slice_in_dim(cells, 0, width, axis=dim)
        tail = lax.slice_in_dim(cells, cells.shape[dim] - width, cells.shape[dim], axis=dim)
        cells = jnp.concatenate(
            [
                lax.ppermute(tail, axis, [(i, (i + 1) % count) for i in range(ends)]),
                cells,
                lax.ppermute(head, axis, [((i + 1) % count, i) for i in range(ends)]),
            ],
            axis=dim,
        )
    return cells


def from_draw(draws):
    shape = (5,) + (1,) * (draws.ndim - 1)
    offsets = jnp.array([1.0, 0.8, 0.0, 0.0, 0.8], jnp.float32).reshape(shape)
    spreads = jnp.array([0.3, 0.3, 0.3, 0.3, 0.2], jnp.float32).reshape(shape)
    return offsets + spreads * draws


def conserved(primitives):
    dens = primitives[0]
    velocity = primitives[1:4]
    kinetic = 0.5 * dens * jnp.sum(velocity * velocity, axis=0)
    energy = primitives[4] / (gamma_gas - 1.0) + kinetic
    return jnp.concatenate([dens[None], dens[None] * velocity, energy[None]], axis=0)


def primitive(conserved_vars):
    dens = conserved_vars[0]
    velocity = conserved_vars[1:4] / dens
    pressure = (gamma_gas - 1.0) * (
        conserved_vars[4] - 0.5 * dens * jnp.sum(velocity * velocity, axis=0)
    )
    return jnp.concatenate([dens[None], velocity, pressure[None]], axis=0)


def entropy_fix(eigen_val, sound_speed):
    spread = entropy_share * sound_speed
    magnitude = jnp.abs(eigen_val)
    return jnp.where(
        magnitude >= spread, magnitude, (eigen_val * eigen_val + spread * spread) / (2.0 * spread)
    )


def euler_flux(dens, velocity, pressure, enthalpy, normal):
    normal_vel = velocity[normal]
    values = [dens * normal_vel]
    for component in range(3):
        moment = dens * velocity[component] * normal_vel
        if component == normal:
            moment = moment + pressure
        values.append(moment)
    values.append(dens * enthalpy * normal_vel)
    return values


def face_flux(left_cells, right_cells, normal):
    dens_left, vel_left, pres_left = (left_cells[0], left_cells[1:4], left_cells[4])
    dens_right, vel_right, pres_right = (right_cells[0], right_cells[1:4], right_cells[4])
    ratio = gamma_gas / (gamma_gas - 1.0)
    sq_left = jnp.sum(vel_left * vel_left, axis=0)
    sq_right = jnp.sum(vel_right * vel_right, axis=0)
    enth_left = ratio * pres_left / dens_left + 0.5 * sq_left
    enth_right = ratio * pres_right / dens_right + 0.5 * sq_right
    flux_left = euler_flux(dens_left, vel_left, pres_left, enth_left, normal)
    flux_right = euler_flux(dens_right, vel_right, pres_right, enth_right, normal)
    root_left = jnp.sqrt(dens_left)
    root_right = jnp.sqrt(dens_right)
    root_sum = root_left + root_right
    vel_roe = (root_left * vel_left + root_right * vel_right) / root_sum
    enth_roe = (root_left * enth_left + root_right * enth_right) / root_sum
    speed_sq = jnp.sum(vel_roe * vel_roe, axis=0)
    sound_sq = (gamma_gas - 1.0) * (enth_roe - 0.5 * speed_sq)
    sound_speed = jnp.sqrt(sound_sq)
    normal_vel = vel_roe[normal]
    dens_roe = root_left * root_right
    jump_dens = dens_right - dens_left
    jump_pres = pres_right - pres_left
    jump_vel = vel_right - vel_left
    jump_normal = jump_vel[normal]
    wave_slow = (jump_pres - dens_roe * sound_speed * jump_normal) / (2.0 * sound_sq)
    wave_fast = (jump_pres + dens_roe * sound_speed * jump_normal) / (2.0 * sound_sq)
    wave_mid = jump_dens - jump_pres / sound_sq
    eigen_mid = entropy_fix(normal_vel, sound_speed)
    flux_slow = entropy_fix(normal_vel - sound_speed, sound_speed) * wave_slow
    flux_fast = entropy_fix(normal_vel + sound_speed, sound_speed) * wave_fast
    dissipation = [flux_slow + eigen_mid * wave_mid + flux_fast]
    for component in range(3):
        unit_dir = 1.0 if component == normal else 0.0
        term = flux_slow * (vel_roe[component] - unit_dir * sound_speed)
        term = term + eigen_mid * (
            wave_mid * vel_roe[component]
            + dens_roe * (jump_vel[component] - unit_dir * jump_normal)
        )
        term = term + flux_fast * (vel_roe[component] + unit_dir * sound_speed)
        dissipation.append(term)
    shear_work = jnp.sum(vel_roe * jump_vel, axis=0) - normal_vel * jump_normal
    energy_term = flux_slow * (enth_roe - normal_vel * sound_speed)
    energy_term = energy_term + eigen_mid * (wave_mid * 0.5 * speed_sq + dens_roe * shear_work)
    energy_term = energy_term + flux_fast * (enth_roe + normal_vel * sound_speed)
    dissipation.append(energy_term)
    jump_temp = pres_right / dens_right - pres_left / dens_left
    jump_kin = 0.5 * (sq_right - sq_left)
    viscous_terms = [
        jnp.zeros_like(jump_dens),
        jump_vel[0],
        jump_vel[1],
        jump_vel[2],
        jump_kin + gamma_gas / ((gamma_gas - 1.0) * prandtl) * jump_temp,
    ]
    values = []
    for component in range(5):
        values.append(
            0.5 * (flux_left[component] + flux_right[component])
            - 0.5 * dissipation[component]
            - viscosity * viscous_terms[component]
        )
    return jnp.stack(values, axis=0)


def flux_change(padded, along, normal):
    length = padded.shape[along]
    face_values = face_flux(
        lax.slice_in_dim(padded, 0, length - 1, axis=along),
        lax.slice_in_dim(padded, 1, length, axis=along),
        normal,
    )
    return lax.slice_in_dim(face_values, 1, length - 1, axis=along) - lax.slice_in_dim(
        face_values, 0, length - 2, axis=along
    )


def spectral_entry(offset, number):
    wrapped = jnp.mod(offset, number)
    parity = 1.0 - 2.0 * jnp.mod(wrapped, 2).astype(jnp.float32)
    angles = math.pi * wrapped.astype(jnp.float32) / number
    sine_val = jnp.where(wrapped == 0, 1.0, jnp.sin(angles))
    derivative = jnp.where(
        wrapped == 0, 0.0, math.pi / number * parity * jnp.cos(angles) / sine_val
    )
    return derivative + 0.5 * parity


def on_device(flow_state, period_match):
    instances = lax.axis_size("inst")
    phase_lag = instances // 4
    instance = lax.axis_index("inst")
    space_parts = lax.axis_size("space")
    position = lax.axis_index("space")
    labels = jnp.arange(period_match.shape[0], dtype=jnp.int32)
    matches = (period_match[:, None] == labels[None, :]).astype(jnp.int32)
    inverse = jnp.sum(labels[:, None] * matches, axis=0)
    mirror = jnp.array([1.0, 1.0, 1.0, -1.0, 1.0], jnp.float32).reshape(5, 1, 1, 1)

    def lagged(plane, steps):
        return from_behind(plane, "inst", steps)

    def timewise(conserved_vars):
        pieces = lax.all_gather(conserved_vars[None], "inst", axis=0, tiled=True)
        number = pieces.shape[0]
        others = jnp.arange(number, dtype=jnp.int32)
        weights = spectral_entry(instance - others, instances)
        return jnp.tensordot(weights, pieces, axes=1, precision=lax.Precision.HIGHEST)

    def evaluate(conserved_vars):
        prims = primitive(conserved_vars)
        padded = extended(prims, (("space", 1),), 1)
        lower_edge = jnp.where(position == 0, prims[:, :1], padded[:, :1])
        upper_edge = jnp.where(position == space_parts - 1, prims[:, -1:], padded[:, -1:])
        along_axial = jnp.concatenate([lower_edge, prims, upper_edge], axis=1)
        along_span = jnp.concatenate(
            [prims[:, :, :1] * mirror, prims, prims[:, :, -1:] * mirror], axis=2
        )
        ghost_below = jnp.take(lagged(prims[..., -1], phase_lag), period_match, axis=2)
        ghost_above = jnp.take(lagged(prims[..., 0], -phase_lag), inverse, axis=2)
        along_pitch = jnp.concatenate(
            [ghost_below[..., None], prims, ghost_above[..., None]], axis=3
        )
        spatial = (
            flux_change(along_axial, 1, 0)
            + flux_change(along_span, 2, 2)
            + flux_change(along_pitch, 3, 1)
        )
        return timewise(conserved_vars) + spatial

    initial = conserved(from_draw(flow_state[0]))
    section_state = initial - pseudo_step * evaluate(initial)
    return evaluate(section_state)[None]


inst_count = 4
layers = 4
chunk = 32
rows = 16
lanes = 128
tile = (rows, lanes)
vmem = pl.BlockSpec(memory_space=pltpu.VMEM)
smem = pl.BlockSpec(memory_space=pltpu.SMEM)
starts = (1.0, 0.8, 0.0, 0.0, 0.8)
spreads_of = (0.3, 0.3, 0.3, 0.3, 0.2)
ratio = gamma_gas / (gamma_gas - 1.0)


def weight_of(distance):
    parity = 1.0 - 2.0 * (distance % 2)
    if distance == 0:
        return 0.5
    if 2 * distance == inst_count:
        return 0.5 * parity
    angle = math.pi * distance / inst_count
    return math.pi / inst_count * parity * math.cos(angle) / math.sin(angle) + 0.5 * parity


order = (2, 3, 1, 0)
back = (3, 2, 1, 0)


def in_order(items, order=order):
    return [items[order.index(distance)] for distance in range(inst_count)]


def unrolled(count, body, carry=None):
    for number in range(count):
        carry = body(number, carry)
    return carry


def lane_ids():
    return lax.broadcasted_iota(jnp.int32, tile, 1)


def row_ids():
    return lax.broadcasted_iota(jnp.int32, tile, 0)


def band_ids():
    return jnp.bitwise_and(lane_ids() // 4, 7)


def pick_lanes(values, index):
    return jnp.take_along_axis(values, index, axis=1, mode="promise_in_bounds")


def pick_rows(values, index):
    half = rows // 2
    low, high = values[:half], values[half:]
    parts = []
    for part in (index[:half], index[half:]):
        inner = jnp.bitwise_and(part, half - 1)
        from_low = jnp.take_along_axis(low, inner, axis=0, mode="promise_in_bounds")
        from_high = jnp.take_along_axis(high, inner, axis=0, mode="promise_in_bounds")
        parts.append(jnp.where(part < half, from_low, from_high))
    return jnp.concatenate(parts, axis=0)


def turn(values, amount):
    return pltpu.roll(values, amount % lanes if isinstance(amount, int) else amount, 1)


def mod_lanes(amount):
    if isinstance(amount, int):
        return amount % lanes
    return jnp.bitwise_and(amount, lanes - 1)


def group_ids():
    return lane_ids() // chunk


class Groups:
    def __init__(self, me):
        group = group_ids()
        self.me = me
        self.amounts = [chunk * (me + layer) for layer in range(layers)]
        self.masks = []
        for distance in range(inst_count):
            total = jnp.bitwise_xor(me, distance) + me
            self.masks.append([group == jnp.bitwise_and(total + layer, 3) for layer in range(layers)])

    def send(self, tiles):
        return self.share([self.turned(values, layer) for layer, values in enumerate(tiles)])

    def turned(self, values, layer):
        return turn(values, mod_lanes(chunk * (self.me + layer)))

    def share(self, turned):
        messages = []
        for masks in self.masks:
            out = turned[0]
            for layer in range(1, layers):
                out = jnp.where(masks[layer], turned[layer], out)
            messages.append(out)
        return messages

    def receive(self, messages):
        tiles = []
        for layer, amount in enumerate(self.amounts):
            out = messages[0]
            for distance in range(1, inst_count):
                out = jnp.where(self.masks[distance][layer], messages[distance], out)
            tiles.append(turn(out, mod_lanes(4 * lanes - amount)))
        return tiles


def pack_kernel(flow, *refs):
    messages = in_order(refs)
    me = lax.axis_index("inst")
    lane = lane_ids()
    place = lane // 4
    slot = jnp.bitwise_and(lane, 3)
    step = jnp.where(slot < 2, slot - 2, slot + chunk - 2)
    part_at = jnp.bitwise_and(place, 3)
    index = [mod_lanes(step + (chunk * jnp.bitwise_xor(part_at, layer) + lanes)) for layer in range(layers)]
    edges = [jnp.zeros(tile, jnp.float32)] * inst_count
    groups = Groups(me)
    for field in range(5):
        tiles = [flow[0, field, layer] for layer in range(layers)]
        for distance, values in enumerate(groups.send(tiles)):
            messages[distance][field] = values
        for layer in range(layers):
            got = pick_lanes(tiles[layer], index[layer])
            for distance in range(inst_count):
                here = place == field * 4 + jnp.bitwise_xor(me, distance ^ layer)
                edges[distance] = jnp.where(here, got, edges[distance])
    for distance in range(inst_count):
        messages[distance][5] = edges[distance]


def unpack_kernel(*refs):
    received, (near_a, near_b, main, halo) = in_order(refs[:4]), refs[5:]
    me = lax.axis_index("inst")
    even = jnp.bitwise_and(lax.axis_index("space"), 1) == 0
    lane = lane_ids()
    owner = group_ids()
    band = band_ids()
    level = jnp.clip(band - 1, 0, layers - 1)
    inner = jnp.bitwise_xor(level, me) * 4 + jnp.bitwise_and(lane, 3)
    up_edge = down_edge = jnp.zeros(tile, jnp.float32)
    groups = Groups(me)
    for field in range(5):
        tiles = groups.receive([message[field] for message in received])
        for layer in range(layers):
            main[field, layer] = tiles[layer]
        for place in range(2):
            near_a[2 * field + place] = jnp.where(even, tiles[2 + place], tiles[place])
            near_b[2 * field + place] = jnp.where(even, tiles[place], tiles[2 + place])
        edges = None
        for distance in range(inst_count):
            got = pick_lanes(received[distance][5], inner + 16 * field)
            edges = got if edges is None else jnp.where(owner == jnp.bitwise_xor(me, distance), got, edges)
        halo[field] = edges
        up_edge = jnp.where(band == field, turn(edges, 4 * (field - layers)), up_edge)
        down_edge = jnp.where(band == field, turn(edges, 4 * (field - 1)), down_edge)
    near_a[10] = jnp.where(even, up_edge, down_edge)
    near_b[10] = jnp.where(even, down_edge, up_edge)


class Cells:
    def __init__(self, parts):
        self.parts = list(parts)
        self.root, self.vel, self.temp = parts[0], list(parts[1:4]), parts[4]
        if len(parts) == 5:
            dens = self.root * self.root
            kinetic = 0.5 * (self.vel[0] * self.vel[0] + self.vel[1] * self.vel[1] + self.vel[2] * self.vel[2])
            enth = ratio * self.temp + kinetic
            heat = 2.0 * viscosity * (kinetic + ratio / prandtl * self.temp)
            self.parts += [dens, dens * self.temp, enth, heat]
        self.dens, self.pres, self.enth, self.heat = self.parts[5:]
        self.base = self.parts[:5]

    def map(self, change):
        return Cells([change(part) for part in self.base])

    def conserved(self):
        dens, enth = self.dens, self.enth
        return [dens] + [dens * part for part in self.vel] + [dens * enth - self.pres]


fields_kept = 9


def cells_of(dens, vel, pres):
    inverse_root = lax.rsqrt(dens)
    return Cells([dens * inverse_root] + list(vel) + [pres * (inverse_root * inverse_root)])


def cells_of_draws(draws):
    start = [base + spread * draw if base else spread * draw for base, spread, draw in zip(starts, spreads_of, draws)]
    return cells_of(start[0], start[1:4], start[4])


def cells_of_conserved(state):
    dens = state[0]
    inverse_root = lax.rsqrt(dens)
    inverse = inverse_root * inverse_root
    vel = [part * inverse for part in state[1:4]]
    kinetic = 0.5 * (vel[0] * vel[0] + vel[1] * vel[1] + vel[2] * vel[2])
    return Cells([dens * inverse_root] + vel + [(gamma_gas - 1.0) * (state[4] * inverse - kinetic)])


def roe_flux(low, high, normal):
    jump_dens = high.dens - low.dens
    jump_pres = high.pres - low.pres
    jump = [b - a for a, b in zip(low.vel, high.vel)]
    share = high.root / (low.root + high.root)
    vel = [a + share * d for a, d in zip(low.vel, jump)]
    enth = low.enth + share * (high.enth - low.enth)
    half_sq = 0.5 * (vel[0] * vel[0] + vel[1] * vel[1] + vel[2] * vel[2])
    sound_sq = (gamma_gas - 1.0) * (enth - half_sq)
    inverse = lax.rsqrt(sound_sq)
    sound = sound_sq * inverse
    dens_roe = low.root * high.root
    along = vel[normal]
    jump_along = jump[normal]
    press_part = jump_pres * (inverse * inverse)
    speed_part = dens_roe * inverse * jump_along
    bound = entropy_share * sound
    curve = (0.5 / entropy_share) * inverse
    floor = 0.5 * bound

    def fixed(speed):
        size = jnp.abs(speed)
        return jnp.where(size >= bound, size, speed * speed * curve + floor)

    slow = 0.5 * fixed(along - sound) * (press_part - speed_part)
    fast = 0.5 * fixed(along + sound) * (press_part + speed_part)
    middle = fixed(along)
    entropy = middle * (jump_dens - press_part)
    both = slow + fast
    total = both + entropy
    push = sound * (fast - slow)
    shear = middle * dens_roe
    mass_low = low.dens * low.vel[normal]
    mass_high = high.dens * high.vel[normal]
    out = [mass_low + mass_high - total]
    work = None
    for part in range(3):
        value = mass_low * low.vel[part] + mass_high * high.vel[part] - vel[part] * total
        if part == normal:
            value = value + (low.pres + high.pres) - push - (2.0 * viscosity) * jump_along
        else:
            value = value - (shear + 2.0 * viscosity) * jump[part]
            term = vel[part] * jump[part]
            work = term if work is None else work + term
        out.append(value)
    lost = enth * both + along * push + entropy * half_sq + shear * work
    out.append(mass_low * low.enth + mass_high * high.enth - lost - (high.heat - low.heat))
    return out


def span_change(cells):
    row = row_ids()
    faces = roe_flux(cells, cells.map(lambda part: pltpu.roll(part, rows - 1, 0)), 2)
    w = cells.vel[2]
    sound_sq = (gamma_gas - 1.0) * (cells.enth - 0.5 * (cells.vel[0] * cells.vel[0] + cells.vel[1] * cells.vel[1]))
    sound = sound_sq * lax.rsqrt(sound_sq)
    still = 2.0 * (cells.dens * w * w + cells.pres)
    moving = 2.0 * w * (sound * cells.dens + 2.0 * viscosity)
    changes = []
    for part in range(5):
        top = still + moving if part == 3 else 0.0
        bottom = still - moving if part == 3 else 0.0
        upper = jnp.where(row == rows - 1, top, faces[part])
        lower = jnp.where(row == 0, bottom, pltpu.roll(faces[part], 1, 0))
        changes.append(upper - lower)
    return changes


def over_instances(values):
    weights = [weight_of(distance) for distance in range(inst_count)]
    across = turn(values, 2 * chunk)
    return (weights[0] * values + weights[2] * across) + turn(weights[1] * values + weights[3] * across, chunk)


def put(ref, place, cells):
    for number, part in enumerate(cells.parts):
        ref[place, number] = part


def get(ref, place):
    return Cells([ref[place, number] for number in range(fields_kept)])


class Pitch:
    def __init__(self, above, below, edge_faces):
        self.above, self.below, self.edge_faces = above, below, edge_faces
        self.lag = inst_count // 4
        me = lax.axis_index("inst")
        lane = lane_ids()
        self.slot = jnp.bitwise_and(lane, 3)
        self.band = band_ids()
        column = jnp.bitwise_and(lane, chunk - 1)
        self.is_first, self.is_last = column == 0, column == chunk - 1
        self.seam = self.slot == jnp.where(me == 0, 1, jnp.where(me == inst_count - 1, 3, -1))
        start = group_ids() * chunk
        ahead = chunk * self.lag
        low_seam, high_seam = me == 0, me == inst_count - 1
        self.to_main = start + jnp.where(self.is_first, jnp.where(low_seam, 1 - ahead, 1), 3)
        self.from_main = mod_lanes(start + jnp.where(self.slot == 1, jnp.where(low_seam, ahead, 0), chunk - 1))
        self.beside_end = start + jnp.where(self.slot == 3, jnp.where(high_seam, ahead + 2, 2), 1)
        self.beside = mod_lanes(lane + jnp.where(self.slot == 3, jnp.where(high_seam, ahead - 1, -1), 1))

    def mains(self, ref, places):
        out = [None] * 5
        for layer, place in places:
            for number in range(5):
                got = pick_lanes(ref[place, number], self.from_main)
                out[number] = got if out[number] is None else jnp.where(self.band == layer + 1, got, out[number])
        return out

    def edges(self, cells, mains):
        slot = self.slot
        lower = Cells([jnp.where(slot == 3, b, a) for a, b in zip(cells.base, mains)])
        upper = []
        for a, b in zip(cells.base, mains):
            value = jnp.where(slot == 1, b, pick_lanes(a, self.beside))
            upper.append(jnp.where(self.seam, pick_rows(value, self.above), value))
        faces = roe_flux(lower, Cells(upper), 1)
        moved = [pick_rows(face, self.below) for face in faces]
        at_low = jnp.logical_and(self.seam, slot == 1)
        for part in range(5):
            self.edge_faces[part] = jnp.where(at_low, moved[part], faces[part])
        return faces, moved

    def as_upper(self, face, moved):
        return jnp.where(self.seam, turn(moved, chunk * self.lag), face)

    def end_faces(self, cells, band, mains):
        slot = self.slot
        index = mod_lanes(self.beside_end + band * 4)
        halo = [pick_lanes(part, index) for part in cells.base]
        lower = Cells([jnp.where(slot == 3, b, a) for a, b in zip(halo, mains)])
        upper = [jnp.where(slot == 1, b, a) for a, b in zip(halo, mains)]
        upper = Cells([jnp.where(self.seam, pick_rows(part, self.above), part) for part in upper])
        faces = roe_flux(lower, upper, 1)
        packed = faces[0]
        for part in range(1, 5):
            packed = jnp.where(self.band == part, faces[part], packed)
        at_low = jnp.logical_and(self.seam, slot == 1)
        return jnp.where(at_low, pick_rows(packed, self.below), packed)

    def change(self, cells, layer, packed=None):
        faces = roe_flux(cells, cells.map(lambda part: turn(part, -1)), 1)
        changes = []
        for part in range(5):
            tile_of, band = (self.edge_faces[part], layer + 1) if packed is None else (packed, part)
            edge = pick_lanes(tile_of, mod_lanes(band * 4 + self.to_main + lanes))
            upper = jnp.where(self.is_last, edge, faces[part])
            lower = jnp.where(self.is_first, edge, turn(faces[part], 1))
            changes.append(upper - lower)
        return changes


def index_kernel(match, behind, above, below):
    row = row_ids()
    below_of = jnp.zeros(tile, jnp.int32)
    above_of = jnp.zeros(tile, jnp.int32)
    for k in range(rows):
        value = match[k]
        below_of = jnp.where(row == k, value, below_of)
        above_of = jnp.where(row == value, k, above_of)
    below[...], above[...] = below_of, above_of


def inner_kernel(above, below, main, halo, first, edge_first, part_first, part_edge, second, part_second, edge_faces):
    pitch = Pitch(above[...], below[...], edge_faces)
    slot = pitch.slot
    middle = range(1, layers - 1)
    for layer in range(layers):
        put(first, layer, cells_of_draws([main[field, layer] for field in range(5)]))
    cells = cells_of_draws([halo[field] for field in range(5)])
    for number, part in enumerate(cells.parts):
        edge_first[number] = part
    faces, moved = pitch.edges(cells, pitch.mains(first, [(layer, layer) for layer in range(layers)]))
    span = span_change(cells)
    axial = roe_flux(cells, cells.map(lambda part: turn(part, -4)), 0)
    state = cells.conserved()
    for part in range(5):
        lower_use = pitch.as_upper(faces[part], moved[part])
        along = jnp.where(slot == 1, faces[part] - turn(faces[part], 1), faces[part] - turn(lower_use, -1))
        between = jnp.where(jnp.logical_and(pitch.band > 0, pitch.band < layers), axial[part], 0.0)
        value = over_instances(state[part]) + 0.5 * (along + span[part] + (between - turn(between, 4)))
        part_edge[part] = value
        state[part] = state[part] - pseudo_step * value
    edge_second = cells_of_conserved(state)

    def step(layer, below_faces):
        cells = get(first, layer)
        above_faces = roe_flux(cells, get(first, jnp.minimum(layer + 1, layers - 1)), 0)
        span = span_change(cells)
        along = pitch.change(cells, layer)
        state = cells.conserved()
        outs = []
        for part in range(5):
            upper = jnp.where(layer == layers - 1, 0.0, above_faces[part])
            part_first[layer, part] = over_instances(state[part]) + 0.5 * (
                (upper - below_faces[part]) + span[part] + along[part]
            )
            outs.append(upper)
        return tuple(outs)

    lax.fori_loop(0, layers, step, (jnp.zeros(tile, jnp.float32),) * 5)

    for place, layer in enumerate(middle):
        state = get(first, layer).conserved()
        state = [value - pseudo_step * part_first[layer, part] for part, value in enumerate(state)]
        put(second, place, cells_of_conserved(state))
    pitch.edges(edge_second, pitch.mains(second, [(layer, place) for place, layer in enumerate(middle)]))
    between = roe_flux(get(second, 0), get(second, 1), 0)
    for part in range(5):
        part_second[0, part] = between[part]
        part_second[1, part] = -between[part]

    def second_step(place, carry):
        cells = get(second, place)
        span = span_change(cells)
        along = pitch.change(cells, place + 1)
        state = cells.conserved()
        for part in range(5):
            value = part_second[place, part] + span[part] + along[part]
            part_second[place, part] = over_instances(state[part]) + 0.5 * value
        return carry

    unrolled(layers - 2, second_step)


def side_values(high, closed, near, shared, scratch):
    first, edge_first, part_first, part_edge, second_middle, part_second, above, below, halo = shared
    ends, second = scratch
    pitch = Pitch(above[...], below[...], None)
    own = high * (layers - 1)

    own_cells = get(first, own)
    put(ends, 2 - 2 * high, own_cells)
    put(second, 2 - 2 * high, get(second_middle, high))
    for place, part in ((2 * high, high), (1, 1 - high)):
        cells = cells_of_draws([near[2 * field + part] for field in range(5)])
        if closed is not None:
            cells = Cells([jnp.where(closed, a, b) for a, b in zip(own_cells.parts, cells.parts)])
        put(ends, place, cells)
    draws = []
    for field in range(5):
        value = turn(near[10], mod_lanes(4 * (own + 1 - field) + lanes))
        draws.append(value if closed is None else jnp.where(closed, halo[field], value))
    outside = cells_of_draws(draws)
    inside = Cells([edge_first[number] for number in range(fields_kept)])
    axial = roe_flux(inside, outside, 0) if high else roe_flux(outside, inside, 0)
    state = inside.conserved()
    for part in range(5):
        value = part_edge[part] + 0.5 * (axial[part] if high else -axial[part])
        state[part] = state[part] - pseudo_step * value
    edge_second = cells_of_conserved(state)

    def middle_values(ref, edge_cells):
        cells = get(ref, 1)
        packed = pitch.end_faces(edge_cells, own + 1, pitch.mains(ref, [(0, 1)]))
        lower = roe_flux(get(ref, 0), cells, 0)
        upper = roe_flux(cells, get(ref, 2), 0)
        span = span_change(cells)
        along = pitch.change(cells, None, packed)
        state = cells.conserved()
        values, inward = [], []
        for part in range(5):
            value = (upper[part] - lower[part]) + span[part] + along[part]
            values.append(over_instances(state[part]) + 0.5 * value)
            inward.append(0.5 * (lower[part] if high else -upper[part]))
        return state, values, inward

    state, values, inward = middle_values(ends, outside)
    beyond = cells_of_conserved([a - pseudo_step * b for a, b in zip(state, values)])
    state = own_cells.conserved()
    state = [a - pseudo_step * (part_first[own, part] + inward[part]) for part, a in enumerate(state)]
    own_second = cells_of_conserved(state)
    if closed is not None:
        beyond = Cells([jnp.where(closed, a, b) for a, b in zip(own_second.parts, beyond.parts)])
    put(second, 1, own_second)
    put(second, 2 * high, beyond)
    _, values, inward = middle_values(second, edge_second)
    groups = Groups(lax.axis_index("inst"))
    inner = [part_second[high, part] + inward[part] for part in range(5)]
    return [groups.turned(part, own) for part in values], [groups.turned(part, 1 + high) for part in inner]


def near_side_kernel(near, *refs):
    shared, out, scratch = refs[:9], refs[9], refs[10:]
    odd = jnp.bitwise_and(lax.axis_index("space"), 1)

    for side in range(2):

        @pl.when(odd == 1 - side)
        def _(high=side):
            for place, values in enumerate(side_values(high, None, near, shared, scratch)):
                for part in range(5):
                    out[place, part] = values[part]


def far_side_kernel(near, other, *refs):
    shared, messages, scratch = refs[:9], in_order(refs[9:13], back), refs[13:]
    where_on = lax.axis_index("space")
    odd = jnp.bitwise_and(where_on, 1)
    closed = jnp.logical_or(where_on == 0, where_on == lax.axis_size("space") - 1)

    for side in range(2):

        @pl.when(odd == side)
        def _(high=side):
            end, inner = side_values(high, closed, near, shared, scratch)
            groups = Groups(lax.axis_index("inst"))
            for field in range(5):
                others = [other[place, field] for place in range(2)]
                tiles = [others[0], others[1], inner[field], end[field]]
                tiles = tiles if high else [end[field], inner[field], others[1], others[0]]
                for distance, values in enumerate(groups.share(tiles)):
                    messages[distance][field] = values


def return_kernel(*refs):
    received, out = in_order(refs[:4], back), refs[4]
    groups = Groups(lax.axis_index("inst"))
    for field in range(5):
        for layer, values in enumerate(groups.receive([message[field] for message in received])):
            out[0, field, layer] = values


def call(kernel, outs, operands, scratch=(), scalars=0):
    shapes = [jax.ShapeDtypeStruct(shape, kind) for shape, kind in outs]
    return pl.pallas_call(
        kernel,
        out_shape=shapes,
        in_specs=[smem] * scalars + [vmem] * (len(operands) - scalars),
        out_specs=[vmem] * len(shapes),
        scratch_shapes=[pltpu.VMEM(shape, jnp.float32) for shape in scratch],
        compiler_params=pltpu.CompilerParams(vmem_limit_bytes=16 * 2**20),
    )(*operands)


def floats(*shape):
    return shape + tile, jnp.float32


def swap_instances(messages, order=order):
    got = []
    for distance, message in zip(order, messages):
        route = [(i, i ^ distance) for i in range(inst_count)]
        got.append(lax.ppermute(message, "inst", route) if distance else message)
    return got


def on_device_fast(flow_state, period_match):
    count = lax.axis_size("space")
    messages = call(pack_kernel, [floats(6)] * inst_count, [flow_state])
    integers = (tile, jnp.int32)
    above, below = call(index_kernel, [integers, integers], [period_match, messages[-1]], scalars=1)
    near_a, near_b, main, halo = call(
        unpack_kernel, [floats(11), floats(11), floats(5, layers), floats(5)], [*swap_instances(messages), above]
    )
    route_a = [(i, i ^ 1) for i in range(count)]
    route_b = []
    for n in range(inst_count):
        for i in range(count):
            far = (n, ((i - 1) ^ 1) + 1) if 0 < i < count - 1 else (n ^ 1, i)
            route_b.append((n * count + i, far[0] * count + far[1]))
    near_a = lax.ppermute(near_a, "space", route_a)
    near_b = lax.ppermute(near_b, ("inst", "space"), route_b)
    inner = call(
        inner_kernel,
        [
            floats(layers, fields_kept),
            floats(fields_kept),
            floats(layers, 5),
            floats(5),
            floats(layers - 2, fields_kept),
            floats(layers - 2, 5),
        ],
        [above, below, main, halo],
        [(5,) + tile],
    )
    shared = [*inner, above, below, halo]
    scratch = [(3, fields_kept) + tile, (3, fields_kept) + tile]
    (other,) = call(near_side_kernel, [floats(2, 5)], [near_a, *shared], scratch)
    results = call(far_side_kernel, [floats(5)] * inst_count, [near_b, other, *shared], scratch)
    return call(return_kernel, [(flow_state.shape, jnp.float32)], swap_instances(results, back))[0]


def solution(mesh):
    in_specs = (P(("groups", "inst"), None, "space", None, None), P())
    out_specs = P(("groups", "inst"), None, "space", None, None)

    def whole(flow_state, period_match):
        block = (flow_state.shape[2] // mesh.shape["space"],) + flow_state.shape[3:]
        fits = mesh.shape["inst"] == inst_count and mesh.shape["space"] % 2 == 0
        body = on_device_fast if fits and block == (layers, rows, lanes) else on_device
        return jax.shard_map(body, mesh=mesh, in_specs=in_specs, out_specs=out_specs, check_vma=False)(
            flow_state, period_match
        )

    return whole
```
